32 devices in a mesh: expert: 2 (over y), hidden: 4 (over z), dp: 4 (over x, core).
Axes of the slice: x: 2, y: 2, z: 4, core: 2. Of those that a mesh axis runs over, the one named last changes fastest.
Arguments:
- tokens: bfloat16 [2, 4, 512, 2048], P('expert', 'dp', None, 'hidden'), may hold values from -6 to 6
- grad_out: bfloat16 [2, 4, 512, 2048], P('expert', 'dp', None, 'hidden'), may hold values from -0.25 to 0.25
- gate_weight: bfloat16 [4, 2048, 512], P('expert', 'dp', 'hidden'), may hold values from -0.125 to 0.125
- up_weight: bfloat16 [4, 2048, 512], P('expert', 'dp', 'hidden'), may hold values from -0.125 to 0.125
- down_weight: bfloat16 [4, 512, 2048], P('expert', 'hidden', 'dp'), may hold values from -0.25 to 0.25
- matching: int32 [2], replicated, may hold values from 0 to 1, each once
- block_counts: int32 [2, 4, 2], P('expert', 'dp'), may hold values from 0 to 4, as said below
Outputs:
- grad_gate: bfloat16 [4, 2048, 512], P('expert', 'dp', 'hidden')
- grad_up: bfloat16 [4, 2048, 512], P('expert', 'dp', 'hidden')
- grad_down: bfloat16 [4, 512, 2048], P('expert', 'hidden', 'dp')
The draws below stay inside these ranges and needn't reach their ends.
Inputs may be any that keep to these rules, and one draw needn't show every extreme that they name: `matching`: each expert index appears once. `block_counts`: the 2 counts of one expert index and data index sum to at most 4; on some device one count equals 4.
All inputs are finite; a program needn't handle non-finite values.
Results may differ from the reference program's by a relative error of at most 0.008.
Values may be sent and summed in bfloat16 or wider, within the bound.
A program may use at most 64 MiB of HBM per device.

```python
import jax
import jax.numpy as jnp
from jax import lax

D = 2048
HID = 512
EXP_DEV = 2
BLOCK = 128
BLOCKS = 4
ROWS = 512
EXPERTS = 4
N_EXPERT = 2
N_DP = 4


def draw_block_counts(key, part):
    folded = jax.random.fold_in(key, 11)
    key_total, key_cut, key_pick, key_expert = jax.random.split(folded, 4)
    totals = jax.random.randint(key_total, (N_EXPERT, N_DP), BLOCKS // 2, BLOCKS + 1)
    cut_points = jax.random.randint(key_cut, (N_EXPERT, N_DP, EXP_DEV - 1), 0, BLOCKS + 1)
    cut_points = jnp.sort(jnp.minimum(cut_points, totals[:, :, None]), axis=2)
    boundary = jnp.concatenate([jnp.zeros((N_EXPERT, N_DP, 1), jnp.int32), cut_points.astype(jnp.int32), totals[:, :, None].astype(jnp.int32)], axis=2)
    counts = boundary[:, :, 1:] - boundary[:, :, :-1]
    chosen = jax.random.randint(key_pick, (), 0, N_EXPERT * N_DP)
    expert = jax.random.randint(key_expert, (), 0, EXP_DEV)
    whole_load = (jnp.arange(EXP_DEV) == expert).astype(jnp.int32) * BLOCKS
    stacked = counts.reshape(N_EXPERT * N_DP, EXP_DEV)
    stacked = jnp.where((jnp.arange(N_EXPERT * N_DP) == chosen)[:, None], whole_load[None, :], stacked)
    return stacked.reshape(N_EXPERT, N_DP, EXP_DEV).astype(jnp.int32)


def shard_levels(rng, dims, shards, smallest, high):
    def one(position, shards_of):
        steps = jax.random.uniform(jax.random.fold_in(jax.random.fold_in(rng, 6), position), (shards_of,), jnp.float32, smallest / len(shards), high / len(shards))
        return jnp.repeat(jnp.exp(steps), dims[position] // shards_of).reshape((-1,) + (1,) * (len(dims) - position - 1))

    loudness = one(*shards[0])
    for cut in shards[1:]:
        loudness = loudness * one(*cut)
    return loudness


def centred(stream_key, shape, deviation, reach, cuts=(), kind=jnp.bfloat16):
    entries = deviation * jax.random.normal(stream_key, shape, jnp.float32)
    if cuts:
        entries = entries * shard_levels(stream_key, shape, cuts, -0.22, 0.18)
    return jnp.clip(entries, -reach, reach).astype(kind)


def setup_inputs(seed: int = 0) -> dict:
    splits = jax.random.split(jax.random.key(seed), 8)
    return {
        "tokens": centred(splits[0], (N_EXPERT, N_DP, ROWS, D), 1.0, 6.0, ((0, 2), (1, 4), (3, 4))),
        "grad_out": centred(splits[1], (N_EXPERT, N_DP, ROWS, D), (2.0 / (N_DP * ROWS) ** 0.5), 0.25, ((0, 2), (1, 4), (3, 4))),
        "gate_weight": centred(splits[2], (EXPERTS, D, HID), D ** -0.5, 0.125, ((0, 2), (1, 4), (2, 4))),
        "up_weight": centred(splits[3], (EXPERTS, D, HID), D ** -0.5, 0.125, ((0, 2), (1, 4), (2, 4))),
        "down_weight": centred(splits[4], (EXPERTS, HID, D), HID ** -0.5, 0.25, ((0, 2), (1, 4), (2, 4))),
        "matching": jax.random.permutation(splits[5], N_EXPERT).astype(jnp.int32),
        "block_counts": draw_block_counts(jax.random.fold_in(splits[7], 71), 0),
    }


def contract_rows(left, right):
    return lax.dot_general(left, right, (((0,), (0,)), ((), ())), preferred_element_type=jnp.float32)


def block_owners(counts, blocks):
    bounds = jnp.cumsum(counts).astype(jnp.int32)
    index = jnp.arange(blocks, dtype=jnp.int32)
    owner = jnp.sum((index[:, None] >= bounds[None, :]).astype(jnp.int32), axis=1)
    owner = jnp.minimum(owner, counts.shape[0] - 1).astype(jnp.int32)
    alive = (index < bounds[-1]).astype(jnp.float32)
    return owner, alive


def add_into(total, term, expert):
    current = lax.dynamic_index_in_dim(total, expert, 0, keepdims=True)
    return lax.dynamic_update_index_in_dim(total, current + term[None], expert, 0)


def expert_terms(row_blocks, grad_blocks, weight_gate, weight_up, weight_down, owner, alive):
    zeros_gate = jnp.zeros(weight_gate.shape, jnp.float32)
    zeros_down = jnp.zeros(weight_down.shape, jnp.float32)

    def step(carry, inputs):
        total_gate, total_up, total_down = carry
        row_block, grad_block, expert, live = inputs
        gate_matrix = lax.dynamic_index_in_dim(weight_gate, expert, 0, keepdims=False)
        up_matrix = lax.dynamic_index_in_dim(weight_up, expert, 0, keepdims=False)
        down_matrix = lax.dynamic_index_in_dim(weight_down, expert, 0, keepdims=False)
        gate_value = jnp.dot(row_block, gate_matrix, preferred_element_type=jnp.float32)
        up_value = jnp.dot(row_block, up_matrix, preferred_element_type=jnp.float32)
        sigmoid_gate = jax.nn.sigmoid(gate_value)
        activated = gate_value * sigmoid_gate
        hidden = (activated * up_value * live).astype(jnp.bfloat16)
        grad_hidden = lax.dot_general(grad_block, down_matrix, (((1,), (1,)), ((), ())), preferred_element_type=jnp.float32)
        grad_gate = (grad_hidden * up_value * sigmoid_gate * (1.0 + gate_value * (1.0 - sigmoid_gate)) * live).astype(jnp.bfloat16)
        grad_up = (grad_hidden * activated * live).astype(jnp.bfloat16)
        total_gate = add_into(total_gate, contract_rows(row_block, grad_gate), expert)
        total_up = add_into(total_up, contract_rows(row_block, grad_up), expert)
        total_down = add_into(total_down, contract_rows(hidden, grad_block), expert)
        return (total_gate, total_up, total_down), None

    totals, unused = lax.scan(step, (zeros_gate, zeros_gate, zeros_down), (row_blocks, grad_blocks, owner, alive))
    return totals


def reference(tokens, grad_out, gate_weight, up_weight, down_weight, matching, block_counts):
    blocks = ROWS // BLOCK

    def per_slot(inputs):
        slot_tokens, slot_grads, slot_counts, source = inputs
        start = (source * EXP_DEV).astype(jnp.int32)
        weight_gate = lax.dynamic_slice_in_dim(gate_weight, start, EXP_DEV, 0)
        weight_up = lax.dynamic_slice_in_dim(up_weight, start, EXP_DEV, 0)
        weight_down = lax.dynamic_slice_in_dim(down_weight, start, EXP_DEV, 0)
        sums = None
        for data_index in range(N_DP):
            owner, alive = block_owners(slot_counts[data_index], blocks)
            row_blocks = slot_tokens[data_index].reshape(blocks, BLOCK, D)
            grad_blocks = slot_grads[data_index].reshape(blocks, BLOCK, D)
            terms = expert_terms(row_blocks, grad_blocks, weight_gate, weight_up, weight_down, owner, alive)
            rounded = tuple(lax.optimization_barrier(term.astype(jnp.bfloat16)).astype(jnp.float32) for term in terms)
            if sums is None:
                sums = rounded
            else:
                sums = tuple(left + right for left, right in zip(sums, rounded))
        return tuple(total.astype(jnp.bfloat16) for total in sums)

    moved = lax.map(per_slot, (tokens, grad_out, block_counts, matching))
    grad_gate = moved[0].reshape(EXPERTS, D, HID)
    grad_up = moved[1].reshape(EXPERTS, D, HID)
    grad_down = moved[2].reshape(EXPERTS, HID, D)
    return (grad_gate, grad_up, grad_down)
```

```python
import functools

import jax
import jax.numpy as jnp
from jax import lax
from jax.experimental import pallas as pl
from jax.experimental.pallas import tpu as pltpu
from jax.sharding import PartitionSpec as P

BLOCK = 128


def contract_rows(left, right):
    return lax.dot_general(
        left, right, (((0,), (0,)), ((), ())), preferred_element_type=jnp.float32
    )


def block_owners(counts, blocks):
    bounds = jnp.cumsum(counts)
    index = jnp.arange(blocks, dtype=jnp.int32)
    owner = jnp.sum((index[:, None] >= bounds[None, :]).astype(jnp.int32), axis=1)
    owner = jnp.minimum(owner, counts.shape[0] - 1)
    alive = (index < bounds[-1]).astype(jnp.float32)
    return (owner, alive)


def add_into(total, term, expert):
    current = lax.dynamic_index_in_dim(total, expert, 0, keepdims=True)
    return lax.dynamic_update_index_in_dim(total, current + term[None], expert, 0)


def expert_terms(row_blocks, grad_blocks, weight_gate, weight_up, weight_down, owner, alive):
    zeros_gate = jnp.zeros(weight_gate.shape, jnp.float32)
    zeros_down = jnp.zeros(weight_down.shape, jnp.float32)

    def step(carry, inputs):
        total_gate, total_up, total_down = carry
        row_block, grad_block, expert, live = inputs
        gate_matrix = lax.dynamic_index_in_dim(weight_gate, expert, 0, keepdims=False)
        up_matrix = lax.dynamic_index_in_dim(weight_up, expert, 0, keepdims=False)
        down_matrix = lax.dynamic_index_in_dim(weight_down, expert, 0, keepdims=False)
        gate_value = jnp.dot(row_block, gate_matrix, preferred_element_type=jnp.float32)
        up_value = jnp.dot(row_block, up_matrix, preferred_element_type=jnp.float32)
        sigmoid_gate = jax.nn.sigmoid(gate_value)
        activated = gate_value * sigmoid_gate
        hidden = (activated * up_value * live).astype(jnp.bfloat16)
        grad_hidden = lax.dot_general(
            grad_block, down_matrix, (((1,), (1,)), ((), ())), preferred_element_type=jnp.float32
        )
        grad_gate = (
            grad_hidden * up_value * sigmoid_gate * (1.0 + gate_value * (1.0 - sigmoid_gate)) * live
        ).astype(jnp.bfloat16)
        grad_up = (grad_hidden * activated * live).astype(jnp.bfloat16)
        total_gate = add_into(total_gate, contract_rows(row_block, grad_gate), expert)
        total_up = add_into(total_up, contract_rows(row_block, grad_up), expert)
        total_down = add_into(total_down, contract_rows(hidden, grad_block), expert)
        return ((total_gate, total_up, total_down), None)

    totals, unused = lax.scan(
        step, (zeros_gate, zeros_gate, zeros_down), (row_blocks, grad_blocks, owner, alive)
    )
    return totals


def relocate(arrays, matching):
    groups = lax.axis_size("expert")
    joined = jnp.concatenate([array_piece.reshape(groups, -1) for array_piece in arrays], axis=1)
    spread = lax.all_to_all(joined, "expert", split_axis=0, concat_axis=0, tiled=True)
    ordered = jnp.take(spread, matching, axis=0)
    settled = lax.all_to_all(ordered, "expert", split_axis=0, concat_axis=0, tiled=True)
    pieces = []
    offset = 0
    for array_piece in arrays:
        length = array_piece.size // groups
        pieces.append(settled[:, offset : offset + length].reshape(array_piece.shape))
        offset = offset + length
    return pieces


def on_device_plain(tokens, grad_out, gate_weight, up_weight, down_weight, matching, block_counts):
    moved = relocate((gate_weight, up_weight, down_weight), matching)
    weight_gate, weight_up, weight_down = (
        lax.all_gather(moved[0], "dp", axis=1, tiled=True),
        lax.all_gather(moved[1], "dp", axis=1, tiled=True),
        lax.all_gather(moved[2], "dp", axis=2, tiled=True),
    )
    rows_full, grads_full = (
        lax.all_gather(tokens[0, 0], "hidden", axis=1, tiled=True),
        lax.all_gather(grad_out[0, 0], "hidden", axis=1, tiled=True),
    )
    blocks = rows_full.shape[0] // BLOCK
    width = rows_full.shape[1]
    owner, alive = block_owners(block_counts[0, 0], blocks)
    totals = expert_terms(
        rows_full.reshape(blocks, BLOCK, width),
        grads_full.reshape(blocks, BLOCK, width),
        weight_gate,
        weight_up,
        weight_down,
        owner,
        alive,
    )
    summed = (
        lax.psum_scatter(
            totals[0].astype(jnp.bfloat16), "dp", scatter_dimension=1, tiled=True
        ).astype(jnp.float32),
        lax.psum_scatter(
            totals[1].astype(jnp.bfloat16), "dp", scatter_dimension=1, tiled=True
        ).astype(jnp.float32),
        lax.psum_scatter(
            totals[2].astype(jnp.bfloat16), "dp", scatter_dimension=2, tiled=True
        ).astype(jnp.float32),
    )
    return (
        summed[0].astype(jnp.bfloat16),
        summed[1].astype(jnp.bfloat16),
        summed[2].astype(jnp.bfloat16),
    )


MESH = pl.DeviceIdType.MESH


def flip(index, bit):
    return index + bit - 2 * bit * ((index // bit) % 2)


def fused_kernel(
    exchange, experts, counts_ref, match_ref, tok_ref, grad_ref, gate_ref, up_ref, down_ref,
    out_gate, out_up, out_down,
    tok_all, grad_all, tok_dp, gu_all, dn_all, dn_end,
    own_gate, own_up, own_down, old_gate, old_up, old_down,
    acc_gu, acc_gh, acc_end, acc_out, gate_sel, up_sel, hid, hid_end, hid_out, hid_in, gh_out, gh_in,
    mask_own, mask_dp, pre, pre_dp, wide,
    part_own, part_end, core_own, core_end, sum_own, far_own, sum_far, sum_near, end_far, end_near, end_got,
    z_send, z_recv, y_send, y_recv, w_send, w_recv, t_send, t_recv, p_send, p_recv, m_send, m_recv,
    l_send, l_recv, h_send, h_recv, r_send, r_recv, e_send, e_recv, local_sem,
):
    zs = lax.axis_size("hidden")
    h = lax.axis_index("hidden")
    d = lax.axis_index("dp")
    p = lax.axis_index("expert")
    rows, feats = tok_ref.shape
    width = gate_ref.shape[2]
    blocks = rows // BLOCK
    tall = experts * width
    halves = [slice(0, rows // 2), slice(rows // 2, rows)]
    half_blocks = [range(0, blocks // 2), range(blocks // 2, blocks)]
    near, far = flip(d, 1), flip(d, 2)
    cross = flip(near, 2)
    partners = (near, far, cross)
    middle = (h > 0) & (h < zs - 1)
    border = (h == 0) | (h == zs - 1)
    way = 1 - 2 * (h // (zs // 2))
    inner, outer = h + way, h - way
    second, third = h + 2 * way, h + 3 * way
    full, half = jnp.float32, jnp.bfloat16

    def remote(source, target, send, recv, where):
        return pltpu.make_async_remote_copy(
            src_ref=source, dst_ref=target, send_sem=send, recv_sem=recv,
            device_id=where, device_id_type=MESH,
        )

    local = [
        pltpu.make_async_copy(source, target, local_sem.at[i])
        for i, (source, target) in enumerate((
            (gate_ref, own_gate), (up_ref, own_up), (down_ref, own_down),
            (tok_ref, tok_all.at[h]), (grad_ref, grad_all.at[h]),
        ))
    ]
    for copy in local:
        copy.start()

    barrier = pltpu.get_barrier_semaphore()
    for partner in partners:
        pl.semaphore_signal(barrier, inc=1, device_id={"dp": partner}, device_id_type=MESH)
    if exchange:
        pl.semaphore_signal(barrier, inc=1, device_id={"expert": 1 - p}, device_id_type=MESH)
    pl.semaphore_signal(barrier, inc=1, device_id={"hidden": inner}, device_id_type=MESH)

    @pl.when(middle)
    def _():
        pl.semaphore_signal(barrier, inc=1, device_id={"hidden": outer}, device_id_type=MESH)

    bounds = [counts_ref[0]]
    for e in range(1, experts):
        bounds.append(bounds[-1] + counts_ref[e])
    picks, masks, alive = [], [], []
    for b in range(blocks):
        owner = jnp.int32(0)
        for e in range(experts):
            owner = owner + jnp.where(b >= bounds[e], 1, 0)
        owner = jnp.minimum(owner, experts - 1)
        alive.append(jnp.where(b < bounds[-1], 1.0, 0.0))
        picks.append([jnp.where(owner == e, 1.0, 0.0) for e in range(experts)])
        masks.append([picks[b][e] * alive[b] for e in range(experts)])
        for e in range(experts):
            row = b * experts + e
            mask_own[row : row + 1, :] = jnp.full((1, mask_own.shape[1]), masks[b][e], full)

    peers = (h + zs - 1) // zs + (2 * zs - 2 - h) // zs
    pl.semaphore_wait(barrier, peers + (4 if exchange else 3))

    mine = (tok_ref, grad_ref)
    whole = (tok_all, grad_all)

    def line(kind, slab, r, outward=0, own=False):
        source = mine[kind].at[halves[r]] if own else whole[kind].at[slab, halves[r]]
        return remote(
            source, whole[kind].at[slab, halves[r]],
            z_send.at[outward, kind, slab, r], z_recv.at[kind, slab, r],
            {"hidden": outer if outward else inner},
        )

    def landed(kind, slab, r):
        line(kind, slab, r).wait_recv()

    def mask_copy(k):
        return remote(
            mask_own, mask_dp.at[k], m_send.at[k], m_recv.at[k], {"dp": partners[k]}
        )

    for r in range(2):
        line(0, h, r, 0, True).start()

        @pl.when(middle)
        def _():
            line(0, h, r, 1, True).start()

    @pl.when(border)
    def _():
        for r in range(2):
            line(1, h, r, 0, True).start()

    cut = feats // 2
    feat_halves = [slice(0, cut), slice(cut, feats)]

    def swap(i, e, f=None):
        source = (gate_ref, up_ref, down_ref)[i]
        target = (old_gate, old_up, old_down)[i]
        at = (e,) if f is None else (e, feat_halves[f])
        n = (i * experts + e) * 2 + (f or 0)
        return remote(source.at[at], target.at[at], y_send.at[n], y_recv.at[n], {"expert": 1 - p})

    swaps = []
    if exchange:
        swaps = [[swap(0, e, f), swap(1, e, f)] for e in range(experts) for f in range(2)]
        swaps += [[swap(2, e)] for e in range(experts)]
        for group in swaps:
            for copy in group:
                copy.start()
    for k in range(3):
        mask_copy(k).start()

    def chosen(own, other, at):
        if not exchange:
            return own[at]
        return jnp.where(match_ref[p] == p, own[at], other[at])

    chunks = 3 * experts

    def piece(j, slab):
        if j < 2 * experts:
            return gu_all.at[slab, j // 2, feat_halves[j % 2]]
        e = j - 2 * experts
        return dn_all.at[slab, e * width : (e + 1) * width]

    def spread(j, i):
        ref = piece(j, (d, d, far)[i])
        to = (far, near, near)[i]
        return remote(ref, ref, w_send.at[j, i], w_recv.at[j, i], {"dp": to})

    def arrived(j, i):
        ref = piece(j, (far, near, cross)[i])
        remote(ref, ref, w_send.at[j, i], w_recv.at[j, i], {"dp": near}).wait_recv()

    def take_weights(j):
        if exchange:
            for copy in swaps[j]:
                copy.wait_recv()
        if j < 2 * experts:
            at = (j // 2, feat_halves[j % 2])
            gu_all[d, j // 2, feat_halves[j % 2], :width] = chosen(own_gate, old_gate, at)
            gu_all[d, j // 2, feat_halves[j % 2], width:] = chosen(own_up, old_up, at)
        else:
            e = j - 2 * experts
            dn_all[d, e * width : (e + 1) * width, :] = chosen(own_down, old_down, e)
        spread(j, 0).start()
        spread(j, 1).start()

    def pass_weights(j):
        arrived(j, 0)
        spread(j, 2).start()

    def token_copy(k, r):
        return remote(
            tok_all.at[partners[k], halves[r]], tok_dp.at[k, halves[r]],
            t_send.at[k, r], t_recv.at[k, r], {"dp": partners[k]},
        )

    def share_tokens(slab, r):
        for k in range(3):
            @pl.when(slab == partners[k])
            def _():
                token_copy(k, r).start()

    def relay_tokens(r):
        @pl.when(middle)
        def _():
            landed(0, outer, r)
            line(0, outer, r).start()
            landed(0, inner, r)
            line(0, inner, r, 1).start()

    def relay_late(r):
        @pl.when(middle)
        def _():
            landed(0, second, r)
            line(0, second, r, 1).start()
            landed(1, outer, r)
            line(1, outer, r).start()

    for copy in local[:2]:
        copy.wait()
    take_weights(0)
    relay_tokens(0)
    take_weights(1)
    pass_weights(0)
    take_weights(2)
    relay_tokens(1)

    @pl.when(middle)
    def _():
        for r in range(2):
            line(1, h, r, 0, True).start()

    pass_weights(1)
    for j in range(3, 2 * experts):
        take_weights(j)
    for copy in local[2:]:
        copy.wait()
    pass_weights(2)
    take_weights(2 * experts)
    relay_late(0)
    for j in range(3, 2 * experts):
        pass_weights(j)
    for j in range(2 * experts + 1, chunks):
        take_weights(j)
    for r in range(2):
        share_tokens(h, r)

    @pl.when(border)
    def _():
        for r in range(2):
            landed(0, inner, r)
            share_tokens(inner, r)
        landed(0, second, 0)
        share_tokens(second, 0)

    @pl.when(middle)
    def _():
        for slab in (outer, inner):
            for r in range(2):
                share_tokens(slab, r)
        share_tokens(second, 0)

    pass_weights(2 * experts)
    relay_late(1)

    @pl.when(border)
    def _():
        landed(0, second, 1)

    share_tokens(second, 1)
    for j in range(2 * experts + 1, chunks):
        pass_weights(j)
    for j in range(chunks):
        arrived(j, 1)
        arrived(j, 2)

    core = d % 2
    lot = tall // 2

    def strip(index):
        return pl.ds(pl.multiple_of(index * lot, lot), lot)

    def lend(i, owner):
        slab = owner + (i + 1) * way
        return remote(
            dn_all.at[slab, strip(core)], dn_end.at[slab, strip(core)],
            l_send.at[0, i], l_recv.at[0, i], {"hidden": inner},
        )

    def lend_near(i, which):
        ref = dn_end.at[outer + (i + 1) * way, strip(which)]
        return remote(ref, ref, l_send.at[1, i], l_recv.at[1, i], {"dp": near})

    @pl.when(border)
    def _():
        for i in range(3):
            lend(i, h).start()

    def add_tokens(slabs, r, first):
        for e in range(experts):
            total = None if first else acc_gu[e, halves[r]]
            for slab in slabs:
                term = jnp.dot(tok_all[slab, halves[r]], gu_all[slab, e], preferred_element_type=full)
                total = term if total is None else total + term
            acc_gu[e, halves[r]] = total

    def add_grads(slabs, r, first, total_ref=acc_gh, weight=dn_all):
        total = None if first else total_ref[halves[r]]
        for slab in slabs:
            term = lax.dot_general(
                grad_all[slab, halves[r]], weight[slab], (((1,), (1,)), ((), ())),
                preferred_element_type=full,
            )
            total = term if total is None else total + term
        total_ref[halves[r]] = total

    def activate(r):
        for b in half_blocks[r]:
            part = slice(b * BLOCK, (b + 1) * BLOCK)
            both = sum(acc_gu[e, part] * picks[b][e] for e in range(experts))
            gate_value, up_value = both[:, :width], both[:, width:]
            gate_sel[part] = gate_value
            up_sel[part] = up_value
            hidden = gate_value * jax.nn.sigmoid(gate_value) * up_value
            hid_out[part] = (hidden * alive[b]).astype(half)
            for e in range(experts):
                hid[part, e * width : (e + 1) * width] = (hidden * masks[b][e]).astype(half)

    def hidden_out(r):
        return remote(
            hid_out.at[halves[r]], hid_in.at[halves[r]], h_send.at[0, r], h_recv.at[0, r],
            {"hidden": inner},
        )

    def grads_out(r):
        return remote(
            gh_out.at[halves[r]], gh_in.at[halves[r]], h_send.at[1, r], h_recv.at[1, r],
            {"hidden": outer},
        )

    def make_pre(r, extra=None):
        for b in half_blocks[r]:
            part = slice(b * BLOCK, (b + 1) * BLOCK)
            gate_value, up_value = gate_sel[part], up_sel[part]
            grad_hidden = sum(
                acc_gh[part, e * width : (e + 1) * width] * picks[b][e] for e in range(experts)
            )
            if extra is not None:
                grad_hidden = grad_hidden + extra[part].astype(full)
            s = jax.nn.sigmoid(gate_value)
            grad_gate = grad_hidden * up_value * s * (1.0 + gate_value * (1.0 - s))
            grad_up = grad_hidden * gate_value * s
            pre[part, :width] = (grad_gate * alive[b]).astype(half)
            pre[part, width:] = (grad_up * alive[b]).astype(half)
            for e in range(experts):
                at = e * 2 * width
                wide[3, part, at : at + width] = (grad_gate * masks[b][e]).astype(half)
                wide[3, part, at + width : at + 2 * width] = (grad_up * masks[b][e]).astype(half)

    def pre_copy(k, r):
        source = pre_dp.at[1, halves[r]] if k == 2 else pre.at[halves[r]]
        to = far if k == 1 else near
        return remote(
            source, pre_dp.at[k, halves[r]], p_send.at[k, r], p_recv.at[k, r], {"dp": to}
        )

    def send_pre(r):
        pre_copy(1, r).start()
        pre_copy(0, r).start()

    parts, cores = (part_own, part_end), (core_own, core_end)
    lefts = (hid, hid_end)

    def core_copy(kind, i):
        slab = (cross, near)[i]
        return remote(
            parts[kind].at[slab], cores[kind].at[i], r_send.at[kind, i], r_recv.at[kind, i],
            {"dp": near},
        )

    def down_term(kind, slab):
        parts[kind][slab] = lax.dot_general(
            lefts[kind][...], grad_all[slab], (((0,), (0,)), ((), ())), preferred_element_type=full
        ).astype(half)
        for i in range(2):
            @pl.when(slab == (cross, near)[i])
            def _():
                core_copy(kind, i).start()

    def core_sum(kind, i):
        slab = (far, d)[i]
        return parts[kind][slab].astype(full) + cores[kind][i].astype(full)

    own_far = remote(sum_own, far_own, r_send.at[2, 0], r_recv.at[2, 0], {"dp": far})
    end_far_out = remote(sum_far, end_far, e_send.at[0], e_recv.at[0], {"hidden": outer})
    end_near_out = remote(sum_near, end_near, e_send.at[1], e_recv.at[1], {"hidden": outer})
    end_cross = remote(end_far, end_got, e_send.at[2], e_recv.at[2], {"dp": far})

    def send_end_far():
        core_copy(1, 0).wait_recv()
        sum_far[...] = core_sum(1, 0).astype(half)
        end_far_out.start()

    @pl.when(border)
    def _():
        for r in range(2):
            add_tokens((h, inner, second), r, True)
            add_grads((h,), r, True)
        for r in range(2):
            landed(0, third, r)
            share_tokens(third, r)
            add_tokens((third,), r, False)
            activate(r)
            hidden_out(r).start()
        grads_out(0).wait_recv()
        make_pre(0, gh_in)
        send_pre(0)

        @pl.when(far != third)
        def _():
            end_far_out.wait_recv()
            end_cross.start()

        grads_out(1).wait_recv()
        make_pre(1, gh_in)
        send_pre(1)

        @pl.when(far == third)
        def _():
            end_far_out.wait_recv()
            end_cross.start()

    @pl.when(middle)
    def _():
        for r in range(2):
            add_tokens((h, outer, inner, second), r, True)
            activate(r)
            add_grads((h, outer), r, True)
        for slab in (h, outer):
            down_term(0, slab)
        lend(0, outer).wait_recv()
        lend_near(0, core).start()
        landed(1, inner, 0)
        add_grads((inner,), 0, False)
        lend(1, outer).wait_recv()
        lend_near(1, core).start()
        landed(1, inner, 1)
        add_grads((inner,), 1, False)
        lend(2, outer).wait_recv()
        lend_near(2, core).start()
        down_term(0, inner)
        for i in range(3):
            lend_near(i, 1 - core).wait_recv()
        for r in range(2):
            add_grads((h, inner), r, True, acc_end, dn_end)
        for r in range(2):
            hidden_out(r).wait_recv()
            for b in half_blocks[r]:
                part = slice(b * BLOCK, (b + 1) * BLOCK)
                value = hid_in[part].astype(full)
                for e in range(experts):
                    hid_end[part, e * width : (e + 1) * width] = (value * masks[b][e]).astype(half)

        def last_grads(r):
            landed(1, second, r)
            add_grads((second,), r, False, acc_end, dn_end)
            for b in half_blocks[r]:
                part = slice(b * BLOCK, (b + 1) * BLOCK)
                gh_out[part] = sum(
                    acc_end[part, e * width : (e + 1) * width] * picks[b][e] for e in range(experts)
                ).astype(half)
            grads_out(r).start()
            add_grads((second,), r, False)
            make_pre(r)
            send_pre(r)

        last_grads(0)
        for slab in (h, outer, inner):
            down_term(1, slab)

        @pl.when(far != second)
        def _():
            send_end_far()

        last_grads(1)
        down_term(1, second)
        down_term(0, second)

        @pl.when(far == second)
        def _():
            send_end_far()

        core_copy(0, 0).wait_recv()
        sum_own[...] = core_sum(0, 0).astype(half)
        own_far.start()
        core_copy(1, 1).wait_recv()
        sum_near[...] = core_sum(1, 1).astype(half)
        end_near_out.start()

    def widen(k, r):
        for b in half_blocks[r]:
            part = slice(b * BLOCK, (b + 1) * BLOCK)
            for e in range(experts):
                row = b * experts + e
                keep = mask_dp[k, row : row + 1, :]
                for i in range(2):
                    at = (e * 2 + i) * width
                    value = pre_dp[k, part, i * width : (i + 1) * width].astype(full)
                    wide[k, part, at : at + width] = (value * keep).astype(half)

    def gate_term(k, r):
        left = tok_all[d, halves[r]] if k == 3 else tok_dp[k, halves[r]]
        return lax.dot_general(
            left, wide[k, halves[r]], (((0,), (0,)), ((), ())), preferred_element_type=full
        )

    for k in range(3):
        mask_copy(k).wait_recv()
    for r in range(2):
        token_copy(0, r).wait_recv()
        pre_copy(0, r).wait_recv()
        widen(0, r)
    acc_out[...] = gate_term(3, 0) + gate_term(3, 1) + gate_term(0, 0) + gate_term(0, 1)
    for r in range(2):
        pre_copy(1, r).wait_recv()
        pre_copy(2, r).start()
        widen(1, r)
        for k in (1, 2):
            token_copy(k, r).wait_recv()
        term = gate_term(1, r)
        pre_copy(2, r).wait_recv()
        widen(2, r)
        term = term + gate_term(2, r)
        total = acc_out[...] + term
        if r == 0:
            acc_out[...] = total
        else:
            for e in range(experts):
                at = e * 2 * width
                out_gate[e] = total[:, at : at + width].astype(half)
                out_up[e] = total[:, at + width : at + 2 * width].astype(half)

    @pl.when(middle)
    def _():
        core_copy(0, 1).wait_recv()
        own_far.wait_recv()
        total = core_sum(0, 1) + far_own[...].astype(full)
        for e in range(experts):
            out_down[e] = total[e * width : (e + 1) * width].astype(half)

    @pl.when(border)
    def _():
        end_near_out.wait_recv()
        end_cross.wait_recv()
        total = end_near[...].astype(full) + end_got[...].astype(full)
        for e in range(experts):
            out_down[e] = total[e * width : (e + 1) * width].astype(half)

    for r in range(2):
        line(0, h, r, 0, True).wait_send()
        line(1, h, r, 0, True).wait_send()
    for k in range(3):
        mask_copy(k).wait_send()
        for r in range(2):
            token_copy(k, r).wait_send()
            pre_copy(k, r).wait_send()
    for j in range(chunks):
        for i in range(3):
            spread(j, i).wait_send()
    if exchange:
        for group in swaps:
            for copy in group:
                copy.wait_send()

    @pl.when(middle)
    def _():
        for r in range(2):
            line(0, h, r, 1, True).wait_send()
            line(0, outer, r).wait_send()
            line(1, outer, r).wait_send()
            line(0, inner, r, 1).wait_send()
            line(0, second, r, 1).wait_send()
            grads_out(r).wait_send()
        for i in range(3):
            lend_near(i, core).wait_send()
        for kind in range(2):
            for i in range(2):
                core_copy(kind, i).wait_send()
        own_far.wait_send()
        end_far_out.wait_send()
        end_near_out.wait_send()

    @pl.when(border)
    def _():
        for r in range(2):
            hidden_out(r).wait_send()
        for i in range(3):
            lend(i, h).wait_send()
        end_cross.wait_send()


def settle_kernel(*refs):
    count = len(refs) // 2
    for source, target in zip(refs[:count], refs[count:]):
        target[...] = source[...]


def settle(arrays):
    count = len(arrays)
    vmem = pl.BlockSpec(memory_space=pltpu.VMEM)
    return pl.pallas_call(
        settle_kernel,
        out_shape=tuple(jax.ShapeDtypeStruct(a.shape, a.dtype) for a in arrays),
        in_specs=[vmem] * count,
        out_specs=(vmem,) * count,
    )(*arrays)


def on_device_fused(tokens, grad_out, gate_weight, up_weight, down_weight, matching, block_counts):
    groups = lax.axis_size("expert")
    zs = lax.axis_size("hidden")
    ds = lax.axis_size("dp")
    exchange = groups == 2
    if not exchange:
        gate_weight, up_weight, down_weight = relocate(
            (gate_weight, up_weight, down_weight), matching
        )
        matching = jnp.zeros_like(matching)
    rows, feats = tokens.shape[2:]
    experts, part, width = gate_weight.shape
    vmem = pl.BlockSpec(memory_space=pltpu.VMEM)
    smem = pl.BlockSpec(memory_space=pltpu.SMEM)
    half, full = jnp.bfloat16, jnp.float32
    wide = experts * 2 * width
    tall = experts * width
    chunks = 3 * experts
    dma = pltpu.SemaphoreType.DMA
    down = pltpu.VMEM((tall, part), half)
    narrow = pltpu.VMEM((rows, width), half)
    mask = (experts * (rows // BLOCK), width)
    grads = pl.pallas_call(
        functools.partial(fused_kernel, exchange, experts),
        out_shape=tuple(
            jax.ShapeDtypeStruct(w.shape, half) for w in (gate_weight, up_weight, down_weight)
        ),
        in_specs=[smem, smem] + [pl.BlockSpec(memory_space=pltpu.HBM)] * 5,
        out_specs=(vmem,) * 3,
        scratch_shapes=[
            pltpu.VMEM((zs, rows, feats), half),
            pltpu.VMEM((zs, rows, feats), half),
            pltpu.VMEM((3, rows, feats), half),
            pltpu.VMEM((ds, experts, part, 2 * width), half),
            pltpu.VMEM((ds, tall, part), half),
            pltpu.VMEM((ds, tall, part), half),
            pltpu.VMEM(gate_weight.shape, half),
            pltpu.VMEM(up_weight.shape, half),
            pltpu.VMEM(down_weight.shape, half),
            pltpu.VMEM(gate_weight.shape, half),
            pltpu.VMEM(up_weight.shape, half),
            pltpu.VMEM(down_weight.shape, half),
            pltpu.VMEM((experts, rows, 2 * width), full),
            pltpu.VMEM((rows, tall), full),
            pltpu.VMEM((rows, tall), full),
            pltpu.VMEM((feats, wide), full),
            pltpu.VMEM((rows, width), full),
            pltpu.VMEM((rows, width), full),
            pltpu.VMEM((rows, tall), half),
            pltpu.VMEM((rows, tall), half),
            narrow, narrow, narrow, narrow,
            pltpu.VMEM(mask, full),
            pltpu.VMEM((3,) + mask, full),
            pltpu.VMEM((rows, 2 * width), half),
            pltpu.VMEM((3, rows, 2 * width), half),
            pltpu.VMEM((4, rows, wide), half),
            pltpu.VMEM((ds, tall, part), half),
            pltpu.VMEM((ds, tall, part), half),
            pltpu.VMEM((2, tall, part), half),
            pltpu.VMEM((2, tall, part), half),
            down, down, down, down, down, down, down,
            dma((2, 2, zs, 2)),
            dma((2, zs, 2)),
            dma((3 * experts * 2,)),
            dma((3 * experts * 2,)),
            dma((chunks, 3)),
            dma((chunks, 3)),
            dma((3, 2)),
            dma((3, 2)),
            dma((3, 2)),
            dma((3, 2)),
            dma((3,)),
            dma((3,)),
            dma((2, 3)),
            dma((2, 3)),
            dma((2, 2)),
            dma((2, 2)),
            dma((3, 2)),
            dma((3, 2)),
            dma((3,)),
            dma((3,)),
            dma((5,)),
        ],
        compiler_params=pltpu.CompilerParams(
            collective_id=0, has_side_effects=True, vmem_limit_bytes=48 * 1024 * 1024
        ),
    )(
        block_counts.reshape(-1), matching, tokens.reshape(rows, feats),
        grad_out.reshape(rows, feats), gate_weight, up_weight, down_weight,
    )
    return settle(grads)


def fused_fits(mesh):
    return mesh.shape["dp"] == 4 and mesh.shape["hidden"] == 4


def solution(mesh):
    on_device = on_device_fused if fused_fits(mesh) else on_device_plain
    in_specs = (
        P("expert", "dp", None, "hidden"),
        P("expert", "dp", None, "hidden"),
        P("expert", "dp", "hidden"),
        P("expert", "dp", "hidden"),
        P("expert", "hidden", "dp"),
        P(),
        P("expert", "dp", None),
    )
    out_specs = (
        P("expert", "dp", "hidden"),
        P("expert", "dp", "hidden"),
        P("expert", "hidden", "dp"),
    )
    return jax.shard_map(
        on_device, mesh=mesh, in_specs=in_specs, out_specs=out_specs, check_vma=False
    )
```

```python
import functools

import jax
import jax.numpy as jnp
from jax import lax
from jax.experimental import pallas as pl
from jax.experimental.pallas import tpu as pltpu
from jax.sharding import PartitionSpec as P

BLOCK = 128


def contract_rows(left, right):
    return lax.dot_general(
        left, right, (((0,), (0,)), ((), ())), preferred_element_type=jnp.float32
    )


def block_owners(counts, blocks):
    bounds = jnp.cumsum(counts)
    index = jnp.arange(blocks, dtype=jnp.int32)
    owner = jnp.sum((index[:, None] >= bounds[None, :]).astype(jnp.int32), axis=1)
    owner = jnp.minimum(owner, counts.shape[0] - 1)
    alive = (index < bounds[-1]).astype(jnp.float32)
    return (owner, alive)


def add_into(total, term, expert):
    current = lax.dynamic_index_in_dim(total, expert, 0, keepdims=True)
    return lax.dynamic_update_index_in_dim(total, current + term[None], expert, 0)


def expert_terms(row_blocks, grad_blocks, weight_gate, weight_up, weight_down, owner, alive):
    zeros_gate = jnp.zeros(weight_gate.shape, jnp.float32)
    zeros_down = jnp.zeros(weight_down.shape, jnp.float32)

    def step(carry, inputs):
        total_gate, total_up, total_down = carry
        row_block, grad_block, expert, live = inputs
        gate_matrix = lax.dynamic_index_in_dim(weight_gate, expert, 0, keepdims=False)
        up_matrix = lax.dynamic_index_in_dim(weight_up, expert, 0, keepdims=False)
        down_matrix = lax.dynamic_index_in_dim(weight_down, expert, 0, keepdims=False)
        gate_value = jnp.dot(row_block, gate_matrix, preferred_element_type=jnp.float32)
        up_value = jnp.dot(row_block, up_matrix, preferred_element_type=jnp.float32)
        sigmoid_gate = jax.nn.sigmoid(gate_value)
        activated = gate_value * sigmoid_gate
        hidden = (activated * up_value * live).astype(jnp.bfloat16)
        grad_hidden = lax.dot_general(
            grad_block, down_matrix, (((1,), (1,)), ((), ())), preferred_element_type=jnp.float32
        )
        grad_gate = (
            grad_hidden * up_value * sigmoid_gate * (1.0 + gate_value * (1.0 - sigmoid_gate)) * live
        ).astype(jnp.bfloat16)
        grad_up = (grad_hidden * activated * live).astype(jnp.bfloat16)
        total_gate = add_into(total_gate, contract_rows(row_block, grad_gate), expert)
        total_up = add_into(total_up, contract_rows(row_block, grad_up), expert)
        total_down = add_into(total_down, contract_rows(hidden, grad_block), expert)
        return ((total_gate, total_up, total_down), None)

    totals, unused = lax.scan(
        step, (zeros_gate, zeros_gate, zeros_down), (row_blocks, grad_blocks, owner, alive)
    )
    return totals


def relocate(arrays, matching):
    groups = lax.axis_size("expert")
    joined = jnp.concatenate([array_piece.reshape(groups, -1) for array_piece in arrays], axis=1)
    spread = lax.all_to_all(joined, "expert", split_axis=0, concat_axis=0, tiled=True)
    ordered = jnp.take(spread, matching, axis=0)
    settled = lax.all_to_all(ordered, "expert", split_axis=0, concat_axis=0, tiled=True)
    pieces = []
    offset = 0
    for array_piece in arrays:
        length = array_piece.size // groups
        pieces.append(settled[:, offset : offset + length].reshape(array_piece.shape))
        offset = offset + length
    return pieces


def on_device_plain(tokens, grad_out, gate_weight, up_weight, down_weight, matching, block_counts):
    moved = relocate((gate_weight, up_weight, down_weight), matching)
    weight_gate, weight_up, weight_down = (
        lax.all_gather(moved[0], "dp", axis=1, tiled=True),
        lax.all_gather(moved[1], "dp", axis=1, tiled=True),
        lax.all_gather(moved[2], "dp", axis=2, tiled=True),
    )
    rows_full, grads_full = (
        lax.all_gather(tokens[0, 0], "hidden", axis=1, tiled=True),
        lax.all_gather(grad_out[0, 0], "hidden", axis=1, tiled=True),
    )
    blocks = rows_full.shape[0] // BLOCK
    width = rows_full.shape[1]
    owner, alive = block_owners(block_counts[0, 0], blocks)
    totals = expert_terms(
        rows_full.reshape(blocks, BLOCK, width),
        grads_full.reshape(blocks, BLOCK, width),
        weight_gate,
        weight_up,
        weight_down,
        owner,
        alive,
    )
    summed = (
        lax.psum_scatter(
            totals[0].astype(jnp.bfloat16), "dp", scatter_dimension=1, tiled=True
        ).astype(jnp.float32),
        lax.psum_scatter(
            totals[1].astype(jnp.bfloat16), "dp", scatter_dimension=1, tiled=True
        ).astype(jnp.float32),
        lax.psum_scatter(
            totals[2].astype(jnp.bfloat16), "dp", scatter_dimension=2, tiled=True
        ).astype(jnp.float32),
    )
    return (
        summed[0].astype(jnp.bfloat16),
        summed[1].astype(jnp.bfloat16),
        summed[2].astype(jnp.bfloat16),
    )


MESH = pl.DeviceIdType.MESH


def flip(index, bit):
    return index + bit - 2 * bit * ((index // bit) % 2)


def fused_kernel(
    exchange, experts, counts_ref, match_ref, tok_ref, grad_ref, gate_ref, up_ref, down_ref,
    out_gate, out_up, out_down,
    tok_all, grad_all, tok_dp, gu_all, dn_all, dn_end,
    own_gate, own_up, own_down, old_gate, old_up, old_down,
    acc_gu, acc_gh, acc_end, acc_out, gate_sel, up_sel, hid, hid_end, hid_out, hid_in, gh_out, gh_in,
    mask_own, mask_dp, pre, pre_dp, wide,
    part_own, part_end, core_own, core_end, sum_own, far_own, sum_far, sum_near, end_far, end_near, end_got,
    z_send, z_recv, y_send, y_recv, w_send, w_recv, t_send, t_recv, p_send, p_recv, m_send, m_recv,
    l_send, l_recv, h_send, h_recv, r_send, r_recv, e_send, e_recv, local_sem,
):
    zs = lax.axis_size("hidden")
    h = lax.axis_index("hidden")
    d = lax.axis_index("dp")
    p = lax.axis_index("expert")
    rows, feats = tok_ref.shape
    width = gate_ref.shape[2]
    blocks = rows // BLOCK
    tall = experts * width
    halves = [slice(0, rows // 2), slice(rows // 2, rows)]
    half_blocks = [range(0, blocks // 2), range(blocks // 2, blocks)]
    edges = (0, rows // 2, rows // 4 * 3, rows)
    steps = range(len(edges) - 1)
    cuts = [slice(edges[q], edges[q + 1]) for q in steps]
    cut_blocks = [range(edges[q] // BLOCK, edges[q + 1] // BLOCK) for q in steps]
    near, far = flip(d, 1), flip(d, 2)
    cross = flip(near, 2)
    partners = (near, far, cross)
    middle = (h > 0) & (h < zs - 1)
    border = (h == 0) | (h == zs - 1)
    way = 1 - 2 * (h // (zs // 2))
    inner, outer = h + way, h - way
    second, third = h + 2 * way, h + 3 * way
    full, half = jnp.float32, jnp.bfloat16

    def remote(source, target, send, recv, where):
        return pltpu.make_async_remote_copy(
            src_ref=source, dst_ref=target, send_sem=send, recv_sem=recv,
            device_id=where, device_id_type=MESH,
        )

    local = [
        pltpu.make_async_copy(source, target, local_sem.at[i])
        for i, (source, target) in enumerate((
            (gate_ref, own_gate), (up_ref, own_up), (down_ref, own_down),
            (tok_ref, tok_all.at[h]), (grad_ref, grad_all.at[h]),
        ))
    ]
    for copy in local:
        copy.start()

    barrier = pltpu.get_barrier_semaphore()
    for partner in partners:
        pl.semaphore_signal(barrier, inc=1, device_id={"dp": partner}, device_id_type=MESH)
    if exchange:
        pl.semaphore_signal(barrier, inc=1, device_id={"expert": 1 - p}, device_id_type=MESH)
    pl.semaphore_signal(barrier, inc=1, device_id={"hidden": inner}, device_id_type=MESH)

    @pl.when(middle)
    def _():
        pl.semaphore_signal(barrier, inc=1, device_id={"hidden": outer}, device_id_type=MESH)

    bounds = [counts_ref[0]]
    for e in range(1, experts):
        bounds.append(bounds[-1] + counts_ref[e])
    picks, masks, alive = [], [], []
    for b in range(blocks):
        owner = jnp.int32(0)
        for e in range(experts):
            owner = owner + jnp.where(b >= bounds[e], 1, 0)
        owner = jnp.minimum(owner, experts - 1)
        alive.append(jnp.where(b < bounds[-1], 1.0, 0.0))
        picks.append([jnp.where(owner == e, 1.0, 0.0) for e in range(experts)])
        masks.append([picks[b][e] * alive[b] for e in range(experts)])
        for e in range(experts):
            row = b * experts + e
            mask_own[row : row + 1, :] = jnp.full((1, mask_own.shape[1]), masks[b][e], full)

    peers = (h + zs - 1) // zs + (2 * zs - 2 - h) // zs
    pl.semaphore_wait(barrier, peers + (4 if exchange else 3))

    mine = (tok_ref, grad_ref)
    whole = (tok_all, grad_all)

    def line(kind, slab, r, outward=0, own=False, fine=False):
        part = (cuts if fine else halves)[r]
        source = mine[kind].at[part] if own else whole[kind].at[slab, part]
        return remote(
            source, whole[kind].at[slab, part],
            z_send.at[outward, kind, slab, r], z_recv.at[kind, slab, r],
            {"hidden": outer if outward else inner},
        )

    def landed(kind, slab, r, fine=False):
        line(kind, slab, r, fine=fine).wait_recv()

    def place(k, q):
        size = edges[q + 1] - edges[q]
        start = 2 * edges[q] + (0 if k in (1, 3) else size)
        return (0 if k in (0, 3) else 1), slice(start, start + size)

    def pair(q):
        return slice(2 * edges[q], 2 * edges[q + 1])

    def token_copy(k, q, own=False):
        source = tok_ref.at[cuts[q]] if own else tok_all.at[partners[k], cuts[q]]
        return remote(
            source, tok_dp.at[place(k, q)],
            t_send.at[k, q], t_recv.at[k, q], {"dp": partners[k]},
        )

    def mask_copy(k):
        return remote(
            mask_own, mask_dp.at[k], m_send.at[k], m_recv.at[k], {"dp": partners[k]}
        )

    for r in range(2):
        line(0, h, r, 0, True).start()

        @pl.when(middle)
        def _():
            line(0, h, r, 1, True).start()

    @pl.when(border)
    def _():
        for q in steps:
            line(1, h, q, 0, True, True).start()

    feat_halves = [slice(0, feats // 2), slice(feats // 2, feats)]

    def swap(i, e, f=None):
        source = (gate_ref, up_ref, down_ref)[i]
        target = (old_gate, old_up, old_down)[i]
        at = (e,) if f is None else (e, feat_halves[f])
        n = (i * experts + e) * 2 + (f or 0)
        return remote(source.at[at], target.at[at], y_send.at[n], y_recv.at[n], {"expert": 1 - p})

    swaps = []
    if exchange:
        swaps = [[swap(0, e, f), swap(1, e, f)] for e in range(experts) for f in range(2)]
        swaps += [[swap(2, e)] for e in range(experts)]
        for group in swaps:
            for copy in group:
                copy.start()
    for k in range(3):
        mask_copy(k).start()

    def chosen(own, other, at):
        if not exchange:
            return own[at]
        return jnp.where(match_ref[p] == p, own[at], other[at])

    chunks = 3 * experts

    def piece(j, slab):
        if j < 2 * experts:
            return gu_all.at[slab, j // 2, feat_halves[j % 2]]
        e = j - 2 * experts
        return dn_all.at[slab, e * width : (e + 1) * width]

    def spread(j, i):
        ref = piece(j, (d, d, far)[i])
        to = (far, near, near)[i]
        return remote(ref, ref, w_send.at[j, i], w_recv.at[j, i], {"dp": to})

    def arrived(j, i):
        ref = piece(j, (far, near, cross)[i])
        remote(ref, ref, w_send.at[j, i], w_recv.at[j, i], {"dp": near}).wait_recv()

    def take_weights(j):
        if exchange:
            for copy in swaps[j]:
                copy.wait_recv()
        if j < 2 * experts:
            at = (j // 2, feat_halves[j % 2])
            gu_all[d, j // 2, feat_halves[j % 2], :width] = chosen(own_gate, old_gate, at)
            gu_all[d, j // 2, feat_halves[j % 2], width:] = chosen(own_up, old_up, at)
        else:
            e = j - 2 * experts
            dn_all[d, e * width : (e + 1) * width, :] = chosen(own_down, old_down, e)
        spread(j, 0).start()
        spread(j, 1).start()

    def pass_weights(j):
        arrived(j, 0)
        spread(j, 2).start()

    def share_tokens(slab, r):
        for k in range(3):
            @pl.when(slab == partners[k])
            def _():
                for q in ((0,) if r == 0 else steps[1:]):
                    token_copy(k, q).start()

    def relay_tokens(r):
        @pl.when(middle)
        def _():
            landed(0, outer, r)
            line(0, outer, r).start()
            landed(0, inner, r)
            line(0, inner, r, 1).start()

    def relay_late(r):
        @pl.when(middle)
        def _():
            landed(0, second, r)
            line(0, second, r, 1).start()
            for q in ((0,) if r == 0 else steps[1:]):
                landed(1, outer, q, True)
                line(1, outer, q, fine=True).start()

    for copy in local[:2]:
        copy.wait()
    take_weights(0)
    relay_tokens(0)
    take_weights(1)
    pass_weights(0)
    take_weights(2)
    relay_tokens(1)

    @pl.when(middle)
    def _():
        for r in range(2):
            line(1, h, r, 0, True).start()

    pass_weights(1)
    for j in range(3, 2 * experts):
        take_weights(j)
    for copy in local[2:]:
        copy.wait()
    pass_weights(2)
    take_weights(2 * experts)
    relay_late(0)
    for j in range(3, 2 * experts):
        pass_weights(j)
    for j in range(2 * experts + 1, chunks):
        take_weights(j)
    for r in range(2):
        share_tokens(h, r)

    @pl.when(border)
    def _():
        for r in range(2):
            landed(0, inner, r)
            share_tokens(inner, r)
        landed(0, second, 0)
        share_tokens(second, 0)

    @pl.when(middle)
    def _():
        for slab in (outer, inner):
            for r in range(2):
                share_tokens(slab, r)
        share_tokens(second, 0)

    pass_weights(2 * experts)
    relay_late(1)

    @pl.when(border)
    def _():
        landed(0, second, 1)

    share_tokens(second, 1)
    for j in range(2 * experts + 1, chunks):
        pass_weights(j)
    for j in range(chunks):
        arrived(j, 1)
        arrived(j, 2)

    core = d % 2
    lot = tall // 2

    def strip(index):
        return pl.ds(pl.multiple_of(index * lot, lot), lot)

    def lend(i, owner):
        slab = owner + (i + 1) * way
        return remote(
            dn_all.at[slab, strip(core)], dn_end.at[slab, strip(core)],
            l_send.at[0, i], l_recv.at[0, i], {"hidden": inner},
        )

    def lend_near(i, which):
        ref = dn_end.at[outer + (i + 1) * way, strip(which)]
        return remote(ref, ref, l_send.at[1, i], l_recv.at[1, i], {"dp": near})

    @pl.when(border)
    def _():
        for i in range(3):
            lend(i, h).start()

    def add_tokens(slabs, r, first):
        for e in range(experts):
            total = None if first else acc_gu[e, halves[r]]
            for slab in slabs:
                term = jnp.dot(tok_all[slab, halves[r]], gu_all[slab, e], preferred_element_type=full)
                total = term if total is None else total + term
            acc_gu[e, halves[r]] = total

    def add_grads(slabs, part, first, total_ref=acc_gh, weight=dn_all):
        total = None if first else total_ref[part]
        for slab in slabs:
            term = lax.dot_general(
                grad_all[slab, part], weight[slab], (((1,), (1,)), ((), ())),
                preferred_element_type=full,
            )
            total = term if total is None else total + term
        total_ref[part] = total

    def activate(r):
        for b in half_blocks[r]:
            part = slice(b * BLOCK, (b + 1) * BLOCK)
            both = sum(acc_gu[e, part] * picks[b][e] for e in range(experts))
            gate_value, up_value = both[:, :width], both[:, width:]
            gate_sel[part] = gate_value
            up_sel[part] = up_value
            hidden = gate_value * jax.nn.sigmoid(gate_value) * up_value
            hid_out[part] = (hidden * alive[b]).astype(half)
            for e in range(experts):
                hid[part, e * width : (e + 1) * width] = (hidden * masks[b][e]).astype(half)

    def hidden_out(r):
        return remote(
            hid_out.at[halves[r]], hid_in.at[halves[r]], h_send.at[0, r], h_recv.at[0, r],
            {"hidden": inner},
        )

    def grads_out(q):
        return remote(
            gh_out.at[cuts[q]], gh_in.at[cuts[q]], h_send.at[1, q], h_recv.at[1, q],
            {"hidden": outer},
        )

    def block_place(k, q, b):
        side, spot = place(k, q)
        start = spot.start + b * BLOCK - edges[q]
        return side, slice(start, start + BLOCK)

    def make_pre(q, extra=None):
        for b in cut_blocks[q]:
            part = slice(b * BLOCK, (b + 1) * BLOCK)
            side, spot = block_place(3, q, b)
            gate_value, up_value = gate_sel[part], up_sel[part]
            grad_hidden = sum(
                acc_gh[part, e * width : (e + 1) * width] * picks[b][e] for e in range(experts)
            )
            if extra is not None:
                grad_hidden = grad_hidden + extra[part].astype(full)
            s = jax.nn.sigmoid(gate_value)
            grad_gate = grad_hidden * up_value * s * (1.0 + gate_value * (1.0 - s))
            grad_up = grad_hidden * gate_value * s
            pre[part, :width] = (grad_gate * alive[b]).astype(half)
            pre[part, width:] = (grad_up * alive[b]).astype(half)
            for e in range(experts):
                at = e * 2 * width
                wide[side, spot, at : at + width] = (grad_gate * masks[b][e]).astype(half)
                wide[side, spot, at + width : at + 2 * width] = (grad_up * masks[b][e]).astype(half)

    def pre_copy(k, q):
        source = pre_dp.at[1, cuts[q]] if k == 2 else pre.at[cuts[q]]
        to = far if k == 1 else near
        return remote(
            source, pre_dp.at[k, cuts[q]], p_send.at[k, q], p_recv.at[k, q], {"dp": to}
        )

    def send_pre(q):
        pre_copy(1, q).start()
        pre_copy(0, q).start()

    parts, cores = (part_own, part_end), (core_own, core_end)
    lefts = (hid, hid_end)

    def core_copy(kind, i):
        slab = (cross, near)[i]
        return remote(
            parts[kind].at[slab], cores[kind].at[i], r_send.at[kind, i], r_recv.at[kind, i],
            {"dp": near},
        )

    def down_term(kind, slab, left=None):
        parts[kind][slab] = lax.dot_general(
            (lefts[kind] if left is None else left)[...], grad_all[slab], (((0,), (0,)), ((), ())), preferred_element_type=full
        ).astype(half)
        for i in range(2):
            @pl.when(slab == (cross, near)[i])
            def _():
                core_copy(kind, i).start()

    def core_sum(kind, i):
        slab = (far, d)[i]
        return parts[kind][slab].astype(full) + cores[kind][i].astype(full)

    own_far = remote(sum_own, far_own, r_send.at[2, 0], r_recv.at[2, 0], {"dp": far})
    end_near_out = remote(sum_near, end_near, e_send.at[0, 0], e_recv.at[0, 0], {"hidden": outer})

    def end_far_out(e):
        part = slice(e * width, (e + 1) * width)
        return remote(
            sum_far.at[part], end_far.at[part], e_send.at[1, e], e_recv.at[1, e], {"hidden": outer}
        )

    def end_cross(e):
        part = slice(e * width, (e + 1) * width)
        return remote(
            end_far.at[part], end_got.at[part], e_send.at[2, e], e_recv.at[2, e], {"dp": far}
        )

    def sum_end_far():
        core_copy(1, 0).wait_recv()
        sum_far[...] = core_sum(1, 0).astype(half)

    def widen(k, q):
        for b in cut_blocks[q]:
            part = slice(b * BLOCK, (b + 1) * BLOCK)
            side, spot = block_place(k, q, b)
            for e in range(experts):
                row = b * experts + e
                keep = mask_dp[k, row : row + 1, :]
                for i in range(2):
                    at = (e * 2 + i) * width
                    value = pre_dp[k, part, i * width : (i + 1) * width].astype(full)
                    wide[side, spot, at : at + width] = (value * keep).astype(half)

    def gate_term(side, q):
        return lax.dot_general(
            tok_dp[side, pair(q)], wide[side, pair(q)], (((0,), (0,)), ((), ())),
            preferred_element_type=full,
        )

    def near_gates(q):
        token_copy(0, q).wait_recv()
        pre_copy(0, q).wait_recv()
        widen(0, q)
        term = gate_term(0, q)
        acc_out[...] = term if q == 0 else acc_out[...] + term

    def take_far(q):
        pre_copy(1, q).wait_recv()
        pre_copy(2, q).start()

    def far_gates(q):
        for k in (1, 2):
            token_copy(k, q).wait_recv()
        widen(1, q)
        pre_copy(2, q).wait_recv()
        widen(2, q)
        return acc_out[...] + gate_term(1, q)

    def sent_early():
        for r in range(2):
            line(0, h, r, 0, True).wait_send()
        for k in range(3):
            mask_copy(k).wait_send()
        for j in range(chunks):
            for i in range(3):
                spread(j, i).wait_send()
        if exchange:
            for group in swaps:
                for copy in group:
                    copy.wait_send()

    def pass_end(e):
        @pl.when(far != h)
        def _():
            end_far_out(e).wait_recv()

        end_cross(e).start()

    def send_own_far():
        core_copy(0, 0).wait_recv()
        sum_own[...] = core_sum(0, 0).astype(half)
        own_far.start()

    for k in range(3):
        mask_copy(k).wait_recv()
    own_tokens = [
        pltpu.make_async_copy(tok_all.at[d, cuts[q]], tok_dp.at[place(3, q)], local_sem.at[q])
        for q in steps
    ]

    @pl.when(border)
    def _():
        for r in range(2):
            add_tokens((h, inner, second), r, True)
            add_grads((h,), halves[r], True)
        for r in range(2):
            landed(0, third, r)
            share_tokens(third, r)
            add_tokens((third,), r, False)
            activate(r)
            hidden_out(r).start()
        down_term(1, h, hid)
        for copy in own_tokens:
            copy.start()

        @pl.when(far == h)
        def _():
            core_copy(1, 0).wait_recv()
            end_far[...] = core_sum(1, 0).astype(half)
            for e in range(experts):
                end_cross(e).start()

        @pl.when(d == h)
        def _():
            core_copy(1, 1).wait_recv()
            end_near[...] = core_sum(1, 1).astype(half)

        for q in steps:
            grads_out(q).wait_recv()
            make_pre(q, gh_in)
            send_pre(q)
            if q == 0:
                sent_early()
                for i in steps:
                    line(1, h, i, 0, True, True).wait_send()
                for r in range(2):
                    hidden_out(r).wait_send()
                for i in range(3):
                    lend(i, h).wait_send()

            if q == steps[-1]:
                @pl.when((far != third) & (far != h))
                def _():
                    for e in range(experts):
                        pass_end(e)

            if q == 0:
                for copy in own_tokens:
                    copy.wait()
            else:
                near_gates(q - 1)


    @pl.when(middle)
    def _():
        for r in range(2):
            add_tokens((h, outer, inner, second), r, True)
            activate(r)
            add_grads((h, outer), halves[r], True)
        for copy in own_tokens:
            copy.start()
        for slab in (h, outer):
            down_term(0, slab)
        lend(0, outer).wait_recv()
        lend_near(0, core).start()
        landed(1, inner, 0)
        add_grads((inner,), halves[0], False)
        lend(1, outer).wait_recv()
        lend_near(1, core).start()
        landed(1, inner, 1)
        add_grads((inner,), halves[1], False)
        lend(2, outer).wait_recv()
        lend_near(2, core).start()
        down_term(0, inner)
        for i in range(3):
            lend_near(i, 1 - core).wait_recv()
        for r in range(2):
            add_grads((h, inner), halves[r], True, acc_end, dn_end)
        for copy in own_tokens:
            copy.wait()
        sent_early()
        for r in range(2):
            line(0, h, r, 1, True).wait_send()
            line(1, h, r, 0, True).wait_send()
            line(0, outer, r).wait_send()
            line(0, inner, r, 1).wait_send()
            line(0, second, r, 1).wait_send()
        for r in range(2):
            hidden_out(r).wait_recv()
            for b in half_blocks[r]:
                part = slice(b * BLOCK, (b + 1) * BLOCK)
                value = hid_in[part].astype(full)
                for e in range(experts):
                    hid_end[part, e * width : (e + 1) * width] = (value * masks[b][e]).astype(half)

        def last_grads(q):
            landed(1, second, q, True)
            add_grads((second,), cuts[q], False, acc_end, dn_end)
            for b in cut_blocks[q]:
                part = slice(b * BLOCK, (b + 1) * BLOCK)
                gh_out[part] = sum(
                    acc_end[part, e * width : (e + 1) * width] * picks[b][e] for e in range(experts)
                ).astype(half)
            grads_out(q).start()
            if q == steps[-1]:
                down_term(1, second)
            add_grads((second,), cuts[q], False)
            make_pre(q)
            send_pre(q)

        for slab in (h, inner):
            down_term(1, slab)
        for q in steps:
            last_grads(q)
            if q == 0:
                @pl.when((far != second) & (far != outer))
                def _():
                    sum_end_far()
                    for e in range(experts):
                        end_far_out(e).start()

            elif q < steps[-1]:
                near_gates(q - 1)

        @pl.when(far != second)
        def _():
            send_own_far()

        down_term(0, second)

        @pl.when(far == second)
        def _():
            sum_end_far()
            for e in range(experts):
                end_far_out(e).start()
            send_own_far()

        @pl.when(d != outer)
        def _():
            core_copy(1, 1).wait_recv()
            sum_near[...] = core_sum(1, 1).astype(half)
            end_near_out.start()

        near_gates(steps[-1] - 1)

    take_far(0)
    near_gates(steps[-1])
    acc_out[...] = far_gates(0)

    take_far(1)

    @pl.when(border & (far == third))
    def _():
        for e in range(experts):
            pass_end(e)

    acc_out[...] = far_gates(1)
    take_far(2)

    total = far_gates(2)
    for e in range(experts):
        at = e * 2 * width
        out_gate[e] = total[:, at : at + width].astype(half)
        out_up[e] = total[:, at + width : at + 2 * width].astype(half)

    @pl.when(middle)
    def _():
        core_copy(0, 1).wait_recv()
        own_far.wait_recv()
        total = core_sum(0, 1) + far_own[...].astype(full)
        for e in range(experts):
            out_down[e] = total[e * width : (e + 1) * width].astype(half)

    @pl.when(border)
    def _():
        @pl.when(d != h)
        def _():
            end_near_out.wait_recv()

        for e in range(experts):
            end_cross(e).wait_recv()
        total = end_near[...].astype(full) + end_got[...].astype(full)
        for e in range(experts):
            out_down[e] = total[e * width : (e + 1) * width].astype(half)

    for k in range(3):
        for q in steps:
            token_copy(k, q).wait_send()
            pre_copy(k, q).wait_send()

    @pl.when(middle)
    def _():
        for q in steps:
            line(1, outer, q, fine=True).wait_send()
            grads_out(q).wait_send()
        for i in range(3):
            lend_near(i, core).wait_send()
        for i in range(2):
            core_copy(0, i).wait_send()

            @pl.when((cross, near)[i] != outer)
            def _():
                core_copy(1, i).wait_send()

        own_far.wait_send()

        @pl.when(far != outer)
        def _():
            for e in range(experts):
                end_far_out(e).wait_send()

        @pl.when(d != outer)
        def _():
            end_near_out.wait_send()

    @pl.when(border)
    def _():
        for i in range(2):
            @pl.when((cross, near)[i] == h)
            def _():
                core_copy(1, i).wait_send()

        for e in range(experts):
            end_cross(e).wait_send()


def settle_kernel(*refs):
    count = (len(refs) - 1) // 3
    sems = refs[-1]
    taken = [
        pltpu.make_async_copy(refs[i], refs[2 * count + i], sems.at[0, i]) for i in range(count)
    ]
    given = [
        pltpu.make_async_copy(refs[2 * count + i], refs[count + i], sems.at[1, i])
        for i in range(count)
    ]
    for copy in taken:
        copy.start()
    for i in range(count):
        taken[i].wait()
        given[i].start()
    for copy in given:
        copy.wait()


def settle(arrays):
    count = len(arrays)
    hbm = pl.BlockSpec(memory_space=pl.ANY)
    return pl.pallas_call(
        settle_kernel,
        out_shape=tuple(jax.ShapeDtypeStruct(a.shape, a.dtype) for a in arrays),
        in_specs=[hbm] * count,
        out_specs=(hbm,) * count,
        scratch_shapes=[pltpu.VMEM(a.shape, a.dtype) for a in arrays]
        + [pltpu.SemaphoreType.DMA((2, count))],
    )(*arrays)


def on_device_fused(tokens, grad_out, gate_weight, up_weight, down_weight, matching, block_counts):
    groups = lax.axis_size("expert")
    zs = lax.axis_size("hidden")
    ds = lax.axis_size("dp")
    exchange = groups == 2
    if not exchange:
        gate_weight, up_weight, down_weight = relocate(
            (gate_weight, up_weight, down_weight), matching
        )
        matching = jnp.zeros_like(matching)
    rows, feats = tokens.shape[2:]
    experts, part, width = gate_weight.shape
    vmem = pl.BlockSpec(memory_space=pltpu.VMEM)
    smem = pl.BlockSpec(memory_space=pltpu.SMEM)
    half, full = jnp.bfloat16, jnp.float32
    wide = experts * 2 * width
    tall = experts * width
    chunks = 3 * experts
    dma = pltpu.SemaphoreType.DMA
    down = pltpu.VMEM((tall, part), half)
    narrow = pltpu.VMEM((rows, width), half)
    mask = (experts * (rows // BLOCK), width)
    grads = pl.pallas_call(
        functools.partial(fused_kernel, exchange, experts),
        out_shape=tuple(
            jax.ShapeDtypeStruct(w.shape, half) for w in (gate_weight, up_weight, down_weight)
        ),
        in_specs=[smem, smem] + [pl.BlockSpec(memory_space=pltpu.HBM)] * 5,
        out_specs=(vmem,) * 3,
        scratch_shapes=[
            pltpu.VMEM((zs, rows, feats), half),
            pltpu.VMEM((zs, rows, feats), half),
            pltpu.VMEM((2, 2 * rows, feats), half),
            pltpu.VMEM((ds, experts, part, 2 * width), half),
            pltpu.VMEM((ds, tall, part), half),
            pltpu.VMEM((ds, tall, part), half),
            pltpu.VMEM(gate_weight.shape, half),
            pltpu.VMEM(up_weight.shape, half),
            pltpu.VMEM(down_weight.shape, half),
            pltpu.VMEM(gate_weight.shape, half),
            pltpu.VMEM(up_weight.shape, half),
            pltpu.VMEM(down_weight.shape, half),
            pltpu.VMEM((experts, rows, 2 * width), full),
            pltpu.VMEM((rows, tall), full),
            pltpu.VMEM((rows, tall), full),
            pltpu.VMEM((feats, wide), full),
            pltpu.VMEM((rows, width), full),
            pltpu.VMEM((rows, width), full),
            pltpu.VMEM((rows, tall), half),
            pltpu.VMEM((rows, tall), half),
            narrow, narrow, narrow, narrow,
            pltpu.VMEM(mask, full),
            pltpu.VMEM((3,) + mask, full),
            pltpu.VMEM((rows, 2 * width), half),
            pltpu.VMEM((3, rows, 2 * width), half),
            pltpu.VMEM((2, 2 * rows, wide), half),
            pltpu.VMEM((ds, tall, part), half),
            pltpu.VMEM((ds, tall, part), half),
            pltpu.VMEM((2, tall, part), half),
            pltpu.VMEM((2, tall, part), half),
            down, down, down, down, down, down, down,
            dma((2, 2, zs, 3)),
            dma((2, zs, 3)),
            dma((3 * experts * 2,)),
            dma((3 * experts * 2,)),
            dma((chunks, 3)),
            dma((chunks, 3)),
            dma((3, 3)),
            dma((3, 3)),
            dma((3, 3)),
            dma((3, 3)),
            dma((3,)),
            dma((3,)),
            dma((2, 3)),
            dma((2, 3)),
            dma((2, 3)),
            dma((2, 3)),
            dma((3, 2)),
            dma((3, 2)),
            dma((3, experts)),
            dma((3, experts)),
            dma((5,)),
        ],
        compiler_params=pltpu.CompilerParams(
            collective_id=0, has_side_effects=True, vmem_limit_bytes=63 * 1024 * 1024
        ),
    )(
        block_counts.reshape(-1), matching, tokens.reshape(rows, feats),
        grad_out.reshape(rows, feats), gate_weight, up_weight, down_weight,
    )
    return settle(grads)


def fused_fits(mesh):
    return mesh.shape["dp"] == 4 and mesh.shape["hidden"] == 4


def solution(mesh):
    on_device = on_device_fused if fused_fits(mesh) else on_device_plain
    in_specs = (
        P("expert", "dp", None, "hidden"),
        P("expert", "dp", None, "hidden"),
        P("expert", "dp", "hidden"),
        P("expert", "dp", "hidden"),
        P("expert", "hidden", "dp"),
        P(),
        P("expert", "dp", None),
    )
    out_specs = (
        P("expert", "dp", "hidden"),
        P("expert", "dp", "hidden"),
        P("expert", "hidden", "dp"),
    )
    return jax.shard_map(
        on_device, mesh=mesh, in_specs=in_specs, out_specs=out_specs, check_vma=False
    )
```

```python
import functools

import jax
import jax.numpy as jnp
from jax import lax
from jax.experimental import pallas as pl
from jax.experimental.pallas import tpu as pltpu
from jax.sharding import PartitionSpec as P

BLOCK = 128


def contract_rows(left, right):
    return lax.dot_general(
        left, right, (((0,), (0,)), ((), ())), preferred_element_type=jnp.float32
    )


def block_owners(counts, blocks):
    bounds = jnp.cumsum(counts)
    index = jnp.arange(blocks, dtype=jnp.int32)
    owner = jnp.sum((index[:, None] >= bounds[None, :]).astype(jnp.int32), axis=1)
    owner = jnp.minimum(owner, counts.shape[0] - 1)
    alive = (index < bounds[-1]).astype(jnp.float32)
    return (owner, alive)


def add_into(total, term, expert):
    current = lax.dynamic_index_in_dim(total, expert, 0, keepdims=True)
    return lax.dynamic_update_index_in_dim(total, current + term[None], expert, 0)


def expert_terms(row_blocks, grad_blocks, weight_gate, weight_up, weight_down, owner, alive):
    zeros_gate = jnp.zeros(weight_gate.shape, jnp.float32)
    zeros_down = jnp.zeros(weight_down.shape, jnp.float32)

    def step(carry, inputs):
        total_gate, total_up, total_down = carry
        row_block, grad_block, expert, live = inputs
        gate_matrix = lax.dynamic_index_in_dim(weight_gate, expert, 0, keepdims=False)
        up_matrix = lax.dynamic_index_in_dim(weight_up, expert, 0, keepdims=False)
        down_matrix = lax.dynamic_index_in_dim(weight_down, expert, 0, keepdims=False)
        gate_value = jnp.dot(row_block, gate_matrix, preferred_element_type=jnp.float32)
        up_value = jnp.dot(row_block, up_matrix, preferred_element_type=jnp.float32)
        sigmoid_gate = jax.nn.sigmoid(gate_value)
        activated = gate_value * sigmoid_gate
        hidden = (activated * up_value * live).astype(jnp.bfloat16)
        grad_hidden = lax.dot_general(
            grad_block, down_matrix, (((1,), (1,)), ((), ())), preferred_element_type=jnp.float32
        )
        grad_gate = (
            grad_hidden * up_value * sigmoid_gate * (1.0 + gate_value * (1.0 - sigmoid_gate)) * live
        ).astype(jnp.bfloat16)
        grad_up = (grad_hidden * activated * live).astype(jnp.bfloat16)
        total_gate = add_into(total_gate, contract_rows(row_block, grad_gate), expert)
        total_up = add_into(total_up, contract_rows(row_block, grad_up), expert)
        total_down = add_into(total_down, contract_rows(hidden, grad_block), expert)
        return ((total_gate, total_up, total_down), None)

    totals, unused = lax.scan(
        step, (zeros_gate, zeros_gate, zeros_down), (row_blocks, grad_blocks, owner, alive)
    )
    return totals


def relocate(arrays, matching):
    groups = lax.axis_size("expert")
    joined = jnp.concatenate([array_piece.reshape(groups, -1) for array_piece in arrays], axis=1)
    spread = lax.all_to_all(joined, "expert", split_axis=0, concat_axis=0, tiled=True)
    ordered = jnp.take(spread, matching, axis=0)
    settled = lax.all_to_all(ordered, "expert", split_axis=0, concat_axis=0, tiled=True)
    pieces = []
    offset = 0
    for array_piece in arrays:
        length = array_piece.size // groups
        pieces.append(settled[:, offset : offset + length].reshape(array_piece.shape))
        offset = offset + length
    return pieces


def on_device_plain(tokens, grad_out, gate_weight, up_weight, down_weight, matching, block_counts):
    moved = relocate((gate_weight, up_weight, down_weight), matching)
    weight_gate, weight_up, weight_down = (
        lax.all_gather(moved[0], "dp", axis=1, tiled=True),
        lax.all_gather(moved[1], "dp", axis=1, tiled=True),
        lax.all_gather(moved[2], "dp", axis=2, tiled=True),
    )
    rows_full, grads_full = (
        lax.all_gather(tokens[0, 0], "hidden", axis=1, tiled=True),
        lax.all_gather(grad_out[0, 0], "hidden", axis=1, tiled=True),
    )
    blocks = rows_full.shape[0] // BLOCK
    width = rows_full.shape[1]
    owner, alive = block_owners(block_counts[0, 0], blocks)
    totals = expert_terms(
        rows_full.reshape(blocks, BLOCK, width),
        grads_full.reshape(blocks, BLOCK, width),
        weight_gate,
        weight_up,
        weight_down,
        owner,
        alive,
    )
    summed = (
        lax.psum_scatter(
            totals[0].astype(jnp.bfloat16), "dp", scatter_dimension=1, tiled=True
        ).astype(jnp.float32),
        lax.psum_scatter(
            totals[1].astype(jnp.bfloat16), "dp", scatter_dimension=1, tiled=True
        ).astype(jnp.float32),
        lax.psum_scatter(
            totals[2].astype(jnp.bfloat16), "dp", scatter_dimension=2, tiled=True
        ).astype(jnp.float32),
    )
    return (
        summed[0].astype(jnp.bfloat16),
        summed[1].astype(jnp.bfloat16),
        summed[2].astype(jnp.bfloat16),
    )


MESH = pl.DeviceIdType.MESH


def flip(index, bit):
    return index + bit - 2 * bit * ((index // bit) % 2)


def fused_kernel(
    exchange, experts, counts_ref, match_ref, tok_ref, grad_ref, gate_ref, up_ref, down_ref,
    out_gate, out_up, out_down,
    tok_all, grad_all, tok_dp, gu_all, dn_all, dn_end,
    own_gate, own_up, own_down, old_gate, old_up, old_down,
    acc_gu, acc_gh, acc_end, acc_out, gate_sel, up_sel, hid, hid_end, hid_out, hid_in, gh_out, gh_in,
    mask_own, mask_dp, pre, pre_dp, wide,
    part_own, part_end, core_own, core_end, sum_own, far_own, sum_far, sum_near, end_far, end_near, end_got,
    z_send, z_recv, y_send, y_recv, w_send, w_recv, t_send, t_recv, p_send, p_recv, m_send, m_recv,
    l_send, l_recv, h_send, h_recv, r_send, r_recv, e_send, e_recv, local_sem,
):
    zs = lax.axis_size("hidden")
    h = lax.axis_index("hidden")
    d = lax.axis_index("dp")
    p = lax.axis_index("expert")
    rows, feats = tok_ref.shape
    width = gate_ref.shape[2]
    blocks = rows // BLOCK
    tall = experts * width
    halves = [slice(0, rows // 2), slice(rows // 2, rows)]
    half_blocks = [range(0, blocks // 2), range(blocks // 2, blocks)]
    edges = (0, rows // 2, rows // 4 * 3, rows)
    steps = range(len(edges) - 1)
    cuts = [slice(edges[q], edges[q + 1]) for q in steps]
    cut_blocks = [range(edges[q] // BLOCK, edges[q + 1] // BLOCK) for q in steps]
    near, far = flip(d, 1), flip(d, 2)
    cross = flip(near, 2)
    partners = (near, far, cross)
    middle = (h > 0) & (h < zs - 1)
    border = (h == 0) | (h == zs - 1)
    way = 1 - 2 * (h // (zs // 2))
    inner, outer = h + way, h - way
    second, third = h + 2 * way, h + 3 * way
    full, half = jnp.float32, jnp.bfloat16

    def remote(source, target, send, recv, where):
        return pltpu.make_async_remote_copy(
            src_ref=source, dst_ref=target, send_sem=send, recv_sem=recv,
            device_id=where, device_id_type=MESH,
        )

    local = [
        pltpu.make_async_copy(source, target, local_sem.at[i])
        for i, (source, target) in enumerate((
            (gate_ref, own_gate), (up_ref, own_up), (down_ref, own_down),
            (tok_ref, tok_all.at[h]), (grad_ref, grad_all.at[h]),
        ))
    ]
    for copy in local:
        copy.start()

    barrier = pltpu.get_barrier_semaphore()
    for partner in partners:
        pl.semaphore_signal(barrier, inc=1, device_id={"dp": partner}, device_id_type=MESH)
    if exchange:
        pl.semaphore_signal(barrier, inc=1, device_id={"expert": 1 - p}, device_id_type=MESH)
    pl.semaphore_signal(barrier, inc=1, device_id={"hidden": inner}, device_id_type=MESH)

    @pl.when(middle)
    def _():
        pl.semaphore_signal(barrier, inc=1, device_id={"hidden": outer}, device_id_type=MESH)

    bounds = [counts_ref[0]]
    for e in range(1, experts):
        bounds.append(bounds[-1] + counts_ref[e])
    picks, masks, alive = [], [], []
    for b in range(blocks):
        owner = jnp.int32(0)
        for e in range(experts):
            owner = owner + jnp.where(b >= bounds[e], 1, 0)
        owner = jnp.minimum(owner, experts - 1)
        alive.append(jnp.where(b < bounds[-1], 1.0, 0.0))
        picks.append([jnp.where(owner == e, 1.0, 0.0) for e in range(experts)])
        masks.append([picks[b][e] * alive[b] for e in range(experts)])
        for e in range(experts):
            row = b * experts + e
            mask_own[row : row + 1, :] = jnp.full((1, mask_own.shape[1]), masks[b][e], full)

    peers = (h + zs - 1) // zs + (2 * zs - 2 - h) // zs
    pl.semaphore_wait(barrier, peers + (4 if exchange else 3))

    mine = (tok_ref, grad_ref)
    whole = (tok_all, grad_all)

    def line(kind, slab, r, outward=0, own=False, fine=False):
        part = (cuts if fine else halves)[r]
        source = mine[kind].at[part] if own else whole[kind].at[slab, part]
        return remote(
            source, whole[kind].at[slab, part],
            z_send.at[outward, kind, slab, r], z_recv.at[kind, slab, r],
            {"hidden": outer if outward else inner},
        )

    def landed(kind, slab, r, fine=False):
        line(kind, slab, r, fine=fine).wait_recv()

    def place(k, q):
        size = edges[q + 1] - edges[q]
        start = 2 * edges[q] + (0 if k in (1, 3) else size)
        return (0 if k in (0, 3) else 1), slice(start, start + size)

    def pair(q):
        return slice(2 * edges[q], 2 * edges[q + 1])

    def token_copy(k, q, own=False):
        source = tok_ref.at[cuts[q]] if own else tok_all.at[partners[k], cuts[q]]
        return remote(
            source, tok_dp.at[place(k, q)],
            t_send.at[k, q], t_recv.at[k, q], {"dp": partners[k]},
        )

    def mask_copy(k):
        return remote(
            mask_own, mask_dp.at[k], m_send.at[k], m_recv.at[k], {"dp": partners[k]}
        )

    for r in range(2):
        line(0, h, r, 0, True).start()

        @pl.when(middle)
        def _():
            line(0, h, r, 1, True).start()

    @pl.when(border)
    def _():
        for q in steps:
            line(1, h, q, 0, True, True).start()

    feat_halves = [slice(0, feats // 2), slice(feats // 2, feats)]

    def swap(i, e, f=None):
        source = (gate_ref, up_ref, down_ref)[i]
        target = (old_gate, old_up, old_down)[i]
        at = (e,) if f is None else (e, feat_halves[f])
        n = (i * experts + e) * 2 + (f or 0)
        return remote(source.at[at], target.at[at], y_send.at[n], y_recv.at[n], {"expert": 1 - p})

    swaps = []
    if exchange:
        swaps = [[swap(0, e, f), swap(1, e, f)] for e in range(experts) for f in range(2)]
        swaps += [[swap(2, e)] for e in range(experts)]
        for group in swaps:
            for copy in group:
                copy.start()
    for k in range(3):
        mask_copy(k).start()

    def chosen(own, other, at):
        if not exchange:
            return own[at]
        return jnp.where(match_ref[p] == p, own[at], other[at])

    chunks = 3 * experts

    def piece(j, slab):
        if j < 2 * experts:
            return gu_all.at[slab, j // 2, feat_halves[j % 2]]
        e = j - 2 * experts
        return dn_all.at[slab, e * width : (e + 1) * width]

    def spread(j, i):
        ref = piece(j, (d, d, far)[i])
        to = (far, near, near)[i]
        return remote(ref, ref, w_send.at[j, i], w_recv.at[j, i], {"dp": to})

    def arrived(j, i):
        ref = piece(j, (far, near, cross)[i])
        remote(ref, ref, w_send.at[j, i], w_recv.at[j, i], {"dp": near}).wait_recv()

    def take_weights(j):
        if exchange:
            for copy in swaps[j]:
                copy.wait_recv()
        if j < 2 * experts:
            at = (j // 2, feat_halves[j % 2])
            gu_all[d, j // 2, feat_halves[j % 2], :width] = chosen(own_gate, old_gate, at)
            gu_all[d, j // 2, feat_halves[j % 2], width:] = chosen(own_up, old_up, at)
        else:
            e = j - 2 * experts
            dn_all[d, e * width : (e + 1) * width, :] = chosen(own_down, old_down, e)
        spread(j, 0).start()
        spread(j, 1).start()

    def pass_weights(j):
        arrived(j, 0)
        spread(j, 2).start()

    def share_tokens(slab, r):
        for k in range(3):
            @pl.when(slab == partners[k])
            def _():
                for q in ((0,) if r == 0 else steps[1:]):
                    token_copy(k, q).start()

    def relay_tokens(r):
        @pl.when(middle)
        def _():
            landed(0, outer, r)
            line(0, outer, r).start()
            landed(0, inner, r)
            line(0, inner, r, 1).start()

    def relay_late(r):
        @pl.when(middle)
        def _():
            landed(0, second, r)
            line(0, second, r, 1).start()
            for q in ((0,) if r == 0 else steps[1:]):
                landed(1, outer, q, True)
                line(1, outer, q, fine=True).start()

    for copy in local[:2]:
        copy.wait()
    take_weights(0)
    relay_tokens(0)
    take_weights(1)
    pass_weights(0)
    take_weights(2)
    relay_tokens(1)

    @pl.when(middle)
    def _():
        for r in range(2):
            line(1, h, r, 0, True).start()

    pass_weights(1)
    for j in range(3, 2 * experts):
        take_weights(j)
    for copy in local[2:]:
        copy.wait()
    pass_weights(2)
    take_weights(2 * experts)
    relay_late(0)
    for j in range(3, 2 * experts):
        pass_weights(j)
    for j in range(2 * experts + 1, chunks):
        take_weights(j)
    for r in range(2):
        share_tokens(h, r)

    @pl.when(border)
    def _():
        for r in range(2):
            landed(0, inner, r)
            share_tokens(inner, r)
        landed(0, second, 0)
        share_tokens(second, 0)

    @pl.when(middle)
    def _():
        for slab in (outer, inner):
            for r in range(2):
                share_tokens(slab, r)
        share_tokens(second, 0)

    pass_weights(2 * experts)
    relay_late(1)

    @pl.when(border)
    def _():
        landed(0, second, 1)

    share_tokens(second, 1)
    for j in range(2 * experts + 1, chunks):
        pass_weights(j)
    for j in range(chunks):
        arrived(j, 1)
        arrived(j, 2)

    core = d % 2
    lot = tall // 2

    def strip(index):
        return pl.ds(pl.multiple_of(index * lot, lot), lot)

    def lend(i, owner):
        slab = owner + (i + 1) * way
        return remote(
            dn_all.at[slab, strip(core)], dn_end.at[slab, strip(core)],
            l_send.at[0, i], l_recv.at[0, i], {"hidden": inner},
        )

    def lend_near(i, which):
        ref = dn_end.at[outer + (i + 1) * way, strip(which)]
        return remote(ref, ref, l_send.at[1, i], l_recv.at[1, i], {"dp": near})

    @pl.when(border)
    def _():
        for i in range(3):
            lend(i, h).start()

    def add_tokens(slabs, r, first):
        for e in range(experts):
            total = None if first else acc_gu[e, halves[r]]
            for slab in slabs:
                term = jnp.dot(tok_all[slab, halves[r]], gu_all[slab, e], preferred_element_type=full)
                total = term if total is None else total + term
            acc_gu[e, halves[r]] = total

    def add_grads(slabs, part, first, total_ref=acc_gh, weight=dn_all):
        total = None if first else total_ref[part]
        for slab in slabs:
            term = lax.dot_general(
                grad_all[slab, part], weight[slab], (((1,), (1,)), ((), ())),
                preferred_element_type=full,
            )
            total = term if total is None else total + term
        total_ref[part] = total

    def activate(r):
        for b in half_blocks[r]:
            part = slice(b * BLOCK, (b + 1) * BLOCK)
            both = sum(acc_gu[e, part] * picks[b][e] for e in range(experts))
            gate_value, up_value = both[:, :width], both[:, width:]
            gate_sel[part] = gate_value
            up_sel[part] = up_value
            hidden = gate_value * jax.nn.sigmoid(gate_value) * up_value
            hid_out[part] = (hidden * alive[b]).astype(half)
            for e in range(experts):
                hid[part, e * width : (e + 1) * width] = (hidden * masks[b][e]).astype(half)

    def hidden_out(r):
        return remote(
            hid_out.at[halves[r]], hid_in.at[halves[r]], h_send.at[0, r], h_recv.at[0, r],
            {"hidden": inner},
        )

    def grads_out(q):
        return remote(
            gh_out.at[cuts[q]], gh_in.at[cuts[q]], h_send.at[1, q], h_recv.at[1, q],
            {"hidden": outer},
        )

    def block_place(k, q, b):
        side, spot = place(k, q)
        start = spot.start + b * BLOCK - edges[q]
        return side, slice(start, start + BLOCK)

    def make_pre(q, extra=None):
        for b in cut_blocks[q]:
            part = slice(b * BLOCK, (b + 1) * BLOCK)
            side, spot = block_place(3, q, b)
            gate_value, up_value = gate_sel[part], up_sel[part]
            grad_hidden = sum(
                acc_gh[part, e * width : (e + 1) * width] * picks[b][e] for e in range(experts)
            )
            if extra is not None:
                grad_hidden = grad_hidden + extra[part].astype(full)
            s = jax.nn.sigmoid(gate_value)
            grad_gate = grad_hidden * up_value * s * (1.0 + gate_value * (1.0 - s))
            grad_up = grad_hidden * gate_value * s
            pre[part, :width] = (grad_gate * alive[b]).astype(half)
            pre[part, width:] = (grad_up * alive[b]).astype(half)
            for e in range(experts):
                at = e * 2 * width
                wide[side, spot, at : at + width] = (grad_gate * masks[b][e]).astype(half)
                wide[side, spot, at + width : at + 2 * width] = (grad_up * masks[b][e]).astype(half)

    def pre_copy(k, q):
        source = pre_dp.at[1, cuts[q]] if k == 2 else pre.at[cuts[q]]
        to = far if k == 1 else near
        return remote(
            source, pre_dp.at[k, cuts[q]], p_send.at[k, q], p_recv.at[k, q], {"dp": to}
        )

    def send_pre(q):
        pre_copy(1, q).start()
        pre_copy(0, q).start()

    parts, cores = (part_own, part_end), (core_own, core_end)
    lefts = (hid, hid_end)

    def core_copy(kind, i):
        slab = (cross, near)[i]
        return remote(
            parts[kind].at[slab], cores[kind].at[i], r_send.at[kind, i], r_recv.at[kind, i],
            {"dp": near},
        )

    def down_term(kind, slab, left=None):
        parts[kind][slab] = lax.dot_general(
            (lefts[kind] if left is None else left)[...], grad_all[slab], (((0,), (0,)), ((), ())), preferred_element_type=full
        ).astype(half)
        for i in range(2):
            @pl.when(slab == (cross, near)[i])
            def _():
                core_copy(kind, i).start()

    def core_sum(kind, i):
        slab = (far, d)[i]
        return parts[kind][slab].astype(full) + cores[kind][i].astype(full)

    own_far = remote(sum_own, far_own, r_send.at[2, 0], r_recv.at[2, 0], {"dp": far})
    end_near_out = remote(sum_near, end_near, e_send.at[0, 0], e_recv.at[0, 0], {"hidden": outer})

    def end_far_out(e):
        part = slice(e * width, (e + 1) * width)
        return remote(
            sum_far.at[part], end_far.at[part], e_send.at[1, e], e_recv.at[1, e], {"hidden": outer}
        )

    def end_cross(e):
        part = slice(e * width, (e + 1) * width)
        return remote(
            end_far.at[part], end_got.at[part], e_send.at[2, e], e_recv.at[2, e], {"dp": far}
        )

    def sum_end_far():
        core_copy(1, 0).wait_recv()
        sum_far[...] = core_sum(1, 0).astype(half)

    def widen(k, q):
        for b in cut_blocks[q]:
            part = slice(b * BLOCK, (b + 1) * BLOCK)
            side, spot = block_place(k, q, b)
            for e in range(experts):
                row = b * experts + e
                keep = mask_dp[k, row : row + 1, :]
                for i in range(2):
                    at = (e * 2 + i) * width
                    value = pre_dp[k, part, i * width : (i + 1) * width].astype(full)
                    wide[side, spot, at : at + width] = (value * keep).astype(half)

    def gate_term(side, q):
        return lax.dot_general(
            tok_dp[side, pair(q)], wide[side, pair(q)], (((0,), (0,)), ((), ())),
            preferred_element_type=full,
        )

    def near_gates(q):
        token_copy(0, q).wait_recv()
        pre_copy(0, q).wait_recv()
        widen(0, q)
        term = gate_term(0, q)
        acc_out[...] = term if q == 0 else acc_out[...] + term

    def take_far(q):
        pre_copy(1, q).wait_recv()
        pre_copy(2, q).start()

    def far_gates(q):
        for k in (1, 2):
            token_copy(k, q).wait_recv()
        widen(1, q)
        pre_copy(2, q).wait_recv()
        widen(2, q)
        return acc_out[...] + gate_term(1, q)

    def sent_early():
        for r in range(2):
            line(0, h, r, 0, True).wait_send()
        for k in range(3):
            mask_copy(k).wait_send()
        for j in range(chunks):
            for i in range(3):
                spread(j, i).wait_send()
        if exchange:
            for group in swaps:
                for copy in group:
                    copy.wait_send()

    def pass_end(e):
        @pl.when(far != h)
        def _():
            end_far_out(e).wait_recv()

        end_cross(e).start()

    def send_own_far():
        core_copy(0, 0).wait_recv()
        sum_own[...] = core_sum(0, 0).astype(half)
        own_far.start()

    for k in range(3):
        mask_copy(k).wait_recv()
    own_tokens = [
        pltpu.make_async_copy(tok_all.at[d, cuts[q]], tok_dp.at[place(3, q)], local_sem.at[q])
        for q in steps
    ]

    @pl.when(border)
    def _():
        for r in range(2):
            add_tokens((h, inner, second), r, True)
            add_grads((h,), halves[r], True)
        for r in range(2):
            landed(0, third, r)
            share_tokens(third, r)
            add_tokens((third,), r, False)
            activate(r)
            hidden_out(r).start()
        down_term(1, h, hid)
        for copy in own_tokens:
            copy.start()

        @pl.when(far == h)
        def _():
            core_copy(1, 0).wait_recv()
            end_far[...] = core_sum(1, 0).astype(half)
            for e in range(experts):
                end_cross(e).start()

        @pl.when(d == h)
        def _():
            core_copy(1, 1).wait_recv()
            end_near[...] = core_sum(1, 1).astype(half)

        for q in steps:
            grads_out(q).wait_recv()
            make_pre(q, gh_in)
            send_pre(q)
            if q == 0:
                sent_early()
                for i in steps:
                    line(1, h, i, 0, True, True).wait_send()
                for r in range(2):
                    hidden_out(r).wait_send()
                for i in range(3):
                    lend(i, h).wait_send()

            if q == steps[-1]:
                @pl.when((far != third) & (far != h))
                def _():
                    for e in range(experts):
                        pass_end(e)

            if q == 0:
                for copy in own_tokens:
                    copy.wait()
            else:
                near_gates(q - 1)


    @pl.when(middle)
    def _():
        for r in range(2):
            add_tokens((h, outer, inner, second), r, True)
            activate(r)
            add_grads((h, outer), halves[r], True)
        for copy in own_tokens:
            copy.start()
        for slab in (h, outer):
            down_term(0, slab)
        lend(0, outer).wait_recv()
        lend_near(0, core).start()
        landed(1, inner, 0)
        add_grads((inner,), halves[0], False)
        lend(1, outer).wait_recv()
        lend_near(1, core).start()
        landed(1, inner, 1)
        add_grads((inner,), halves[1], False)
        lend(2, outer).wait_recv()
        lend_near(2, core).start()
        down_term(0, inner)
        for i in range(3):
            lend_near(i, 1 - core).wait_recv()
        for r in range(2):
            add_grads((h, inner), halves[r], True, acc_end, dn_end)
        for copy in own_tokens:
            copy.wait()
        sent_early()
        for r in range(2):
            line(0, h, r, 1, True).wait_send()
            line(1, h, r, 0, True).wait_send()
            line(0, outer, r).wait_send()
            line(0, inner, r, 1).wait_send()
            line(0, second, r, 1).wait_send()
        for r in range(2):
            hidden_out(r).wait_recv()
            for b in half_blocks[r]:
                part = slice(b * BLOCK, (b + 1) * BLOCK)
                value = hid_in[part].astype(full)
                for e in range(experts):
                    hid_end[part, e * width : (e + 1) * width] = (value * masks[b][e]).astype(half)

        def last_grads(q):
            landed(1, second, q, True)
            add_grads((second,), cuts[q], False, acc_end, dn_end)
            for b in cut_blocks[q]:
                part = slice(b * BLOCK, (b + 1) * BLOCK)
                gh_out[part] = sum(
                    acc_end[part, e * width : (e + 1) * width] * picks[b][e] for e in range(experts)
                ).astype(half)
            grads_out(q).start()
            if q == steps[-1]:
                down_term(1, second)
            add_grads((second,), cuts[q], False)
            make_pre(q)
            send_pre(q)

        for slab in (h, inner):
            down_term(1, slab)
        for q in steps:
            last_grads(q)
            if q == 0:
                @pl.when((far != second) & (far != outer))
                def _():
                    sum_end_far()
                    for e in range(experts):
                        end_far_out(e).start()

            elif q < steps[-1]:
                near_gates(q - 1)

        @pl.when(far != second)
        def _():
            send_own_far()

        down_term(0, second)

        @pl.when(far == second)
        def _():
            sum_end_far()
            for e in range(experts):
                end_far_out(e).start()
            send_own_far()

        @pl.when(d != outer)
        def _():
            core_copy(1, 1).wait_recv()
            sum_near[...] = core_sum(1, 1).astype(half)
            end_near_out.start()

        near_gates(steps[-1] - 1)

    take_far(0)
    near_gates(steps[-1])
    take_far(1)

    @pl.when(border & (far == third))
    def _():
        for e in range(experts):
            pass_end(e)

    acc_out[...] = far_gates(0)
    take_far(2)
    acc_out[...] = far_gates(1)
    total = far_gates(2)
    for e in range(experts):
        at = e * 2 * width
        out_gate[e] = total[:, at : at + width].astype(half)
        out_up[e] = total[:, at + width : at + 2 * width].astype(half)

    @pl.when(middle)
    def _():
        core_copy(0, 1).wait_recv()
        own_far.wait_recv()
        total = core_sum(0, 1) + far_own[...].astype(full)
        for e in range(experts):
            out_down[e] = total[e * width : (e + 1) * width].astype(half)

    @pl.when(border)
    def _():
        @pl.when(d != h)
        def _():
            end_near_out.wait_recv()

        for e in range(experts):
            end_cross(e).wait_recv()
        total = end_near[...].astype(full) + end_got[...].astype(full)
        for e in range(experts):
            out_down[e] = total[e * width : (e + 1) * width].astype(half)

    for k in range(3):
        for q in steps:
            token_copy(k, q).wait_send()
            pre_copy(k, q).wait_send()

    @pl.when(middle)
    def _():
        for q in steps:
            line(1, outer, q, fine=True).wait_send()
            grads_out(q).wait_send()
        for i in range(3):
            lend_near(i, core).wait_send()
        for i in range(2):
            core_copy(0, i).wait_send()

            @pl.when((cross, near)[i] != outer)
            def _():
                core_copy(1, i).wait_send()

        own_far.wait_send()

        @pl.when(far != outer)
        def _():
            for e in range(experts):
                end_far_out(e).wait_send()

        @pl.when(d != outer)
        def _():
            end_near_out.wait_send()

    @pl.when(border)
    def _():
        for i in range(2):
            @pl.when((cross, near)[i] == h)
            def _():
                core_copy(1, i).wait_send()

        for e in range(experts):
            end_cross(e).wait_send()


def settle_kernel(*refs):
    count = (len(refs) - 1) // 2
    copies = [
        pltpu.make_async_copy(refs[i], refs[count + i], refs[-1].at[i]) for i in range(count)
    ]
    for copy in copies:
        copy.start()
    for copy in copies:
        copy.wait()


def settle(arrays):
    count = len(arrays)
    return pl.pallas_call(
        settle_kernel,
        out_shape=tuple(jax.ShapeDtypeStruct(a.shape, a.dtype) for a in arrays),
        in_specs=[pl.BlockSpec(memory_space=pltpu.VMEM)] * count,
        out_specs=(pl.BlockSpec(memory_space=pl.ANY),) * count,
        scratch_shapes=[pltpu.SemaphoreType.DMA((count,))],
    )(*[pltpu.with_memory_space_constraint(a, pltpu.VMEM) for a in arrays])


def on_device_fused(tokens, grad_out, gate_weight, up_weight, down_weight, matching, block_counts):
    groups = lax.axis_size("expert")
    zs = lax.axis_size("hidden")
    ds = lax.axis_size("dp")
    exchange = groups == 2
    if not exchange:
        gate_weight, up_weight, down_weight = relocate(
            (gate_weight, up_weight, down_weight), matching
        )
        matching = jnp.zeros_like(matching)
    rows, feats = tokens.shape[2:]
    experts, part, width = gate_weight.shape
    vmem = pl.BlockSpec(memory_space=pltpu.VMEM)
    smem = pl.BlockSpec(memory_space=pltpu.SMEM)
    half, full = jnp.bfloat16, jnp.float32
    wide = experts * 2 * width
    tall = experts * width
    chunks = 3 * experts
    dma = pltpu.SemaphoreType.DMA
    down = pltpu.VMEM((tall, part), half)
    narrow = pltpu.VMEM((rows, width), half)
    mask = (experts * (rows // BLOCK), width)
    grads = pl.pallas_call(
        functools.partial(fused_kernel, exchange, experts),
        out_shape=tuple(
            pltpu.VMEM(w.shape, half) for w in (gate_weight, up_weight, down_weight)
        ),
        in_specs=[smem, smem] + [pl.BlockSpec(memory_space=pltpu.HBM)] * 5,
        out_specs=(vmem,) * 3,
        scratch_shapes=[
            pltpu.VMEM((zs, rows, feats), half),
            pltpu.VMEM((zs, rows, feats), half),
            pltpu.VMEM((2, 2 * rows, feats), half),
            pltpu.VMEM((ds, experts, part, 2 * width), half),
            pltpu.VMEM((ds, tall, part), half),
            pltpu.VMEM((ds, tall, part), half),
            pltpu.VMEM(gate_weight.shape, half),
            pltpu.VMEM(up_weight.shape, half),
            pltpu.VMEM(down_weight.shape, half),
            pltpu.VMEM(gate_weight.shape, half),
            pltpu.VMEM(up_weight.shape, half),
            pltpu.VMEM(down_weight.shape, half),
            pltpu.VMEM((experts, rows, 2 * width), full),
            pltpu.VMEM((rows, tall), full),
            pltpu.VMEM((rows, tall), full),
            pltpu.VMEM((feats, wide), full),
            pltpu.VMEM((rows, width), full),
            pltpu.VMEM((rows, width), full),
            pltpu.VMEM((rows, tall), half),
            pltpu.VMEM((rows, tall), half),
            narrow, narrow, narrow, narrow,
            pltpu.VMEM(mask, full),
            pltpu.VMEM((3,) + mask, full),
            pltpu.VMEM((rows, 2 * width), half),
            pltpu.VMEM((3, rows, 2 * width), half),
            pltpu.VMEM((2, 2 * rows, wide), half),
            pltpu.VMEM((ds, tall, part), half),
            pltpu.VMEM((ds, tall, part), half),
            pltpu.VMEM((2, tall, part), half),
            pltpu.VMEM((2, tall, part), half),
            down, down, down, down, down, down, down,
            dma((2, 2, zs, 3)),
            dma((2, zs, 3)),
            dma((3 * experts * 2,)),
            dma((3 * experts * 2,)),
            dma((chunks, 3)),
            dma((chunks, 3)),
            dma((3, 3)),
            dma((3, 3)),
            dma((3, 3)),
            dma((3, 3)),
            dma((3,)),
            dma((3,)),
            dma((2, 3)),
            dma((2, 3)),
            dma((2, 3)),
            dma((2, 3)),
            dma((3, 2)),
            dma((3, 2)),
            dma((3, experts)),
            dma((3, experts)),
            dma((5,)),
        ],
        compiler_params=pltpu.CompilerParams(
            collective_id=0, has_side_effects=True, vmem_limit_bytes=63 * 1024 * 1024
        ),
    )(
        block_counts.reshape(-1), matching, tokens.reshape(rows, feats),
        grad_out.reshape(rows, feats), gate_weight, up_weight, down_weight,
    )
    return settle(grads)


def fused_fits(mesh):
    return mesh.shape["dp"] == 4 and mesh.shape["hidden"] == 4


def solution(mesh):
    on_device = on_device_fused if fused_fits(mesh) else on_device_plain
    in_specs = (
        P("expert", "dp", None, "hidden"),
        P("expert", "dp", None, "hidden"),
        P("expert", "dp", "hidden"),
        P("expert", "dp", "hidden"),
        P("expert", "hidden", "dp"),
        P(),
        P("expert", "dp", None),
    )
    out_specs = (
        P("expert", "dp", "hidden"),
        P("expert", "dp", "hidden"),
        P("expert", "hidden", "dp"),
    )
    return jax.shard_map(
        on_device, mesh=mesh, in_specs=in_specs, out_specs=out_specs, check_vma=False
    )
```

```python
import functools

import jax
import jax.numpy as jnp
from jax import lax
from jax.experimental import pallas as pl
from jax.experimental.pallas import tpu as pltpu
from jax.sharding import PartitionSpec as P

BLOCK = 128


def contract_rows(left, right):
    return lax.dot_general(
        left, right, (((0,), (0,)), ((), ())), preferred_element_type=jnp.float32
    )


def block_owners(counts, blocks):
    bounds = jnp.cumsum(counts)
    index = jnp.arange(blocks, dtype=jnp.int32)
    owner = jnp.sum((index[:, None] >= bounds[None, :]).astype(jnp.int32), axis=1)
    owner = jnp.minimum(owner, counts.shape[0] - 1)
    alive = (index < bounds[-1]).astype(jnp.float32)
    return (owner, alive)


def add_into(total, term, expert):
    current = lax.dynamic_index_in_dim(total, expert, 0, keepdims=True)
    return lax.dynamic_update_index_in_dim(total, current + term[None], expert, 0)


def expert_terms(row_blocks, grad_blocks, weight_gate, weight_up, weight_down, owner, alive):
    zeros_gate = jnp.zeros(weight_gate.shape, jnp.float32)
    zeros_down = jnp.zeros(weight_down.shape, jnp.float32)

    def step(carry, inputs):
        total_gate, total_up, total_down = carry
        row_block, grad_block, expert, live = inputs
        gate_matrix = lax.dynamic_index_in_dim(weight_gate, expert, 0, keepdims=False)
        up_matrix = lax.dynamic_index_in_dim(weight_up, expert, 0, keepdims=False)
        down_matrix = lax.dynamic_index_in_dim(weight_down, expert, 0, keepdims=False)
        gate_value = jnp.dot(row_block, gate_matrix, preferred_element_type=jnp.float32)
        up_value = jnp.dot(row_block, up_matrix, preferred_element_type=jnp.float32)
        sigmoid_gate = jax.nn.sigmoid(gate_value)
        activated = gate_value * sigmoid_gate
        hidden = (activated * up_value * live).astype(jnp.bfloat16)
        grad_hidden = lax.dot_general(
            grad_block, down_matrix, (((1,), (1,)), ((), ())), preferred_element_type=jnp.float32
        )
        grad_gate = (
            grad_hidden * up_value * sigmoid_gate * (1.0 + gate_value * (1.0 - sigmoid_gate)) * live
        ).astype(jnp.bfloat16)
        grad_up = (grad_hidden * activated * live).astype(jnp.bfloat16)
        total_gate = add_into(total_gate, contract_rows(row_block, grad_gate), expert)
        total_up = add_into(total_up, contract_rows(row_block, grad_up), expert)
        total_down = add_into(total_down, contract_rows(hidden, grad_block), expert)
        return ((total_gate, total_up, total_down), None)

    totals, unused = lax.scan(
        step, (zeros_gate, zeros_gate, zeros_down), (row_blocks, grad_blocks, owner, alive)
    )
    return totals


def relocate(arrays, matching):
    groups = lax.axis_size("expert")
    joined = jnp.concatenate([array_piece.reshape(groups, -1) for array_piece in arrays], axis=1)
    spread = lax.all_to_all(joined, "expert", split_axis=0, concat_axis=0, tiled=True)
    ordered = jnp.take(spread, matching, axis=0)
    settled = lax.all_to_all(ordered, "expert", split_axis=0, concat_axis=0, tiled=True)
    pieces = []
    offset = 0
    for array_piece in arrays:
        length = array_piece.size // groups
        pieces.append(settled[:, offset : offset + length].reshape(array_piece.shape))
        offset = offset + length
    return pieces


def on_device_plain(tokens, grad_out, gate_weight, up_weight, down_weight, matching, block_counts):
    moved = relocate((gate_weight, up_weight, down_weight), matching)
    weight_gate, weight_up, weight_down = (
        lax.all_gather(moved[0], "dp", axis=1, tiled=True),
        lax.all_gather(moved[1], "dp", axis=1, tiled=True),
        lax.all_gather(moved[2], "dp", axis=2, tiled=True),
    )
    rows_full, grads_full = (
        lax.all_gather(tokens[0, 0], "hidden", axis=1, tiled=True),
        lax.all_gather(grad_out[0, 0], "hidden", axis=1, tiled=True),
    )
    blocks = rows_full.shape[0] // BLOCK
    width = rows_full.shape[1]
    owner, alive = block_owners(block_counts[0, 0], blocks)
    totals = expert_terms(
        rows_full.reshape(blocks, BLOCK, width),
        grads_full.reshape(blocks, BLOCK, width),
        weight_gate,
        weight_up,
        weight_down,
        owner,
        alive,
    )
    summed = (
        lax.psum_scatter(
            totals[0].astype(jnp.bfloat16), "dp", scatter_dimension=1, tiled=True
        ).astype(jnp.float32),
        lax.psum_scatter(
            totals[1].astype(jnp.bfloat16), "dp", scatter_dimension=1, tiled=True
        ).astype(jnp.float32),
        lax.psum_scatter(
            totals[2].astype(jnp.bfloat16), "dp", scatter_dimension=2, tiled=True
        ).astype(jnp.float32),
    )
    return (
        summed[0].astype(jnp.bfloat16),
        summed[1].astype(jnp.bfloat16),
        summed[2].astype(jnp.bfloat16),
    )


MESH = pl.DeviceIdType.MESH


def flip(index, bit):
    return index + bit - 2 * bit * ((index // bit) % 2)


def fused_kernel(
    exchange, experts, counts_ref, match_ref, tok_ref, grad_ref, gate_ref, up_ref, down_ref,
    out_gate, out_up, out_down,
    tok_all, grad_all, tok_dp, gu_all, dn_all, dn_end,
    own_gate, own_up, own_down, old_gate, old_up, old_down,
    acc_gu, acc_gh, acc_end, acc_out, gate_sel, up_sel, hid, hid_end, hid_out, hid_in, gh_out, gh_in,
    mask_own, mask_dp, pre, pre_dp, wide,
    part_own, part_end, core_own, core_end, sum_own, far_own, sum_far, sum_near, end_far, end_near, end_got,
    z_send, z_recv, y_send, y_recv, w_send, w_recv, t_send, t_recv, p_send, p_recv, m_send, m_recv,
    l_send, l_recv, h_send, h_recv, r_send, r_recv, e_send, e_recv, local_sem,
):
    zs = lax.axis_size("hidden")
    h = lax.axis_index("hidden")
    d = lax.axis_index("dp")
    p = lax.axis_index("expert")
    rows, feats = tok_ref.shape
    width = gate_ref.shape[2]
    blocks = rows // BLOCK
    tall = experts * width
    halves = [slice(0, rows // 2), slice(rows // 2, rows)]
    half_blocks = [range(0, blocks // 2), range(blocks // 2, blocks)]
    edges = (0, rows // 2, rows // 4 * 3, rows)
    steps = range(len(edges) - 1)
    cuts = [slice(edges[q], edges[q + 1]) for q in steps]
    cut_blocks = [range(edges[q] // BLOCK, edges[q + 1] // BLOCK) for q in steps]
    near, far = flip(d, 1), flip(d, 2)
    cross = flip(near, 2)
    partners = (near, far, cross)
    middle = (h > 0) & (h < zs - 1)
    border = (h == 0) | (h == zs - 1)
    way = 1 - 2 * (h // (zs // 2))
    inner, outer = h + way, h - way
    second, third = h + 2 * way, h + 3 * way
    full, half = jnp.float32, jnp.bfloat16

    def remote(source, target, send, recv, where):
        return pltpu.make_async_remote_copy(
            src_ref=source, dst_ref=target, send_sem=send, recv_sem=recv,
            device_id=where, device_id_type=MESH,
        )

    local = [
        pltpu.make_async_copy(source, target, local_sem.at[i])
        for i, (source, target) in enumerate((
            (gate_ref, own_gate), (up_ref, own_up), (down_ref, own_down),
            (tok_ref, tok_all.at[h]), (grad_ref, grad_all.at[h]),
        ))
    ]
    for copy in local:
        copy.start()

    barrier = pltpu.get_barrier_semaphore()
    for partner in partners:
        pl.semaphore_signal(barrier, inc=1, device_id={"dp": partner}, device_id_type=MESH)
    if exchange:
        pl.semaphore_signal(barrier, inc=1, device_id={"expert": 1 - p}, device_id_type=MESH)
    pl.semaphore_signal(barrier, inc=1, device_id={"hidden": inner}, device_id_type=MESH)

    @pl.when(middle)
    def _():
        pl.semaphore_signal(barrier, inc=1, device_id={"hidden": outer}, device_id_type=MESH)

    bounds = [counts_ref[0]]
    for e in range(1, experts):
        bounds.append(bounds[-1] + counts_ref[e])
    picks, masks, alive = [], [], []
    for b in range(blocks):
        owner = jnp.int32(0)
        for e in range(experts):
            owner = owner + jnp.where(b >= bounds[e], 1, 0)
        owner = jnp.minimum(owner, experts - 1)
        alive.append(jnp.where(b < bounds[-1], 1.0, 0.0))
        picks.append([jnp.where(owner == e, 1.0, 0.0) for e in range(experts)])
        masks.append([picks[b][e] * alive[b] for e in range(experts)])
        for e in range(experts):
            row = b * experts + e
            mask_own[row : row + 1, :] = jnp.full((1, mask_own.shape[1]), masks[b][e], full)

    peers = (h + zs - 1) // zs + (2 * zs - 2 - h) // zs
    pl.semaphore_wait(barrier, peers + (4 if exchange else 3))

    mine = (tok_ref, grad_ref)
    whole = (tok_all, grad_all)

    def line(kind, slab, r, outward=0, own=False, fine=False):
        part = (cuts if fine else halves)[r]
        source = mine[kind].at[part] if own else whole[kind].at[slab, part]
        return remote(
            source, whole[kind].at[slab, part],
            z_send.at[outward, kind, slab, r], z_recv.at[kind, slab, r],
            {"hidden": outer if outward else inner},
        )

    def landed(kind, slab, r, fine=False):
        line(kind, slab, r, fine=fine).wait_recv()

    def place(k, q):
        size = edges[q + 1] - edges[q]
        start = 2 * edges[q] + (0 if k in (1, 3) else size)
        return (0 if k in (0, 3) else 1), slice(start, start + size)

    def pair(q):
        return slice(2 * edges[q], 2 * edges[q + 1])

    def token_copy(k, q, own=False):
        source = tok_ref.at[cuts[q]] if own else tok_all.at[partners[k], cuts[q]]
        return remote(
            source, tok_dp.at[place(k, q)],
            t_send.at[k, q], t_recv.at[k, q], {"dp": partners[k]},
        )

    def mask_copy(k):
        return remote(
            mask_own, mask_dp.at[k], m_send.at[k], m_recv.at[k], {"dp": partners[k]}
        )

    for r in range(2):
        line(0, h, r, 0, True).start()

        @pl.when(middle)
        def _():
            line(0, h, r, 1, True).start()

    @pl.when(border)
    def _():
        for q in steps:
            line(1, h, q, 0, True, True).start()

    feat_halves = [slice(0, feats // 2), slice(feats // 2, feats)]

    def swap(i, e, f=None):
        source = (gate_ref, up_ref, down_ref)[i]
        target = (old_gate, old_up, old_down)[i]
        at = (e,) if f is None else (e, feat_halves[f])
        n = (i * experts + e) * 2 + (f or 0)
        return remote(source.at[at], target.at[at], y_send.at[n], y_recv.at[n], {"expert": 1 - p})

    swaps = []
    if exchange:
        swaps = [[swap(0, e, f), swap(1, e, f)] for e in range(experts) for f in range(2)]
        swaps += [[swap(2, e)] for e in range(experts)]
        for group in swaps:
            for copy in group:
                copy.start()
    for k in range(3):
        mask_copy(k).start()

    def chosen(own, other, at):
        if not exchange:
            return own[at]
        return jnp.where(match_ref[p] == p, own[at], other[at])

    chunks = 3 * experts

    def piece(j, slab):
        if j < 2 * experts:
            return gu_all.at[slab, j // 2, feat_halves[j % 2]]
        e = j - 2 * experts
        return dn_all.at[slab, e * width : (e + 1) * width]

    def spread(j, i):
        ref = piece(j, (d, d, far)[i])
        to = (far, near, near)[i]
        return remote(ref, ref, w_send.at[j, i], w_recv.at[j, i], {"dp": to})

    def arrived(j, i):
        ref = piece(j, (far, near, cross)[i])
        remote(ref, ref, w_send.at[j, i], w_recv.at[j, i], {"dp": near}).wait_recv()

    def take_weights(j):
        if exchange:
            for copy in swaps[j]:
                copy.wait_recv()
        if j < 2 * experts:
            at = (j // 2, feat_halves[j % 2])
            gu_all[d, j // 2, feat_halves[j % 2], :width] = chosen(own_gate, old_gate, at)
            gu_all[d, j // 2, feat_halves[j % 2], width:] = chosen(own_up, old_up, at)
        else:
            e = j - 2 * experts
            dn_all[d, e * width : (e + 1) * width, :] = chosen(own_down, old_down, e)
        spread(j, 0).start()
        spread(j, 1).start()

    def pass_weights(j):
        arrived(j, 0)
        spread(j, 2).start()

    def share_tokens(slab, r):
        for k in range(3):
            @pl.when(slab == partners[k])
            def _():
                for q in ((0,) if r == 0 else steps[1:]):
                    token_copy(k, q).start()

    def relay_tokens(r):
        @pl.when(middle)
        def _():
            landed(0, outer, r)
            line(0, outer, r).start()
            landed(0, inner, r)
            line(0, inner, r, 1).start()

    def relay_late(r):
        @pl.when(middle)
        def _():
            landed(0, second, r)
            line(0, second, r, 1).start()
            for q in ((0,) if r == 0 else steps[1:]):
                landed(1, outer, q, True)
                line(1, outer, q, fine=True).start()

    for copy in local[:2]:
        copy.wait()
    take_weights(0)
    relay_tokens(0)
    take_weights(1)
    pass_weights(0)
    take_weights(2)
    relay_tokens(1)

    @pl.when(middle)
    def _():
        for r in range(2):
            line(1, h, r, 0, True).start()

    pass_weights(1)
    for j in range(3, 2 * experts):
        take_weights(j)
    for copy in local[2:]:
        copy.wait()
    pass_weights(2)
    take_weights(2 * experts)
    relay_late(0)
    for j in range(3, 2 * experts):
        pass_weights(j)
    for j in range(2 * experts + 1, chunks):
        take_weights(j)
    for r in range(2):
        share_tokens(h, r)

    @pl.when(border)
    def _():
        for r in range(2):
            landed(0, inner, r)
            share_tokens(inner, r)
        landed(0, second, 0)
        share_tokens(second, 0)

    @pl.when(middle)
    def _():
        for slab in (outer, inner):
            for r in range(2):
                share_tokens(slab, r)
        share_tokens(second, 0)

    pass_weights(2 * experts)
    relay_late(1)

    @pl.when(border)
    def _():
        landed(0, second, 1)

    share_tokens(second, 1)
    for j in range(2 * experts + 1, chunks):
        pass_weights(j)
    for j in range(chunks):
        arrived(j, 1)
        arrived(j, 2)

    core = d % 2
    lot = tall // 2

    def strip(index):
        return pl.ds(pl.multiple_of(index * lot, lot), lot)

    def lend(i, owner):
        slab = owner + (i + 1) * way
        return remote(
            dn_all.at[slab, strip(core)], dn_end.at[slab, strip(core)],
            l_send.at[0, i], l_recv.at[0, i], {"hidden": inner},
        )

    def lend_near(i, which):
        ref = dn_end.at[outer + (i + 1) * way, strip(which)]
        return remote(ref, ref, l_send.at[1, i], l_recv.at[1, i], {"dp": near})

    @pl.when(border)
    def _():
        for i in range(3):
            lend(i, h).start()

    def add_tokens(slabs, r, first):
        for e in range(experts):
            total = None if first else acc_gu[e, halves[r]]
            for slab in slabs:
                term = jnp.dot(tok_all[slab, halves[r]], gu_all[slab, e], preferred_element_type=full)
                total = term if total is None else total + term
            acc_gu[e, halves[r]] = total

    def add_grads(slabs, part, first, total_ref=acc_gh, weight=dn_all):
        total = None if first else total_ref[part]
        for slab in slabs:
            term = lax.dot_general(
                grad_all[slab, part], weight[slab], (((1,), (1,)), ((), ())),
                preferred_element_type=full,
            )
            total = term if total is None else total + term
        total_ref[part] = total

    def activate(r):
        for b in half_blocks[r]:
            part = slice(b * BLOCK, (b + 1) * BLOCK)
            both = sum(acc_gu[e, part] * picks[b][e] for e in range(experts))
            gate_value, up_value = both[:, :width], both[:, width:]
            gate_sel[part] = gate_value
            up_sel[part] = up_value
            hidden = gate_value * jax.nn.sigmoid(gate_value) * up_value
            hid_out[part] = (hidden * alive[b]).astype(half)
            for e in range(experts):
                hid[part, e * width : (e + 1) * width] = (hidden * masks[b][e]).astype(half)

    def hidden_out(r):
        return remote(
            hid_out.at[halves[r]], hid_in.at[halves[r]], h_send.at[0, r], h_recv.at[0, r],
            {"hidden": inner},
        )

    def grads_out(q):
        return remote(
            gh_out.at[cuts[q]], gh_in.at[cuts[q]], h_send.at[1, q], h_recv.at[1, q],
            {"hidden": outer},
        )

    def block_place(k, q, b):
        side, spot = place(k, q)
        start = spot.start + b * BLOCK - edges[q]
        return side, slice(start, start + BLOCK)

    def make_pre(q, extra=None):
        for b in cut_blocks[q]:
            part = slice(b * BLOCK, (b + 1) * BLOCK)
            side, spot = block_place(3, q, b)
            gate_value, up_value = gate_sel[part], up_sel[part]
            grad_hidden = sum(
                acc_gh[part, e * width : (e + 1) * width] * picks[b][e] for e in range(experts)
            )
            if extra is not None:
                grad_hidden = grad_hidden + extra[part].astype(full)
            s = jax.nn.sigmoid(gate_value)
            grad_gate = grad_hidden * up_value * s * (1.0 + gate_value * (1.0 - s))
            grad_up = grad_hidden * gate_value * s
            pre[part, :width] = (grad_gate * alive[b]).astype(half)
            pre[part, width:] = (grad_up * alive[b]).astype(half)
            for e in range(experts):
                at = e * 2 * width
                wide[side, spot, at : at + width] = (grad_gate * masks[b][e]).astype(half)
                wide[side, spot, at + width : at + 2 * width] = (grad_up * masks[b][e]).astype(half)

    def pre_copy(k, q):
        source = pre_dp.at[1, cuts[q]] if k == 2 else pre.at[cuts[q]]
        to = far if k == 1 else near
        return remote(
            source, pre_dp.at[k, cuts[q]], p_send.at[k, q], p_recv.at[k, q], {"dp": to}
        )

    def send_pre(q):
        pre_copy(1, q).start()
        pre_copy(0, q).start()

    parts, cores = (part_own, part_end), (core_own, core_end)
    lefts = (hid, hid_end)

    def core_copy(kind, i):
        slab = (cross, near)[i]
        return remote(
            parts[kind].at[slab], cores[kind].at[i], r_send.at[kind, i], r_recv.at[kind, i],
            {"dp": near},
        )

    def down_term(kind, slab, left=None):
        parts[kind][slab] = lax.dot_general(
            (lefts[kind] if left is None else left)[...], grad_all[slab], (((0,), (0,)), ((), ())), preferred_element_type=full
        ).astype(half)
        for i in range(2):
            @pl.when(slab == (cross, near)[i])
            def _():
                core_copy(kind, i).start()

    def core_sum(kind, i):
        slab = (far, d)[i]
        return parts[kind][slab].astype(full) + cores[kind][i].astype(full)

    own_far = remote(sum_own, far_own, r_send.at[2, 0], r_recv.at[2, 0], {"dp": far})
    end_near_out = remote(sum_near, end_near, e_send.at[0, 0], e_recv.at[0, 0], {"hidden": outer})

    def end_far_out(e):
        part = slice(e * width, (e + 1) * width)
        return remote(
            sum_far.at[part], end_far.at[part], e_send.at[1, e], e_recv.at[1, e], {"hidden": outer}
        )

    def end_cross(e):
        part = slice(e * width, (e + 1) * width)
        return remote(
            end_far.at[part], end_got.at[part], e_send.at[2, e], e_recv.at[2, e], {"dp": far}
        )

    def sum_end_far():
        core_copy(1, 0).wait_recv()
        sum_far[...] = core_sum(1, 0).astype(half)

    def widen(k, q):
        for b in cut_blocks[q]:
            part = slice(b * BLOCK, (b + 1) * BLOCK)
            side, spot = block_place(k, q, b)
            for e in range(experts):
                row = b * experts + e
                keep = mask_dp[k, row : row + 1, :]
                for i in range(2):
                    at = (e * 2 + i) * width
                    value = pre_dp[k, part, i * width : (i + 1) * width].astype(full)
                    wide[side, spot, at : at + width] = (value * keep).astype(half)

    def gate_term(side, q, past=None):
        rows_of = slice(pair(q).start, pair(q if past is None else past).stop)
        return lax.dot_general(
            tok_dp[side, rows_of], wide[side, rows_of], (((0,), (0,)), ((), ())),
            preferred_element_type=full,
        )

    def near_gates(q):
        token_copy(0, q).wait_recv()
        pre_copy(0, q).wait_recv()
        widen(0, q)
        term = gate_term(0, q)
        acc_out[...] = term if q == 0 else acc_out[...] + term

    def take_far(q):
        pre_copy(1, q).wait_recv()
        pre_copy(2, q).start()

    def widen_far(q):
        for k in (1, 2):
            token_copy(k, q).wait_recv()
        widen(1, q)
        pre_copy(2, q).wait_recv()
        widen(2, q)

    def sent_early():
        for r in range(2):
            line(0, h, r, 0, True).wait_send()
        for k in range(3):
            mask_copy(k).wait_send()
        for j in range(chunks):
            for i in range(3):
                spread(j, i).wait_send()
        if exchange:
            for group in swaps:
                for copy in group:
                    copy.wait_send()

    def pass_end(e):
        @pl.when(far != h)
        def _():
            end_far_out(e).wait_recv()

        end_cross(e).start()

    def send_own_far():
        core_copy(0, 0).wait_recv()
        sum_own[...] = core_sum(0, 0).astype(half)
        own_far.start()

    for k in range(3):
        mask_copy(k).wait_recv()
    own_tokens = [
        pltpu.make_async_copy(tok_all.at[d, cuts[q]], tok_dp.at[place(3, q)], local_sem.at[q])
        for q in steps
    ]

    @pl.when(border)
    def _():
        for r in range(2):
            add_tokens((h, inner, second), r, True)
            add_grads((h,), halves[r], True)
        for r in range(2):
            landed(0, third, r)
            share_tokens(third, r)
            add_tokens((third,), r, False)
            activate(r)
            hidden_out(r).start()
        down_term(1, h, hid)
        for copy in own_tokens:
            copy.start()

        @pl.when(far == h)
        def _():
            core_copy(1, 0).wait_recv()
            end_far[...] = core_sum(1, 0).astype(half)
            for e in range(experts):
                end_cross(e).start()

        @pl.when(d == h)
        def _():
            core_copy(1, 1).wait_recv()
            end_near[...] = core_sum(1, 1).astype(half)

        for q in steps:
            grads_out(q).wait_recv()
            make_pre(q, gh_in)
            send_pre(q)
            if q == 0:
                sent_early()
                for i in steps:
                    line(1, h, i, 0, True, True).wait_send()
                for r in range(2):
                    hidden_out(r).wait_send()
                for i in range(3):
                    lend(i, h).wait_send()

            if q == steps[-1]:
                @pl.when((far != third) & (far != h))
                def _():
                    for e in range(experts):
                        pass_end(e)

            if q == 0:
                for copy in own_tokens:
                    copy.wait()
            else:
                near_gates(q - 1)


    @pl.when(middle)
    def _():
        for r in range(2):
            add_tokens((h, outer, inner, second), r, True)
            activate(r)
            add_grads((h, outer), halves[r], True)
        for copy in own_tokens:
            copy.start()
        for slab in (h, outer):
            down_term(0, slab)
        lend(0, outer).wait_recv()
        lend_near(0, core).start()
        landed(1, inner, 0)
        add_grads((inner,), halves[0], False)
        lend(1, outer).wait_recv()
        lend_near(1, core).start()
        landed(1, inner, 1)
        add_grads((inner,), halves[1], False)
        lend(2, outer).wait_recv()
        lend_near(2, core).start()
        down_term(0, inner)
        for i in range(3):
            lend_near(i, 1 - core).wait_recv()
        for r in range(2):
            add_grads((h, inner), halves[r], True, acc_end, dn_end)
        for copy in own_tokens:
            copy.wait()
        sent_early()
        for r in range(2):
            line(0, h, r, 1, True).wait_send()
            line(1, h, r, 0, True).wait_send()
            line(0, outer, r).wait_send()
            line(0, inner, r, 1).wait_send()
            line(0, second, r, 1).wait_send()
        for r in range(2):
            hidden_out(r).wait_recv()
            for b in half_blocks[r]:
                part = slice(b * BLOCK, (b + 1) * BLOCK)
                value = hid_in[part].astype(full)
                for e in range(experts):
                    hid_end[part, e * width : (e + 1) * width] = (value * masks[b][e]).astype(half)

        def last_grads(q):
            landed(1, second, q, True)
            add_grads((second,), cuts[q], False, acc_end, dn_end)
            for b in cut_blocks[q]:
                part = slice(b * BLOCK, (b + 1) * BLOCK)
                gh_out[part] = sum(
                    acc_end[part, e * width : (e + 1) * width] * picks[b][e] for e in range(experts)
                ).astype(half)
            grads_out(q).start()
            if q == steps[-1]:
                down_term(1, second)
            add_grads((second,), cuts[q], False)
            make_pre(q)
            send_pre(q)

        for slab in (h, inner):
            down_term(1, slab)
        @pl.when((far != second) & (far != outer))
        def _():
            sum_end_far()
            for e in range(experts):
                end_far_out(e).start()

        for q in steps:
            last_grads(q)
            if 0 < q < steps[-1]:
                near_gates(q - 1)

        @pl.when(far != second)
        def _():
            send_own_far()

        down_term(0, second)

        @pl.when(far == second)
        def _():
            sum_end_far()
            for e in range(experts):
                end_far_out(e).start()
            send_own_far()

        @pl.when(d != outer)
        def _():
            core_copy(1, 1).wait_recv()
            sum_near[...] = core_sum(1, 1).astype(half)
            end_near_out.start()

        near_gates(steps[-1] - 1)

    take_far(0)
    near_gates(steps[-1])
    take_far(1)

    @pl.when(border & (far == third))
    def _():
        for e in range(experts):
            pass_end(e)

    widen_far(0)
    take_far(2)
    widen_far(1)
    acc_out[...] = acc_out[...] + gate_term(1, 0, 1)
    widen_far(2)
    total = acc_out[...] + gate_term(1, 2)
    for e in range(experts):
        at = e * 2 * width
        out_gate[e] = total[:, at : at + width].astype(half)
        out_up[e] = total[:, at + width : at + 2 * width].astype(half)

    @pl.when(middle)
    def _():
        core_copy(0, 1).wait_recv()
        own_far.wait_recv()
        total = core_sum(0, 1) + far_own[...].astype(full)
        for e in range(experts):
            out_down[e] = total[e * width : (e + 1) * width].astype(half)

    @pl.when(border)
    def _():
        @pl.when(d != h)
        def _():
            end_near_out.wait_recv()

        for e in range(experts):
            end_cross(e).wait_recv()
        total = end_near[...].astype(full) + end_got[...].astype(full)
        for e in range(experts):
            out_down[e] = total[e * width : (e + 1) * width].astype(half)

    for k in range(3):
        for q in steps:
            token_copy(k, q).wait_send()
            pre_copy(k, q).wait_send()

    @pl.when(middle)
    def _():
        for q in steps:
            line(1, outer, q, fine=True).wait_send()
            grads_out(q).wait_send()
        for i in range(3):
            lend_near(i, core).wait_send()
        for i in range(2):
            core_copy(0, i).wait_send()

            @pl.when((cross, near)[i] != outer)
            def _():
                core_copy(1, i).wait_send()

        own_far.wait_send()

        @pl.when(far != outer)
        def _():
            for e in range(experts):
                end_far_out(e).wait_send()

        @pl.when(d != outer)
        def _():
            end_near_out.wait_send()

    @pl.when(border)
    def _():
        for i in range(2):
            @pl.when((cross, near)[i] == h)
            def _():
                core_copy(1, i).wait_send()

        for e in range(experts):
            end_cross(e).wait_send()


def settle_kernel(*refs):
    count = (len(refs) - 1) // 2
    copies = [
        pltpu.make_async_copy(refs[i], refs[count + i], refs[-1].at[i]) for i in range(count)
    ]
    for copy in copies:
        copy.start()
    for copy in copies:
        copy.wait()


def settle(arrays):
    count = len(arrays)
    return pl.pallas_call(
        settle_kernel,
        out_shape=tuple(jax.ShapeDtypeStruct(a.shape, a.dtype) for a in arrays),
        in_specs=[pl.BlockSpec(memory_space=pltpu.VMEM)] * count,
        out_specs=(pl.BlockSpec(memory_space=pl.ANY),) * count,
        scratch_shapes=[pltpu.SemaphoreType.DMA((count,))],
    )(*[pltpu.with_memory_space_constraint(a, pltpu.VMEM) for a in arrays])


def on_device_fused(tokens, grad_out, gate_weight, up_weight, down_weight, matching, block_counts):
    groups = lax.axis_size("expert")
    zs = lax.axis_size("hidden")
    ds = lax.axis_size("dp")
    exchange = groups == 2
    if not exchange:
        gate_weight, up_weight, down_weight = relocate(
            (gate_weight, up_weight, down_weight), matching
        )
        matching = jnp.zeros_like(matching)
    rows, feats = tokens.shape[2:]
    experts, part, width = gate_weight.shape
    vmem = pl.BlockSpec(memory_space=pltpu.VMEM)
    smem = pl.BlockSpec(memory_space=pltpu.SMEM)
    half, full = jnp.bfloat16, jnp.float32
    wide = experts * 2 * width
    tall = experts * width
    chunks = 3 * experts
    dma = pltpu.SemaphoreType.DMA
    down = pltpu.VMEM((tall, part), half)
    narrow = pltpu.VMEM((rows, width), half)
    mask = (experts * (rows // BLOCK), width)
    grads = pl.pallas_call(
        functools.partial(fused_kernel, exchange, experts),
        out_shape=tuple(
            pltpu.VMEM(w.shape, half) for w in (gate_weight, up_weight, down_weight)
        ),
        in_specs=[smem, smem] + [pl.BlockSpec(memory_space=pltpu.HBM)] * 5,
        out_specs=(vmem,) * 3,
        scratch_shapes=[
            pltpu.VMEM((zs, rows, feats), half),
            pltpu.VMEM((zs, rows, feats), half),
            pltpu.VMEM((2, 2 * rows, feats), half),
            pltpu.VMEM((ds, experts, part, 2 * width), half),
            pltpu.VMEM((ds, tall, part), half),
            pltpu.VMEM((ds, tall, part), half),
            pltpu.VMEM(gate_weight.shape, half),
            pltpu.VMEM(up_weight.shape, half),
            pltpu.VMEM(down_weight.shape, half),
            pltpu.VMEM(gate_weight.shape, half),
            pltpu.VMEM(up_weight.shape, half),
            pltpu.VMEM(down_weight.shape, half),
            pltpu.VMEM((experts, rows, 2 * width), full),
            pltpu.VMEM((rows, tall), full),
            pltpu.VMEM((rows, tall), full),
            pltpu.VMEM((feats, wide), full),
            pltpu.VMEM((rows, width), full),
            pltpu.VMEM((rows, width), full),
            pltpu.VMEM((rows, tall), half),
            pltpu.VMEM((rows, tall), half),
            narrow, narrow, narrow, narrow,
            pltpu.VMEM(mask, full),
            pltpu.VMEM((3,) + mask, full),
            pltpu.VMEM((rows, 2 * width), half),
            pltpu.VMEM((3, rows, 2 * width), half),
            pltpu.VMEM((2, 2 * rows, wide), half),
            pltpu.VMEM((ds, tall, part), half),
            pltpu.VMEM((ds, tall, part), half),
            pltpu.VMEM((2, tall, part), half),
            pltpu.VMEM((2, tall, part), half),
            down, down, down, down, down, down, down,
            dma((2, 2, zs, 3)),
            dma((2, zs, 3)),
            dma((3 * experts * 2,)),
            dma((3 * experts * 2,)),
            dma((chunks, 3)),
            dma((chunks, 3)),
            dma((3, 3)),
            dma((3, 3)),
            dma((3, 3)),
            dma((3, 3)),
            dma((3,)),
            dma((3,)),
            dma((2, 3)),
            dma((2, 3)),
            dma((2, 3)),
            dma((2, 3)),
            dma((3, 2)),
            dma((3, 2)),
            dma((3, experts)),
            dma((3, experts)),
            dma((5,)),
        ],
        compiler_params=pltpu.CompilerParams(
            collective_id=0, has_side_effects=True, vmem_limit_bytes=63 * 1024 * 1024
        ),
    )(
        block_counts.reshape(-1), matching, tokens.reshape(rows, feats),
        grad_out.reshape(rows, feats), gate_weight, up_weight, down_weight,
    )
    return settle(grads)


def fused_fits(mesh):
    return mesh.shape["dp"] == 4 and mesh.shape["hidden"] == 4


def solution(mesh):
    on_device = on_device_fused if fused_fits(mesh) else on_device_plain
    in_specs = (
        P("expert", "dp", None, "hidden"),
        P("expert", "dp", None, "hidden"),
        P("expert", "dp", "hidden"),
        P("expert", "dp", "hidden"),
        P("expert", "hidden", "dp"),
        P(),
        P("expert", "dp", None),
    )
    out_specs = (
        P("expert", "dp", "hidden"),
        P("expert", "dp", "hidden"),
        P("expert", "hidden", "dp"),
    )
    return jax.shard_map(
        on_device, mesh=mesh, in_specs=in_specs, out_specs=out_specs, check_vma=False
    )
```

```python
import functools

import jax
import jax.numpy as jnp
from jax import lax
from jax.experimental import pallas as pl
from jax.experimental.pallas import tpu as pltpu
from jax.sharding import PartitionSpec as P

BLOCK = 128


def contract_rows(left, right):
    return lax.dot_general(
        left, right, (((0,), (0,)), ((), ())), preferred_element_type=jnp.float32
    )


def block_owners(counts, blocks):
    bounds = jnp.cumsum(counts)
    index = jnp.arange(blocks, dtype=jnp.int32)
    owner = jnp.sum((index[:, None] >= bounds[None, :]).astype(jnp.int32), axis=1)
    owner = jnp.minimum(owner, counts.shape[0] - 1)
    alive = (index < bounds[-1]).astype(jnp.float32)
    return (owner, alive)


def add_into(total, term, expert):
    current = lax.dynamic_index_in_dim(total, expert, 0, keepdims=True)
    return lax.dynamic_update_index_in_dim(total, current + term[None], expert, 0)


def expert_terms(row_blocks, grad_blocks, weight_gate, weight_up, weight_down, owner, alive):
    zeros_gate = jnp.zeros(weight_gate.shape, jnp.float32)
    zeros_down = jnp.zeros(weight_down.shape, jnp.float32)

    def step(carry, inputs):
        total_gate, total_up, total_down = carry
        row_block, grad_block, expert, live = inputs
        gate_matrix = lax.dynamic_index_in_dim(weight_gate, expert, 0, keepdims=False)
        up_matrix = lax.dynamic_index_in_dim(weight_up, expert, 0, keepdims=False)
        down_matrix = lax.dynamic_index_in_dim(weight_down, expert, 0, keepdims=False)
        gate_value = jnp.dot(row_block, gate_matrix, preferred_element_type=jnp.float32)
        up_value = jnp.dot(row_block, up_matrix, preferred_element_type=jnp.float32)
        sigmoid_gate = jax.nn.sigmoid(gate_value)
        activated = gate_value * sigmoid_gate
        hidden = (activated * up_value * live).astype(jnp.bfloat16)
        grad_hidden = lax.dot_general(
            grad_block, down_matrix, (((1,), (1,)), ((), ())), preferred_element_type=jnp.float32
        )
        grad_gate = (
            grad_hidden * up_value * sigmoid_gate * (1.0 + gate_value * (1.0 - sigmoid_gate)) * live
        ).astype(jnp.bfloat16)
        grad_up = (grad_hidden * activated * live).astype(jnp.bfloat16)
        total_gate = add_into(total_gate, contract_rows(row_block, grad_gate), expert)
        total_up = add_into(total_up, contract_rows(row_block, grad_up), expert)
        total_down = add_into(total_down, contract_rows(hidden, grad_block), expert)
        return ((total_gate, total_up, total_down), None)

    totals, unused = lax.scan(
        step, (zeros_gate, zeros_gate, zeros_down), (row_blocks, grad_blocks, owner, alive)
    )
    return totals


def relocate(arrays, matching):
    groups = lax.axis_size("expert")
    joined = jnp.concatenate([array_piece.reshape(groups, -1) for array_piece in arrays], axis=1)
    spread = lax.all_to_all(joined, "expert", split_axis=0, concat_axis=0, tiled=True)
    ordered = jnp.take(spread, matching, axis=0)
    settled = lax.all_to_all(ordered, "expert", split_axis=0, concat_axis=0, tiled=True)
    pieces = []
    offset = 0
    for array_piece in arrays:
        length = array_piece.size // groups
        pieces.append(settled[:, offset : offset + length].reshape(array_piece.shape))
        offset = offset + length
    return pieces


def on_device_plain(tokens, grad_out, gate_weight, up_weight, down_weight, matching, block_counts):
    moved = relocate((gate_weight, up_weight, down_weight), matching)
    weight_gate, weight_up, weight_down = (
        lax.all_gather(moved[0], "dp", axis=1, tiled=True),
        lax.all_gather(moved[1], "dp", axis=1, tiled=True),
        lax.all_gather(moved[2], "dp", axis=2, tiled=True),
    )
    rows_full, grads_full = (
        lax.all_gather(tokens[0, 0], "hidden", axis=1, tiled=True),
        lax.all_gather(grad_out[0, 0], "hidden", axis=1, tiled=True),
    )
    blocks = rows_full.shape[0] // BLOCK
    width = rows_full.shape[1]
    owner, alive = block_owners(block_counts[0, 0], blocks)
    totals = expert_terms(
        rows_full.reshape(blocks, BLOCK, width),
        grads_full.reshape(blocks, BLOCK, width),
        weight_gate,
        weight_up,
        weight_down,
        owner,
        alive,
    )
    summed = (
        lax.psum_scatter(
            totals[0].astype(jnp.bfloat16), "dp", scatter_dimension=1, tiled=True
        ).astype(jnp.float32),
        lax.psum_scatter(
            totals[1].astype(jnp.bfloat16), "dp", scatter_dimension=1, tiled=True
        ).astype(jnp.float32),
        lax.psum_scatter(
            totals[2].astype(jnp.bfloat16), "dp", scatter_dimension=2, tiled=True
        ).astype(jnp.float32),
    )
    return (
        summed[0].astype(jnp.bfloat16),
        summed[1].astype(jnp.bfloat16),
        summed[2].astype(jnp.bfloat16),
    )


MESH = pl.DeviceIdType.MESH


def flip(index, bit):
    return index + bit - 2 * bit * ((index // bit) % 2)


def fused_kernel(
    exchange, experts, counts_ref, match_ref, tok_ref, grad_ref, gate_ref, up_ref, down_ref,
    out_gate, out_up, out_down,
    tok_all, grad_all, tok_dp, gu_all, dn_all, dn_end,
    own_gate, own_up, own_down, old_gate, old_up, old_down,
    acc_gu, acc_gh, acc_end, acc_out, gate_sel, up_sel, hid, hid_end, hid_out, hid_in, gh_out, gh_in,
    mask_own, mask_dp, pre, pre_dp, wide,
    part_own, part_end, core_own, core_end, sum_own, far_own, sum_far, sum_near, end_far, end_near, end_got,
    z_send, z_recv, y_send, y_recv, w_send, w_recv, t_send, t_recv, p_send, p_recv, m_send, m_recv,
    l_send, l_recv, h_send, h_recv, r_send, r_recv, e_send, e_recv, local_sem,
):
    zs = lax.axis_size("hidden")
    h = lax.axis_index("hidden")
    d = lax.axis_index("dp")
    p = lax.axis_index("expert")
    rows, feats = tok_ref.shape
    width = gate_ref.shape[2]
    blocks = rows // BLOCK
    tall = experts * width
    halves = [slice(0, rows // 2), slice(rows // 2, rows)]
    half_blocks = [range(0, blocks // 2), range(blocks // 2, blocks)]
    edges = (0, rows // 2, rows // 4 * 3, rows)
    steps = range(len(edges) - 1)
    cuts = [slice(edges[q], edges[q + 1]) for q in steps]
    cut_blocks = [range(edges[q] // BLOCK, edges[q + 1] // BLOCK) for q in steps]
    near, far = flip(d, 1), flip(d, 2)
    cross = flip(near, 2)
    partners = (near, far, cross)
    middle = (h > 0) & (h < zs - 1)
    border = (h == 0) | (h == zs - 1)
    way = 1 - 2 * (h // (zs // 2))
    inner, outer = h + way, h - way
    second, third = h + 2 * way, h + 3 * way
    full, half = jnp.float32, jnp.bfloat16

    def remote(source, target, send, recv, where):
        return pltpu.make_async_remote_copy(
            src_ref=source, dst_ref=target, send_sem=send, recv_sem=recv,
            device_id=where, device_id_type=MESH,
        )

    local = [
        pltpu.make_async_copy(source, target, local_sem.at[i])
        for i, (source, target) in enumerate((
            (gate_ref, own_gate), (up_ref, own_up), (down_ref, own_down),
            (tok_ref, tok_all.at[h]), (grad_ref, grad_all.at[h]),
        ))
    ]
    for copy in local:
        copy.start()

    barrier = pltpu.get_barrier_semaphore()
    for partner in partners:
        pl.semaphore_signal(barrier, inc=1, device_id={"dp": partner}, device_id_type=MESH)
    if exchange:
        pl.semaphore_signal(barrier, inc=1, device_id={"expert": 1 - p}, device_id_type=MESH)
    pl.semaphore_signal(barrier, inc=1, device_id={"hidden": inner}, device_id_type=MESH)

    @pl.when(middle)
    def _():
        pl.semaphore_signal(barrier, inc=1, device_id={"hidden": outer}, device_id_type=MESH)

    bounds = [counts_ref[0]]
    for e in range(1, experts):
        bounds.append(bounds[-1] + counts_ref[e])
    picks, masks, alive = [], [], []
    for b in range(blocks):
        owner = jnp.int32(0)
        for e in range(experts):
            owner = owner + jnp.where(b >= bounds[e], 1, 0)
        owner = jnp.minimum(owner, experts - 1)
        alive.append(jnp.where(b < bounds[-1], 1.0, 0.0))
        picks.append([jnp.where(owner == e, 1.0, 0.0) for e in range(experts)])
        masks.append([picks[b][e] * alive[b] for e in range(experts)])
        for e in range(experts):
            row = b * experts + e
            mask_own[row : row + 1, :] = jnp.full((1, mask_own.shape[1]), masks[b][e], full)

    peers = (h + zs - 1) // zs + (2 * zs - 2 - h) // zs
    pl.semaphore_wait(barrier, peers + (4 if exchange else 3))

    mine = (tok_ref, grad_ref)
    whole = (tok_all, grad_all)

    def line(kind, slab, r, outward=0, own=False, fine=False):
        part = (cuts if fine else halves)[r]
        source = mine[kind].at[part] if own else whole[kind].at[slab, part]
        return remote(
            source, whole[kind].at[slab, part],
            z_send.at[outward, kind, slab, r], z_recv.at[kind, slab, r],
            {"hidden": outer if outward else inner},
        )

    def landed(kind, slab, r, fine=False):
        line(kind, slab, r, fine=fine).wait_recv()

    def place(k, q):
        size = edges[q + 1] - edges[q]
        start = 2 * edges[q] + (0 if k in (1, 3) else size)
        return (0 if k in (0, 3) else 1), slice(start, start + size)

    def pair(q):
        return slice(2 * edges[q], 2 * edges[q + 1])

    def token_copy(k, q, own=False):
        source = tok_ref.at[cuts[q]] if own else tok_all.at[partners[k], cuts[q]]
        return remote(
            source, tok_dp.at[place(k, q)],
            t_send.at[k, q], t_recv.at[k, q], {"dp": partners[k]},
        )

    def mask_copy(k):
        return remote(
            mask_own, mask_dp.at[k], m_send.at[k], m_recv.at[k], {"dp": partners[k]}
        )

    for r in range(2):
        line(0, h, r, 0, True).start()

        @pl.when(middle)
        def _():
            line(0, h, r, 1, True).start()

    @pl.when(border)
    def _():
        for q in steps:
            line(1, h, q, 0, True, True).start()

    feat_halves = [slice(0, feats // 2), slice(feats // 2, feats)]

    def swap(i, e, f=None):
        source = (gate_ref, up_ref, down_ref)[i]
        target = (old_gate, old_up, old_down)[i]
        at = (e,) if f is None else (e, feat_halves[f])
        n = (i * experts + e) * 2 + (f or 0)
        return remote(source.at[at], target.at[at], y_send.at[n], y_recv.at[n], {"expert": 1 - p})

    swaps = []
    if exchange:
        swaps = [[swap(0, e, f), swap(1, e, f)] for e in range(experts) for f in range(2)]
        swaps += [[swap(2, e)] for e in range(experts)]
        for group in swaps:
            for copy in group:
                copy.start()
    for k in range(3):
        mask_copy(k).start()

        @pl.when(h == partners[k])
        def _():
            token_copy(k, steps[-1], True).start()

    def chosen(own, other, at):
        if not exchange:
            return own[at]
        return jnp.where(match_ref[p] == p, own[at], other[at])

    chunks = 3 * experts

    def piece(j, slab):
        if j < 2 * experts:
            return gu_all.at[slab, j // 2, feat_halves[j % 2]]
        e = j - 2 * experts
        return dn_all.at[slab, e * width : (e + 1) * width]

    def spread(j, i):
        ref = piece(j, (d, d, far)[i])
        to = (far, near, near)[i]
        return remote(ref, ref, w_send.at[j, i], w_recv.at[j, i], {"dp": to})

    def arrived(j, i):
        ref = piece(j, (far, near, cross)[i])
        remote(ref, ref, w_send.at[j, i], w_recv.at[j, i], {"dp": near}).wait_recv()

    def take_weights(j):
        if exchange:
            for copy in swaps[j]:
                copy.wait_recv()
        if j < 2 * experts:
            at = (j // 2, feat_halves[j % 2])
            gu_all[d, j // 2, feat_halves[j % 2], :width] = chosen(own_gate, old_gate, at)
            gu_all[d, j // 2, feat_halves[j % 2], width:] = chosen(own_up, old_up, at)
        else:
            e = j - 2 * experts
            dn_all[d, e * width : (e + 1) * width, :] = chosen(own_down, old_down, e)
        spread(j, 0).start()
        spread(j, 1).start()

    def pass_weights(j):
        arrived(j, 0)
        spread(j, 2).start()

    def share_tokens(slab, r):
        for k in range(3):
            @pl.when(slab == partners[k])
            def _():
                for q in ((0,) if r == 0 else steps[1:]):
                    token_copy(k, q).start()

    def relay_tokens(r):
        @pl.when(middle)
        def _():
            landed(0, outer, r)
            line(0, outer, r).start()
            landed(0, inner, r)
            line(0, inner, r, 1).start()

    def relay_late(r):
        @pl.when(middle)
        def _():
            landed(0, second, r)
            line(0, second, r, 1).start()
            for q in ((0,) if r == 0 else steps[1:]):
                landed(1, outer, q, True)
                line(1, outer, q, fine=True).start()

    for copy in local[:2]:
        copy.wait()
    take_weights(0)
    relay_tokens(0)
    take_weights(1)
    pass_weights(0)
    take_weights(2)
    relay_tokens(1)

    @pl.when(middle)
    def _():
        for r in range(2):
            line(1, h, r, 0, True).start()

    pass_weights(1)
    for j in range(3, 2 * experts):
        take_weights(j)
    for copy in local[2:]:
        copy.wait()
    pass_weights(2)
    take_weights(2 * experts)
    relay_late(0)
    for j in range(3, 2 * experts):
        pass_weights(j)
    for j in range(2 * experts + 1, chunks):
        take_weights(j)
    for k in range(3):
        @pl.when(h == partners[k])
        def _():
            for q in steps[:-1]:
                token_copy(k, q).start()

    @pl.when(border)
    def _():
        for r in range(2):
            landed(0, inner, r)
            share_tokens(inner, r)
        landed(0, second, 0)
        share_tokens(second, 0)

    @pl.when(middle)
    def _():
        for slab in (outer, inner):
            for r in range(2):
                share_tokens(slab, r)
        share_tokens(second, 0)

    pass_weights(2 * experts)
    relay_late(1)

    @pl.when(border)
    def _():
        landed(0, second, 1)

    share_tokens(second, 1)
    for j in range(2 * experts + 1, chunks):
        pass_weights(j)
    for j in range(chunks):
        arrived(j, 1)
        arrived(j, 2)

    core = d % 2
    lot = tall // 2

    def strip(index):
        return pl.ds(pl.multiple_of(index * lot, lot), lot)

    def lend(i, owner):
        slab = owner + (i + 1) * way
        return remote(
            dn_all.at[slab, strip(core)], dn_end.at[slab, strip(core)],
            l_send.at[0, i], l_recv.at[0, i], {"hidden": inner},
        )

    def lend_near(i, which):
        ref = dn_end.at[outer + (i + 1) * way, strip(which)]
        return remote(ref, ref, l_send.at[1, i], l_recv.at[1, i], {"dp": near})

    @pl.when(border)
    def _():
        for i in range(3):
            lend(i, h).start()

    def add_tokens(slabs, r, first):
        for e in range(experts):
            total = None if first else acc_gu[e, halves[r]]
            for slab in slabs:
                term = jnp.dot(tok_all[slab, halves[r]], gu_all[slab, e], preferred_element_type=full)
                total = term if total is None else total + term
            acc_gu[e, halves[r]] = total

    def add_grads(slabs, part, first, total_ref=acc_gh, weight=dn_all):
        total = None if first else total_ref[part]
        for slab in slabs:
            term = lax.dot_general(
                grad_all[slab, part], weight[slab], (((1,), (1,)), ((), ())),
                preferred_element_type=full,
            )
            total = term if total is None else total + term
        total_ref[part] = total

    def activate(r):
        for b in half_blocks[r]:
            part = slice(b * BLOCK, (b + 1) * BLOCK)
            both = sum(acc_gu[e, part] * picks[b][e] for e in range(experts))
            gate_value, up_value = both[:, :width], both[:, width:]
            gate_sel[part] = gate_value
            up_sel[part] = up_value
            hidden = gate_value * jax.nn.sigmoid(gate_value) * up_value
            hid_out[part] = (hidden * alive[b]).astype(half)
            for e in range(experts):
                hid[part, e * width : (e + 1) * width] = (hidden * masks[b][e]).astype(half)

    def hidden_out(r):
        return remote(
            hid_out.at[halves[r]], hid_in.at[halves[r]], h_send.at[0, r], h_recv.at[0, r],
            {"hidden": inner},
        )

    def grads_out(q):
        return remote(
            gh_out.at[cuts[q]], gh_in.at[cuts[q]], h_send.at[1, q], h_recv.at[1, q],
            {"hidden": outer},
        )

    def block_place(k, q, b):
        side, spot = place(k, q)
        start = spot.start + b * BLOCK - edges[q]
        return side, slice(start, start + BLOCK)

    def make_pre(q, extra=None):
        for b in cut_blocks[q]:
            part = slice(b * BLOCK, (b + 1) * BLOCK)
            side, spot = block_place(3, q, b)
            gate_value, up_value = gate_sel[part], up_sel[part]
            grad_hidden = sum(
                acc_gh[part, e * width : (e + 1) * width] * picks[b][e] for e in range(experts)
            )
            if extra is not None:
                grad_hidden = grad_hidden + extra[part].astype(full)
            s = jax.nn.sigmoid(gate_value)
            grad_gate = grad_hidden * up_value * s * (1.0 + gate_value * (1.0 - s))
            grad_up = grad_hidden * gate_value * s
            pre[part, :width] = (grad_gate * alive[b]).astype(half)
            pre[part, width:] = (grad_up * alive[b]).astype(half)
            for e in range(experts):
                at = e * 2 * width
                wide[side, spot, at : at + width] = (grad_gate * masks[b][e]).astype(half)
                wide[side, spot, at + width : at + 2 * width] = (grad_up * masks[b][e]).astype(half)

    def pre_copy(k, q):
        source = pre_dp.at[1, cuts[q]] if k == 2 else pre.at[cuts[q]]
        to = far if k == 1 else near
        return remote(
            source, pre_dp.at[k, cuts[q]], p_send.at[k, q], p_recv.at[k, q], {"dp": to}
        )

    def send_pre(q):
        pre_copy(1, q).start()
        pre_copy(0, q).start()

    parts, cores = (part_own, part_end), (core_own, core_end)
    lefts = (hid, hid_end)

    def core_copy(kind, i):
        slab = (cross, near)[i]
        return remote(
            parts[kind].at[slab], cores[kind].at[i], r_send.at[kind, i], r_recv.at[kind, i],
            {"dp": near},
        )

    def down_term(kind, slab, left=None):
        parts[kind][slab] = lax.dot_general(
            (lefts[kind] if left is None else left)[...], grad_all[slab], (((0,), (0,)), ((), ())), preferred_element_type=full
        ).astype(half)
        for i in range(2):
            @pl.when(slab == (cross, near)[i])
            def _():
                core_copy(kind, i).start()

    def core_sum(kind, i):
        slab = (far, d)[i]
        return parts[kind][slab].astype(full) + cores[kind][i].astype(full)

    own_far = remote(sum_own, far_own, r_send.at[2, 0], r_recv.at[2, 0], {"dp": far})
    end_near_out = remote(sum_near, end_near, e_send.at[0, 0], e_recv.at[0, 0], {"hidden": outer})

    def end_far_out(e):
        part = slice(e * width, (e + 1) * width)
        return remote(
            sum_far.at[part], end_far.at[part], e_send.at[1, e], e_recv.at[1, e], {"hidden": outer}
        )

    def end_cross(e):
        part = slice(e * width, (e + 1) * width)
        return remote(
            end_far.at[part], end_got.at[part], e_send.at[2, e], e_recv.at[2, e], {"dp": far}
        )

    def sum_end_far():
        core_copy(1, 0).wait_recv()
        sum_far[...] = core_sum(1, 0).astype(half)

    def widen(k, q):
        for b in cut_blocks[q]:
            part = slice(b * BLOCK, (b + 1) * BLOCK)
            side, spot = block_place(k, q, b)
            for e in range(experts):
                row = b * experts + e
                keep = mask_dp[k, row : row + 1, :]
                for i in range(2):
                    at = (e * 2 + i) * width
                    value = pre_dp[k, part, i * width : (i + 1) * width].astype(full)
                    wide[side, spot, at : at + width] = (value * keep).astype(half)

    def gate_term(side, q, past=None):
        rows_of = slice(pair(q).start, pair(q if past is None else past).stop)
        return lax.dot_general(
            tok_dp[side, rows_of], wide[side, rows_of], (((0,), (0,)), ((), ())),
            preferred_element_type=full,
        )

    def near_gates(q):
        token_copy(0, q).wait_recv()
        pre_copy(0, q).wait_recv()
        widen(0, q)
        term = gate_term(0, q)
        acc_out[...] = term if q == 0 else acc_out[...] + term

    def take_far(q):
        pre_copy(1, q).wait_recv()
        pre_copy(2, q).start()

    def widen_far(q):
        for k in (1, 2):
            token_copy(k, q).wait_recv()
        widen(1, q)
        pre_copy(2, q).wait_recv()
        widen(2, q)

    def sent_early():
        for r in range(2):
            line(0, h, r, 0, True).wait_send()
        for k in range(3):
            mask_copy(k).wait_send()
        for j in range(chunks):
            for i in range(3):
                spread(j, i).wait_send()
        if exchange:
            for group in swaps:
                for copy in group:
                    copy.wait_send()

    def pass_end(e):
        @pl.when(far != h)
        def _():
            end_far_out(e).wait_recv()

        end_cross(e).start()

    def send_own_far():
        core_copy(0, 0).wait_recv()
        sum_own[...] = core_sum(0, 0).astype(half)
        own_far.start()

    for k in range(3):
        mask_copy(k).wait_recv()
    own_tokens = [
        pltpu.make_async_copy(tok_all.at[d, cuts[q]], tok_dp.at[place(3, q)], local_sem.at[q])
        for q in steps
    ]

    @pl.when(border)
    def _():
        for r in range(2):
            add_tokens((h, inner, second), r, True)
            add_grads((h,), halves[r], True)
        for r in range(2):
            landed(0, third, r)
            share_tokens(third, r)
            add_tokens((third,), r, False)
            activate(r)
            hidden_out(r).start()
        down_term(1, h, hid)
        for copy in own_tokens:
            copy.start()

        @pl.when(far == h)
        def _():
            core_copy(1, 0).wait_recv()
            end_far[...] = core_sum(1, 0).astype(half)
            for e in range(experts):
                end_cross(e).start()

        @pl.when(d == h)
        def _():
            core_copy(1, 1).wait_recv()
            end_near[...] = core_sum(1, 1).astype(half)

        for q in steps:
            grads_out(q).wait_recv()
            make_pre(q, gh_in)
            send_pre(q)
            if q == 0:
                sent_early()
                for i in steps:
                    line(1, h, i, 0, True, True).wait_send()
                for r in range(2):
                    hidden_out(r).wait_send()
                for i in range(3):
                    lend(i, h).wait_send()

            if q == steps[-1]:
                @pl.when((far != third) & (far != h))
                def _():
                    for e in range(experts):
                        pass_end(e)

            if q == 0:
                for copy in own_tokens:
                    copy.wait()
            else:
                near_gates(q - 1)


    @pl.when(middle)
    def _():
        for r in range(2):
            add_tokens((h, outer, inner, second), r, True)
            activate(r)
            add_grads((h, outer), halves[r], True)
        for copy in own_tokens:
            copy.start()
        for slab in (h, outer):
            down_term(0, slab)
        lend(0, outer).wait_recv()
        lend_near(0, core).start()
        landed(1, inner, 0)
        add_grads((inner,), halves[0], False)
        lend(1, outer).wait_recv()
        lend_near(1, core).start()
        landed(1, inner, 1)
        add_grads((inner,), halves[1], False)
        lend(2, outer).wait_recv()
        lend_near(2, core).start()
        down_term(0, inner)
        for i in range(3):
            lend_near(i, 1 - core).wait_recv()
        for r in range(2):
            add_grads((h, inner), halves[r], True, acc_end, dn_end)
        for copy in own_tokens:
            copy.wait()
        sent_early()
        for r in range(2):
            line(0, h, r, 1, True).wait_send()
            line(1, h, r, 0, True).wait_send()
            line(0, outer, r).wait_send()
            line(0, inner, r, 1).wait_send()
            line(0, second, r, 1).wait_send()
        for r in range(2):
            hidden_out(r).wait_recv()
            for b in half_blocks[r]:
                part = slice(b * BLOCK, (b + 1) * BLOCK)
                value = hid_in[part].astype(full)
                for e in range(experts):
                    hid_end[part, e * width : (e + 1) * width] = (value * masks[b][e]).astype(half)

        def last_grads(q):
            landed(1, second, q, True)
            add_grads((second,), cuts[q], False, acc_end, dn_end)
            for b in cut_blocks[q]:
                part = slice(b * BLOCK, (b + 1) * BLOCK)
                gh_out[part] = sum(
                    acc_end[part, e * width : (e + 1) * width] * picks[b][e] for e in range(experts)
                ).astype(half)
            grads_out(q).start()
            if q == steps[-1]:
                down_term(1, second)
            add_grads((second,), cuts[q], False)
            make_pre(q)
            send_pre(q)

        for slab in (h, inner):
            down_term(1, slab)
        @pl.when((far != second) & (far != outer))
        def _():
            sum_end_far()
            for e in range(experts):
                end_far_out(e).start()

        for q in steps:
            last_grads(q)
            if 0 < q < steps[-1]:
                near_gates(q - 1)

        @pl.when(far != second)
        def _():
            send_own_far()

        down_term(0, second)

        @pl.when(far == second)
        def _():
            sum_end_far()
            for e in range(experts):
                end_far_out(e).start()
            send_own_far()

        @pl.when(d != outer)
        def _():
            core_copy(1, 1).wait_recv()
            sum_near[...] = core_sum(1, 1).astype(half)
            end_near_out.start()

        near_gates(steps[-1] - 1)

    take_far(0)
    near_gates(steps[-1])
    take_far(1)

    @pl.when(border & (far == third))
    def _():
        for e in range(experts):
            pass_end(e)

    widen_far(0)
    take_far(2)
    widen_far(1)
    acc_out[...] = acc_out[...] + gate_term(1, 0, 1)
    widen_far(2)
    total = acc_out[...] + gate_term(1, 2)
    for e in range(experts):
        at = e * 2 * width
        out_gate[e] = total[:, at : at + width].astype(half)
        out_up[e] = total[:, at + width : at + 2 * width].astype(half)

    @pl.when(middle)
    def _():
        core_copy(0, 1).wait_recv()
        own_far.wait_recv()
        total = core_sum(0, 1) + far_own[...].astype(full)
        for e in range(experts):
            out_down[e] = total[e * width : (e + 1) * width].astype(half)

    @pl.when(border)
    def _():
        @pl.when(d != h)
        def _():
            end_near_out.wait_recv()

        for e in range(experts):
            end_cross(e).wait_recv()
        total = end_near[...].astype(full) + end_got[...].astype(full)
        for e in range(experts):
            out_down[e] = total[e * width : (e + 1) * width].astype(half)

    for k in range(3):
        for q in steps:
            token_copy(k, q).wait_send()
            pre_copy(k, q).wait_send()

    @pl.when(middle)
    def _():
        for q in steps:
            line(1, outer, q, fine=True).wait_send()
            grads_out(q).wait_send()
        for i in range(3):
            lend_near(i, core).wait_send()
        for i in range(2):
            core_copy(0, i).wait_send()

            @pl.when((cross, near)[i] != outer)
            def _():
                core_copy(1, i).wait_send()

        own_far.wait_send()

        @pl.when(far != outer)
        def _():
            for e in range(experts):
                end_far_out(e).wait_send()

        @pl.when(d != outer)
        def _():
            end_near_out.wait_send()

    @pl.when(border)
    def _():
        for i in range(2):
            @pl.when((cross, near)[i] == h)
            def _():
                core_copy(1, i).wait_send()

        for e in range(experts):
            end_cross(e).wait_send()


def settle_kernel(*refs):
    count = (len(refs) - 1) // 2
    copies = [
        pltpu.make_async_copy(refs[i], refs[count + i], refs[-1].at[i]) for i in range(count)
    ]
    for copy in copies:
        copy.start()
    for copy in copies:
        copy.wait()


def settle(arrays):
    count = len(arrays)
    return pl.pallas_call(
        settle_kernel,
        out_shape=tuple(jax.ShapeDtypeStruct(a.shape, a.dtype) for a in arrays),
        in_specs=[pl.BlockSpec(memory_space=pltpu.VMEM)] * count,
        out_specs=(pl.BlockSpec(memory_space=pl.ANY),) * count,
        scratch_shapes=[pltpu.SemaphoreType.DMA((count,))],
    )(*[pltpu.with_memory_space_constraint(a, pltpu.VMEM) for a in arrays])


def on_device_fused(tokens, grad_out, gate_weight, up_weight, down_weight, matching, block_counts):
    groups = lax.axis_size("expert")
    zs = lax.axis_size("hidden")
    ds = lax.axis_size("dp")
    exchange = groups == 2
    if not exchange:
        gate_weight, up_weight, down_weight = relocate(
            (gate_weight, up_weight, down_weight), matching
        )
        matching = jnp.zeros_like(matching)
    rows, feats = tokens.shape[2:]
    experts, part, width = gate_weight.shape
    vmem = pl.BlockSpec(memory_space=pltpu.VMEM)
    smem = pl.BlockSpec(memory_space=pltpu.SMEM)
    half, full = jnp.bfloat16, jnp.float32
    wide = experts * 2 * width
    tall = experts * width
    chunks = 3 * experts
    dma = pltpu.SemaphoreType.DMA
    down = pltpu.VMEM((tall, part), half)
    narrow = pltpu.VMEM((rows, width), half)
    mask = (experts * (rows // BLOCK), width)
    grads = pl.pallas_call(
        functools.partial(fused_kernel, exchange, experts),
        out_shape=tuple(
            pltpu.VMEM(w.shape, half) for w in (gate_weight, up_weight, down_weight)
        ),
        in_specs=[smem, smem] + [pl.BlockSpec(memory_space=pltpu.HBM)] * 5,
        out_specs=(vmem,) * 3,
        scratch_shapes=[
            pltpu.VMEM((zs, rows, feats), half),
            pltpu.VMEM((zs, rows, feats), half),
            pltpu.VMEM((2, 2 * rows, feats), half),
            pltpu.VMEM((ds, experts, part, 2 * width), half),
            pltpu.VMEM((ds, tall, part), half),
            pltpu.VMEM((ds, tall, part), half),
            pltpu.VMEM(gate_weight.shape, half),
            pltpu.VMEM(up_weight.shape, half),
            pltpu.VMEM(down_weight.shape, half),
            pltpu.VMEM(gate_weight.shape, half),
            pltpu.VMEM(up_weight.shape, half),
            pltpu.VMEM(down_weight.shape, half),
            pltpu.VMEM((experts, rows, 2 * width), full),
            pltpu.VMEM((rows, tall), full),
            pltpu.VMEM((rows, tall), full),
            pltpu.VMEM((feats, wide), full),
            pltpu.VMEM((rows, width), full),
            pltpu.VMEM((rows, width), full),
            pltpu.VMEM((rows, tall), half),
            pltpu.VMEM((rows, tall), half),
            narrow, narrow, narrow, narrow,
            pltpu.VMEM(mask, full),
            pltpu.VMEM((3,) + mask, full),
            pltpu.VMEM((rows, 2 * width), half),
            pltpu.VMEM((3, rows, 2 * width), half),
            pltpu.VMEM((2, 2 * rows, wide), half),
            pltpu.VMEM((ds, tall, part), half),
            pltpu.VMEM((ds, tall, part), half),
            pltpu.VMEM((2, tall, part), half),
            pltpu.VMEM((2, tall, part), half),
            down, down, down, down, down, down, down,
            dma((2, 2, zs, 3)),
            dma((2, zs, 3)),
            dma((3 * experts * 2,)),
            dma((3 * experts * 2,)),
            dma((chunks, 3)),
            dma((chunks, 3)),
            dma((3, 3)),
            dma((3, 3)),
            dma((3, 3)),
            dma((3, 3)),
            dma((3,)),
            dma((3,)),
            dma((2, 3)),
            dma((2, 3)),
            dma((2, 3)),
            dma((2, 3)),
            dma((3, 2)),
            dma((3, 2)),
            dma((3, experts)),
            dma((3, experts)),
            dma((5,)),
        ],
        compiler_params=pltpu.CompilerParams(
            collective_id=0, has_side_effects=True, vmem_limit_bytes=63 * 1024 * 1024
        ),
    )(
        block_counts.reshape(-1), matching, tokens.reshape(rows, feats),
        grad_out.reshape(rows, feats), gate_weight, up_weight, down_weight,
    )
    return settle(grads)


def fused_fits(mesh):
    return mesh.shape["dp"] == 4 and mesh.shape["hidden"] == 4


def solution(mesh):
    on_device = on_device_fused if fused_fits(mesh) else on_device_plain
    in_specs = (
        P("expert", "dp", None, "hidden"),
        P("expert", "dp", None, "hidden"),
        P("expert", "dp", "hidden"),
        P("expert", "dp", "hidden"),
        P("expert", "hidden", "dp"),
        P(),
        P("expert", "dp", None),
    )
    out_specs = (
        P("expert", "dp", "hidden"),
        P("expert", "dp", "hidden"),
        P("expert", "hidden", "dp"),
    )
    return jax.shard_map(
        on_device, mesh=mesh, in_specs=in_specs, out_specs=out_specs, check_vma=False
    )
```

```python
import functools

import jax
import jax.numpy as jnp
from jax import lax
from jax.experimental import pallas as pl
from jax.experimental.pallas import tpu as pltpu
from jax.sharding import PartitionSpec as P

BLOCK = 128


def contract_rows(left, right):
    return lax.dot_general(
        left, right, (((0,), (0,)), ((), ())), preferred_element_type=jnp.float32
    )


def block_owners(counts, blocks):
    bounds = jnp.cumsum(counts)
    index = jnp.arange(blocks, dtype=jnp.int32)
    owner = jnp.sum((index[:, None] >= bounds[None, :]).astype(jnp.int32), axis=1)
    owner = jnp.minimum(owner, counts.shape[0] - 1)
    alive = (index < bounds[-1]).astype(jnp.float32)
    return (owner, alive)


def add_into(total, term, expert):
    current = lax.dynamic_index_in_dim(total, expert, 0, keepdims=True)
    return lax.dynamic_update_index_in_dim(total, current + term[None], expert, 0)


def expert_terms(row_blocks, grad_blocks, weight_gate, weight_up, weight_down, owner, alive):
    zeros_gate = jnp.zeros(weight_gate.shape, jnp.float32)
    zeros_down = jnp.zeros(weight_down.shape, jnp.float32)

    def step(carry, inputs):
        total_gate, total_up, total_down = carry
        row_block, grad_block, expert, live = inputs
        gate_matrix = lax.dynamic_index_in_dim(weight_gate, expert, 0, keepdims=False)
        up_matrix = lax.dynamic_index_in_dim(weight_up, expert, 0, keepdims=False)
        down_matrix = lax.dynamic_index_in_dim(weight_down, expert, 0, keepdims=False)
        gate_value = jnp.dot(row_block, gate_matrix, preferred_element_type=jnp.float32)
        up_value = jnp.dot(row_block, up_matrix, preferred_element_type=jnp.float32)
        sigmoid_gate = jax.nn.sigmoid(gate_value)
        activated = gate_value * sigmoid_gate
        hidden = (activated * up_value * live).astype(jnp.bfloat16)
        grad_hidden = lax.dot_general(
            grad_block, down_matrix, (((1,), (1,)), ((), ())), preferred_element_type=jnp.float32
        )
        grad_gate = (
            grad_hidden * up_value * sigmoid_gate * (1.0 + gate_value * (1.0 - sigmoid_gate)) * live
        ).astype(jnp.bfloat16)
        grad_up = (grad_hidden * activated * live).astype(jnp.bfloat16)
        total_gate = add_into(total_gate, contract_rows(row_block, grad_gate), expert)
        total_up = add_into(total_up, contract_rows(row_block, grad_up), expert)
        total_down = add_into(total_down, contract_rows(hidden, grad_block), expert)
        return ((total_gate, total_up, total_down), None)

    totals, unused = lax.scan(
        step, (zeros_gate, zeros_gate, zeros_down), (row_blocks, grad_blocks, owner, alive)
    )
    return totals


def relocate(arrays, matching):
    groups = lax.axis_size("expert")
    joined = jnp.concatenate([array_piece.reshape(groups, -1) for array_piece in arrays], axis=1)
    spread = lax.all_to_all(joined, "expert", split_axis=0, concat_axis=0, tiled=True)
    ordered = jnp.take(spread, matching, axis=0)
    settled = lax.all_to_all(ordered, "expert", split_axis=0, concat_axis=0, tiled=True)
    pieces = []
    offset = 0
    for array_piece in arrays:
        length = array_piece.size // groups
        pieces.append(settled[:, offset : offset + length].reshape(array_piece.shape))
        offset = offset + length
    return pieces


def on_device_plain(tokens, grad_out, gate_weight, up_weight, down_weight, matching, block_counts):
    moved = relocate((gate_weight, up_weight, down_weight), matching)
    weight_gate, weight_up, weight_down = (
        lax.all_gather(moved[0], "dp", axis=1, tiled=True),
        lax.all_gather(moved[1], "dp", axis=1, tiled=True),
        lax.all_gather(moved[2], "dp", axis=2, tiled=True),
    )
    rows_full, grads_full = (
        lax.all_gather(tokens[0, 0], "hidden", axis=1, tiled=True),
        lax.all_gather(grad_out[0, 0], "hidden", axis=1, tiled=True),
    )
    blocks = rows_full.shape[0] // BLOCK
    width = rows_full.shape[1]
    owner, alive = block_owners(block_counts[0, 0], blocks)
    totals = expert_terms(
        rows_full.reshape(blocks, BLOCK, width),
        grads_full.reshape(blocks, BLOCK, width),
        weight_gate,
        weight_up,
        weight_down,
        owner,
        alive,
    )
    summed = (
        lax.psum_scatter(
            totals[0].astype(jnp.bfloat16), "dp", scatter_dimension=1, tiled=True
        ).astype(jnp.float32),
        lax.psum_scatter(
            totals[1].astype(jnp.bfloat16), "dp", scatter_dimension=1, tiled=True
        ).astype(jnp.float32),
        lax.psum_scatter(
            totals[2].astype(jnp.bfloat16), "dp", scatter_dimension=2, tiled=True
        ).astype(jnp.float32),
    )
    return (
        summed[0].astype(jnp.bfloat16),
        summed[1].astype(jnp.bfloat16),
        summed[2].astype(jnp.bfloat16),
    )


MESH = pl.DeviceIdType.MESH


def flip(index, bit):
    return index + bit - 2 * bit * ((index // bit) % 2)


def fused_kernel(
    exchange, experts, counts_ref, match_ref, tok_ref, grad_ref, gate_ref, up_ref, down_ref,
    out_gate, out_up, out_down,
    tok_all, grad_all, tok_dp, gu_all, dn_all, dn_end,
    own_gate, own_up, own_down, old_gate, old_up, old_down,
    acc_gu, acc_gh, acc_end, acc_out, gate_sel, up_sel, hid, hid_end, hid_out, hid_in, gh_out, gh_in,
    mask_own, mask_dp, pre, pre_dp, wide,
    part_own, part_end, core_own, core_end, sum_own, far_own, sum_far, sum_near, end_far, end_near, end_got,
    z_send, z_recv, y_send, y_recv, w_send, w_recv, t_send, t_recv, p_send, p_recv, m_send, m_recv,
    l_send, l_recv, h_send, h_recv, r_send, r_recv, e_send, e_recv, local_sem,
):
    zs = lax.axis_size("hidden")
    h = lax.axis_index("hidden")
    d = lax.axis_index("dp")
    p = lax.axis_index("expert")
    rows, feats = tok_ref.shape
    width = gate_ref.shape[2]
    blocks = rows // BLOCK
    tall = experts * width
    halves = [slice(0, rows // 2), slice(rows // 2, rows)]
    half_blocks = [range(0, blocks // 2), range(blocks // 2, blocks)]
    edges = (0, rows // 2, rows // 4 * 3, rows)
    steps = range(len(edges) - 1)
    cuts = [slice(edges[q], edges[q + 1]) for q in steps]
    cut_blocks = [range(edges[q] // BLOCK, edges[q + 1] // BLOCK) for q in steps]
    near, far = flip(d, 1), flip(d, 2)
    cross = flip(near, 2)
    partners = (near, far, cross)
    middle = (h > 0) & (h < zs - 1)
    border = (h == 0) | (h == zs - 1)
    way = 1 - 2 * (h // (zs // 2))
    inner, outer = h + way, h - way
    second, third = h + 2 * way, h + 3 * way
    full, half = jnp.float32, jnp.bfloat16

    def remote(source, target, send, recv, where):
        return pltpu.make_async_remote_copy(
            src_ref=source, dst_ref=target, send_sem=send, recv_sem=recv,
            device_id=where, device_id_type=MESH,
        )

    local = [
        pltpu.make_async_copy(source, target, local_sem.at[i])
        for i, (source, target) in enumerate((
            (gate_ref, own_gate), (up_ref, own_up), (down_ref, own_down),
            (tok_ref, tok_all.at[h]), (grad_ref, grad_all.at[h]),
        ))
    ]
    for copy in local:
        copy.start()

    barrier = pltpu.get_barrier_semaphore()
    for partner in partners:
        pl.semaphore_signal(barrier, inc=1, device_id={"dp": partner}, device_id_type=MESH)
    if exchange:
        pl.semaphore_signal(barrier, inc=1, device_id={"expert": 1 - p}, device_id_type=MESH)
    pl.semaphore_signal(barrier, inc=1, device_id={"hidden": inner}, device_id_type=MESH)

    @pl.when(middle)
    def _():
        pl.semaphore_signal(barrier, inc=1, device_id={"hidden": outer}, device_id_type=MESH)

    bounds = [counts_ref[0]]
    for e in range(1, experts):
        bounds.append(bounds[-1] + counts_ref[e])
    picks, masks, alive = [], [], []
    for b in range(blocks):
        owner = jnp.int32(0)
        for e in range(experts):
            owner = owner + jnp.where(b >= bounds[e], 1, 0)
        owner = jnp.minimum(owner, experts - 1)
        alive.append(jnp.where(b < bounds[-1], 1.0, 0.0))
        picks.append([jnp.where(owner == e, 1.0, 0.0) for e in range(experts)])
        masks.append([picks[b][e] * alive[b] for e in range(experts)])
        for e in range(experts):
            row = b * experts + e
            mask_own[row : row + 1, :] = jnp.full((1, mask_own.shape[1]), masks[b][e], full)

    peers = (h + zs - 1) // zs + (2 * zs - 2 - h) // zs
    pl.semaphore_wait(barrier, peers + (4 if exchange else 3))

    mine = (tok_ref, grad_ref)
    whole = (tok_all, grad_all)

    def line(kind, slab, r, outward=0, own=False, fine=False):
        part = (cuts if fine else halves)[r]
        source = mine[kind].at[part] if own else whole[kind].at[slab, part]
        return remote(
            source, whole[kind].at[slab, part],
            z_send.at[outward, kind, slab, r], z_recv.at[kind, slab, r],
            {"hidden": outer if outward else inner},
        )

    def landed(kind, slab, r, fine=False):
        line(kind, slab, r, fine=fine).wait_recv()

    def place(k, q):
        size = edges[q + 1] - edges[q]
        start = 2 * edges[q] + (0 if k in (1, 3) else size)
        return (0 if k in (0, 3) else 1), slice(start, start + size)

    def pair(q):
        return slice(2 * edges[q], 2 * edges[q + 1])

    def token_copy(k, q, own=False):
        source = tok_ref.at[cuts[q]] if own else tok_all.at[partners[k], cuts[q]]
        return remote(
            source, tok_dp.at[place(k, q)],
            t_send.at[k, q], t_recv.at[k, q], {"dp": partners[k]},
        )

    def mask_copy(k):
        return remote(
            mask_own, mask_dp.at[k], m_send.at[k], m_recv.at[k], {"dp": partners[k]}
        )

    for r in range(2):
        line(0, h, r, 0, True).start()

        @pl.when(middle)
        def _():
            line(0, h, r, 1, True).start()

    @pl.when(border)
    def _():
        for q in steps:
            line(1, h, q, 0, True, True).start()

    feat_halves = [slice(0, feats // 2), slice(feats // 2, feats)]

    def swap(i, e, f=None):
        source = (gate_ref, up_ref, down_ref)[i]
        target = (old_gate, old_up, old_down)[i]
        at = (e,) if f is None else (e, feat_halves[f])
        n = (i * experts + e) * 2 + (f or 0)
        return remote(source.at[at], target.at[at], y_send.at[n], y_recv.at[n], {"expert": 1 - p})

    swaps = []
    if exchange:
        swaps = [[swap(0, e, f), swap(1, e, f)] for e in range(experts) for f in range(2)]
        swaps += [[swap(2, e)] for e in range(experts)]
        for group in swaps:
            for copy in group:
                copy.start()
    for k in range(3):
        mask_copy(k).start()

        @pl.when(h == partners[k])
        def _():
            token_copy(k, steps[-1], True).start()

    def chosen(own, other, at):
        if not exchange:
            return own[at]
        return jnp.where(match_ref[p] == p, own[at], other[at])

    chunks = 3 * experts

    def piece(j, slab):
        if j < 2 * experts:
            return gu_all.at[slab, j // 2, feat_halves[j % 2]]
        e = j - 2 * experts
        return dn_all.at[slab, e * width : (e + 1) * width]

    def spread(j, i):
        ref = piece(j, (d, d, far)[i])
        to = (far, near, near)[i]
        return remote(ref, ref, w_send.at[j, i], w_recv.at[j, i], {"dp": to})

    def arrived(j, i):
        ref = piece(j, (far, near, cross)[i])
        remote(ref, ref, w_send.at[j, i], w_recv.at[j, i], {"dp": near}).wait_recv()

    def take_weights(j):
        if exchange:
            for copy in swaps[j]:
                copy.wait_recv()
        if j < 2 * experts:
            at = (j // 2, feat_halves[j % 2])
            gu_all[d, j // 2, feat_halves[j % 2], :width] = chosen(own_gate, old_gate, at)
            gu_all[d, j // 2, feat_halves[j % 2], width:] = chosen(own_up, old_up, at)
        else:
            e = j - 2 * experts
            dn_all[d, e * width : (e + 1) * width, :] = chosen(own_down, old_down, e)
        spread(j, 0).start()
        spread(j, 1).start()

    def pass_weights(j):
        arrived(j, 0)
        spread(j, 2).start()

    def share_tokens(slab, r):
        for k in range(3):
            @pl.when(slab == partners[k])
            def _():
                for q in ((0,) if r == 0 else steps[1:]):
                    token_copy(k, q).start()

    def relay_tokens(r):
        @pl.when(middle)
        def _():
            landed(0, outer, r)
            line(0, outer, r).start()
            landed(0, inner, r)
            line(0, inner, r, 1).start()

    def relay_late(r):
        @pl.when(middle)
        def _():
            landed(0, second, r)
            line(0, second, r, 1).start()
            for q in ((0,) if r == 0 else steps[1:]):
                landed(1, outer, q, True)
                line(1, outer, q, fine=True).start()

    for copy in local[:2]:
        copy.wait()
    take_weights(0)
    relay_tokens(0)
    take_weights(1)
    pass_weights(0)
    take_weights(2)
    relay_tokens(1)

    @pl.when(middle)
    def _():
        for r in range(2):
            line(1, h, r, 0, True).start()

    pass_weights(1)
    for j in range(3, 2 * experts):
        take_weights(j)
    for copy in local[2:]:
        copy.wait()
    pass_weights(2)
    take_weights(2 * experts)
    relay_late(0)
    for j in range(3, 2 * experts):
        pass_weights(j)
    for j in range(2 * experts + 1, chunks):
        take_weights(j)
    for k in range(3):
        @pl.when(h == partners[k])
        def _():
            for q in steps[:-1]:
                token_copy(k, q).start()

    @pl.when(border)
    def _():
        for r in range(2):
            landed(0, inner, r)
            share_tokens(inner, r)
        landed(0, second, 0)
        share_tokens(second, 0)

    @pl.when(middle)
    def _():
        for slab in (outer, inner):
            for r in range(2):
                share_tokens(slab, r)
        share_tokens(second, 0)

    pass_weights(2 * experts)
    relay_late(1)

    @pl.when(border)
    def _():
        landed(0, second, 1)

    share_tokens(second, 1)
    for j in range(2 * experts + 1, chunks):
        pass_weights(j)
    for j in range(chunks):
        arrived(j, 1)
        arrived(j, 2)

    core = d % 2
    lot = tall // 2

    def strip(index):
        return pl.ds(pl.multiple_of(index * lot, lot), lot)

    def lend(i, owner):
        slab = owner + (i + 1) * way
        return remote(
            dn_all.at[slab, strip(core)], dn_end.at[slab, strip(core)],
            l_send.at[0, i], l_recv.at[0, i], {"hidden": inner},
        )

    def lend_near(i, which):
        ref = dn_end.at[outer + (i + 1) * way, strip(which)]
        return remote(ref, ref, l_send.at[1, i], l_recv.at[1, i], {"dp": near})

    @pl.when(border)
    def _():
        for i in range(3):
            lend(i, h).start()

    def add_tokens(slabs, r, first):
        for e in range(experts):
            total = None if first else acc_gu[e, halves[r]]
            for slab in slabs:
                term = jnp.dot(tok_all[slab, halves[r]], gu_all[slab, e], preferred_element_type=full)
                total = term if total is None else total + term
            acc_gu[e, halves[r]] = total

    def add_grads(slabs, part, first, total_ref=acc_gh, weight=dn_all):
        total = None if first else total_ref[part]
        for slab in slabs:
            term = lax.dot_general(
                grad_all[slab, part], weight[slab], (((1,), (1,)), ((), ())),
                preferred_element_type=full,
            )
            total = term if total is None else total + term
        total_ref[part] = total

    def activate(r):
        for b in half_blocks[r]:
            part = slice(b * BLOCK, (b + 1) * BLOCK)
            both = sum(acc_gu[e, part] * picks[b][e] for e in range(experts))
            gate_value, up_value = both[:, :width], both[:, width:]
            gate_sel[part] = gate_value
            up_sel[part] = up_value
            hidden = gate_value * jax.nn.sigmoid(gate_value) * up_value
            hid_out[part] = (hidden * alive[b]).astype(half)
            for e in range(experts):
                hid[part, e * width : (e + 1) * width] = (hidden * masks[b][e]).astype(half)

    def hidden_out(r):
        return remote(
            hid_out.at[halves[r]], hid_in.at[halves[r]], h_send.at[0, r], h_recv.at[0, r],
            {"hidden": inner},
        )

    def grads_out(q):
        return remote(
            gh_out.at[cuts[q]], gh_in.at[cuts[q]], h_send.at[1, q], h_recv.at[1, q],
            {"hidden": outer},
        )

    def block_place(k, q, b):
        side, spot = place(k, q)
        start = spot.start + b * BLOCK - edges[q]
        return side, slice(start, start + BLOCK)

    def make_pre(q, extra=None):
        for b in cut_blocks[q]:
            part = slice(b * BLOCK, (b + 1) * BLOCK)
            side, spot = block_place(3, q, b)
            gate_value, up_value = gate_sel[part], up_sel[part]
            grad_hidden = sum(
                acc_gh[part, e * width : (e + 1) * width] * picks[b][e] for e in range(experts)
            )
            if extra is not None:
                grad_hidden = grad_hidden + extra[part].astype(full)
            s = jax.nn.sigmoid(gate_value)
            grad_gate = grad_hidden * up_value * s * (1.0 + gate_value * (1.0 - s))
            grad_up = grad_hidden * gate_value * s
            pre[part, :width] = (grad_gate * alive[b]).astype(half)
            pre[part, width:] = (grad_up * alive[b]).astype(half)
            for e in range(experts):
                at = e * 2 * width
                wide[side, spot, at : at + width] = (grad_gate * masks[b][e]).astype(half)
                wide[side, spot, at + width : at + 2 * width] = (grad_up * masks[b][e]).astype(half)

    def pre_copy(k, q):
        source = pre_dp.at[1, cuts[q]] if k == 2 else pre.at[cuts[q]]
        to = far if k == 1 else near
        return remote(
            source, pre_dp.at[k, cuts[q]], p_send.at[k, q], p_recv.at[k, q], {"dp": to}
        )

    def send_pre(q):
        pre_copy(1, q).start()
        pre_copy(0, q).start()

    parts, cores = (part_own, part_end), (core_own, core_end)
    lefts = (hid, hid_end)

    def core_copy(kind, i):
        slab = (cross, near)[i]
        return remote(
            parts[kind].at[slab], cores[kind].at[i], r_send.at[kind, i], r_recv.at[kind, i],
            {"dp": near},
        )

    def down_term(kind, slab, left=None):
        parts[kind][slab] = lax.dot_general(
            (lefts[kind] if left is None else left)[...], grad_all[slab], (((0,), (0,)), ((), ())), preferred_element_type=full
        ).astype(half)
        for i in range(2):
            @pl.when(slab == (cross, near)[i])
            def _():
                core_copy(kind, i).start()

    def core_sum(kind, i):
        slab = (far, d)[i]
        return parts[kind][slab].astype(full) + cores[kind][i].astype(full)

    own_far = remote(sum_own, far_own, r_send.at[2, 0], r_recv.at[2, 0], {"dp": far})
    end_near_out = remote(sum_near, end_near, e_send.at[0, 0], e_recv.at[0, 0], {"hidden": outer})

    def end_far_out(e):
        part = slice(e * width, (e + 1) * width)
        return remote(
            sum_far.at[part], end_far.at[part], e_send.at[1, e], e_recv.at[1, e], {"hidden": outer}
        )

    def end_cross(e):
        part = slice(e * width, (e + 1) * width)
        return remote(
            end_far.at[part], end_got.at[part], e_send.at[2, e], e_recv.at[2, e], {"dp": far}
        )

    def sum_end_far():
        core_copy(1, 0).wait_recv()
        sum_far[...] = core_sum(1, 0).astype(half)

    def widen(k, q):
        for b in cut_blocks[q]:
            part = slice(b * BLOCK, (b + 1) * BLOCK)
            side, spot = block_place(k, q, b)
            for e in range(experts):
                row = b * experts + e
                keep = mask_dp[k, row : row + 1, :]
                for i in range(2):
                    at = (e * 2 + i) * width
                    value = pre_dp[k, part, i * width : (i + 1) * width].astype(full)
                    wide[side, spot, at : at + width] = (value * keep).astype(half)

    def gate_term(side, q, past=None):
        rows_of = slice(pair(q).start, pair(q if past is None else past).stop)
        return lax.dot_general(
            tok_dp[side, rows_of], wide[side, rows_of], (((0,), (0,)), ((), ())),
            preferred_element_type=full,
        )

    def near_gates(q):
        token_copy(0, q).wait_recv()
        pre_copy(0, q).wait_recv()
        widen(0, q)
        term = gate_term(0, q)
        acc_out[...] = term if q == 0 else acc_out[...] + term

    def take_far(q):
        pre_copy(1, q).wait_recv()
        pre_copy(2, q).start()

    def widen_far(q):
        for k in (1, 2):
            token_copy(k, q).wait_recv()
        widen(1, q)
        pre_copy(2, q).wait_recv()
        widen(2, q)

    def sent_early():
        for r in range(2):
            line(0, h, r, 0, True).wait_send()
        for k in range(3):
            mask_copy(k).wait_send()
        for j in range(chunks):
            for i in range(3):
                spread(j, i).wait_send()
        if exchange:
            for group in swaps:
                for copy in group:
                    copy.wait_send()

    def pass_end(e):
        @pl.when(far != h)
        def _():
            end_far_out(e).wait_recv()

        end_cross(e).start()

    def send_own_far():
        core_copy(0, 0).wait_recv()
        sum_own[...] = core_sum(0, 0).astype(half)
        own_far.start()

    for k in range(3):
        mask_copy(k).wait_recv()
    own_tokens = [
        pltpu.make_async_copy(tok_all.at[d, cuts[q]], tok_dp.at[place(3, q)], local_sem.at[q])
        for q in steps
    ]

    @pl.when(border)
    def _():
        for r in range(2):
            add_tokens((h, inner, second), r, True)
            add_grads((h,), halves[r], True)
        for r in range(2):
            landed(0, third, r)
            share_tokens(third, r)
            add_tokens((third,), r, False)
            activate(r)
            hidden_out(r).start()
        down_term(1, h, hid)
        for copy in own_tokens:
            copy.start()

        @pl.when(far == h)
        def _():
            core_copy(1, 0).wait_recv()
            end_far[...] = core_sum(1, 0).astype(half)
            for e in range(experts):
                end_cross(e).start()

        @pl.when(d == h)
        def _():
            core_copy(1, 1).wait_recv()
            end_near[...] = core_sum(1, 1).astype(half)

        for q in steps:
            grads_out(q).wait_recv()
            make_pre(q, gh_in)
            send_pre(q)
            if q == 0:
                sent_early()
                for i in steps:
                    line(1, h, i, 0, True, True).wait_send()
                for r in range(2):
                    hidden_out(r).wait_send()
                for i in range(3):
                    lend(i, h).wait_send()

            if q == steps[-1]:
                @pl.when((far != third) & (far != h))
                def _():
                    for e in range(experts):
                        pass_end(e)

            if q == 0:
                for copy in own_tokens:
                    copy.wait()
            else:
                near_gates(q - 1)


    @pl.when(middle)
    def _():
        for r in range(2):
            add_tokens((h, outer, inner, second), r, True)
            activate(r)
            add_grads((h, outer), halves[r], True)
        for copy in own_tokens:
            copy.start()
        for slab in (h, outer):
            down_term(0, slab)
        lend(0, outer).wait_recv()
        lend_near(0, core).start()
        landed(1, inner, 0)
        add_grads((inner,), halves[0], False)
        lend(1, outer).wait_recv()
        lend_near(1, core).start()
        landed(1, inner, 1)
        add_grads((inner,), halves[1], False)
        lend(2, outer).wait_recv()
        lend_near(2, core).start()
        down_term(0, inner)
        for i in range(3):
            lend_near(i, 1 - core).wait_recv()
        for r in range(2):
            add_grads((h, inner), halves[r], True, acc_end, dn_end)
        for copy in own_tokens:
            copy.wait()
        sent_early()
        for r in range(2):
            line(0, h, r, 1, True).wait_send()
            line(1, h, r, 0, True).wait_send()
            line(0, outer, r).wait_send()
            line(0, inner, r, 1).wait_send()
            line(0, second, r, 1).wait_send()
        for r in range(2):
            hidden_out(r).wait_recv()
            for b in half_blocks[r]:
                part = slice(b * BLOCK, (b + 1) * BLOCK)
                value = hid_in[part].astype(full)
                for e in range(experts):
                    hid_end[part, e * width : (e + 1) * width] = (value * masks[b][e]).astype(half)

        def last_grads(q):
            landed(1, second, q, True)
            add_grads((second,), cuts[q], False, acc_end, dn_end)
            for b in cut_blocks[q]:
                part = slice(b * BLOCK, (b + 1) * BLOCK)
                gh_out[part] = sum(
                    acc_end[part, e * width : (e + 1) * width] * picks[b][e] for e in range(experts)
                ).astype(half)
            grads_out(q).start()
            if q == steps[-1]:
                down_term(1, second)
            add_grads((second,), cuts[q], False)
            make_pre(q)
            send_pre(q)

        for slab in (h, inner):
            down_term(1, slab)
        @pl.when((far != second) & (far != outer))
        def _():
            sum_end_far()
            for e in range(experts):
                end_far_out(e).start()

        for q in steps:
            last_grads(q)
            if 0 < q < steps[-1]:
                near_gates(q - 1)

        @pl.when(far != second)
        def _():
            send_own_far()

        @pl.when(far == second)
        def _():
            sum_end_far()
            for e in range(experts):
                end_far_out(e).start()

        @pl.when(d == second)
        def _():
            core_copy(1, 1).wait_recv()
            sum_near[...] = core_sum(1, 1).astype(half)
            end_near_out.start()

        down_term(0, second)

        @pl.when(far == second)
        def _():
            send_own_far()

        @pl.when((d != outer) & (d != second))
        def _():
            core_copy(1, 1).wait_recv()
            sum_near[...] = core_sum(1, 1).astype(half)
            end_near_out.start()

        near_gates(steps[-1] - 1)

    take_far(0)
    near_gates(steps[-1])
    take_far(1)

    @pl.when(border & (far == third))
    def _():
        for e in range(experts):
            pass_end(e)

    widen_far(0)
    take_far(2)
    widen_far(1)
    acc_out[...] = acc_out[...] + gate_term(1, 0, 1)
    widen_far(2)
    total = acc_out[...] + gate_term(1, 2)
    for e in range(experts):
        at = e * 2 * width
        out_gate[e] = total[:, at : at + width].astype(half)
        out_up[e] = total[:, at + width : at + 2 * width].astype(half)

    @pl.when(middle)
    def _():
        core_copy(0, 1).wait_recv()
        own_far.wait_recv()
        total = core_sum(0, 1) + far_own[...].astype(full)
        for e in range(experts):
            out_down[e] = total[e * width : (e + 1) * width].astype(half)

    @pl.when(border)
    def _():
        @pl.when(d != h)
        def _():
            end_near_out.wait_recv()

        for e in range(experts):
            end_cross(e).wait_recv()
        total = end_near[...].astype(full) + end_got[...].astype(full)
        for e in range(experts):
            out_down[e] = total[e * width : (e + 1) * width].astype(half)

    for k in range(3):
        for q in steps:
            token_copy(k, q).wait_send()
            pre_copy(k, q).wait_send()

    @pl.when(middle)
    def _():
        for q in steps:
            line(1, outer, q, fine=True).wait_send()
            grads_out(q).wait_send()
        for i in range(3):
            lend_near(i, core).wait_send()
        for i in range(2):
            core_copy(0, i).wait_send()

            @pl.when((cross, near)[i] != outer)
            def _():
                core_copy(1, i).wait_send()

        own_far.wait_send()

        @pl.when(far != outer)
        def _():
            for e in range(experts):
                end_far_out(e).wait_send()

        @pl.when(d != outer)
        def _():
            end_near_out.wait_send()

    @pl.when(border)
    def _():
        for i in range(2):
            @pl.when((cross, near)[i] == h)
            def _():
                core_copy(1, i).wait_send()

        for e in range(experts):
            end_cross(e).wait_send()


def settle_kernel(*refs):
    count = (len(refs) - 1) // 2
    copies = [
        pltpu.make_async_copy(refs[i], refs[count + i], refs[-1].at[i]) for i in range(count)
    ]
    for copy in copies:
        copy.start()
    for copy in copies:
        copy.wait()


def settle(arrays):
    count = len(arrays)
    return pl.pallas_call(
        settle_kernel,
        out_shape=tuple(jax.ShapeDtypeStruct(a.shape, a.dtype) for a in arrays),
        in_specs=[pl.BlockSpec(memory_space=pltpu.VMEM)] * count,
        out_specs=(pl.BlockSpec(memory_space=pl.ANY),) * count,
        scratch_shapes=[pltpu.SemaphoreType.DMA((count,))],
    )(*[pltpu.with_memory_space_constraint(a, pltpu.VMEM) for a in arrays])


def on_device_fused(tokens, grad_out, gate_weight, up_weight, down_weight, matching, block_counts):
    groups = lax.axis_size("expert")
    zs = lax.axis_size("hidden")
    ds = lax.axis_size("dp")
    exchange = groups == 2
    if not exchange:
        gate_weight, up_weight, down_weight = relocate(
            (gate_weight, up_weight, down_weight), matching
        )
        matching = jnp.zeros_like(matching)
    rows, feats = tokens.shape[2:]
    experts, part, width = gate_weight.shape
    vmem = pl.BlockSpec(memory_space=pltpu.VMEM)
    smem = pl.BlockSpec(memory_space=pltpu.SMEM)
    half, full = jnp.bfloat16, jnp.float32
    wide = experts * 2 * width
    tall = experts * width
    chunks = 3 * experts
    dma = pltpu.SemaphoreType.DMA
    down = pltpu.VMEM((tall, part), half)
    narrow = pltpu.VMEM((rows, width), half)
    mask = (experts * (rows // BLOCK), width)
    grads = pl.pallas_call(
        functools.partial(fused_kernel, exchange, experts),
        out_shape=tuple(
            pltpu.VMEM(w.shape, half) for w in (gate_weight, up_weight, down_weight)
        ),
        in_specs=[smem, smem] + [pl.BlockSpec(memory_space=pltpu.HBM)] * 5,
        out_specs=(vmem,) * 3,
        scratch_shapes=[
            pltpu.VMEM((zs, rows, feats), half),
            pltpu.VMEM((zs, rows, feats), half),
            pltpu.VMEM((2, 2 * rows, feats), half),
            pltpu.VMEM((ds, experts, part, 2 * width), half),
            pltpu.VMEM((ds, tall, part), half),
            pltpu.VMEM((ds, tall, part), half),
            pltpu.VMEM(gate_weight.shape, half),
            pltpu.VMEM(up_weight.shape, half),
            pltpu.VMEM(down_weight.shape, half),
            pltpu.VMEM(gate_weight.shape, half),
            pltpu.VMEM(up_weight.shape, half),
            pltpu.VMEM(down_weight.shape, half),
            pltpu.VMEM((experts, rows, 2 * width), full),
            pltpu.VMEM((rows, tall), full),
            pltpu.VMEM((rows, tall), full),
            pltpu.VMEM((feats, wide), full),
            pltpu.VMEM((rows, width), full),
            pltpu.VMEM((rows, width), full),
            pltpu.VMEM((rows, tall), half),
            pltpu.VMEM((rows, tall), half),
            narrow, narrow, narrow, narrow,
            pltpu.VMEM(mask, full),
            pltpu.VMEM((3,) + mask, full),
            pltpu.VMEM((rows, 2 * width), half),
            pltpu.VMEM((3, rows, 2 * width), half),
            pltpu.VMEM((2, 2 * rows, wide), half),
            pltpu.VMEM((ds, tall, part), half),
            pltpu.VMEM((ds, tall, part), half),
            pltpu.VMEM((2, tall, part), half),
            pltpu.VMEM((2, tall, part), half),
            down, down, down, down, down, down, down,
            dma((2, 2, zs, 3)),
            dma((2, zs, 3)),
            dma((3 * experts * 2,)),
            dma((3 * experts * 2,)),
            dma((chunks, 3)),
            dma((chunks, 3)),
            dma((3, 3)),
            dma((3, 3)),
            dma((3, 3)),
            dma((3, 3)),
            dma((3,)),
            dma((3,)),
            dma((2, 3)),
            dma((2, 3)),
            dma((2, 3)),
            dma((2, 3)),
            dma((3, 2)),
            dma((3, 2)),
            dma((3, experts)),
            dma((3, experts)),
            dma((5,)),
        ],
        compiler_params=pltpu.CompilerParams(
            collective_id=0, has_side_effects=True, vmem_limit_bytes=63 * 1024 * 1024
        ),
    )(
        block_counts.reshape(-1), matching, tokens.reshape(rows, feats),
        grad_out.reshape(rows, feats), gate_weight, up_weight, down_weight,
    )
    return settle(grads)


def fused_fits(mesh):
    return mesh.shape["dp"] == 4 and mesh.shape["hidden"] == 4


def solution(mesh):
    on_device = on_device_fused if fused_fits(mesh) else on_device_plain
    in_specs = (
        P("expert", "dp", None, "hidden"),
        P("expert", "dp", None, "hidden"),
        P("expert", "dp", "hidden"),
        P("expert", "dp", "hidden"),
        P("expert", "hidden", "dp"),
        P(),
        P("expert", "dp", None),
    )
    out_specs = (
        P("expert", "dp", "hidden"),
        P("expert", "dp", "hidden"),
        P("expert", "hidden", "dp"),
    )
    return jax.shard_map(
        on_device, mesh=mesh, in_specs=in_specs, out_specs=out_specs, check_vma=False
    )
```
